32 devices in a mesh: dp: 8 (over y, x, core), mp: 4 (over z).
Axes of the slice: x: 2, y: 2, z: 4, core: 2. Of those that a mesh axis runs over, the one named last changes fastest.
Arguments:
- inputs: bfloat16 [16, 1024, 1280], P('dp', 'mp'), may hold values from -6 to 6
- cotangent: bfloat16 [16, 1024, 1280], P('dp', 'mp'), may hold values from -6 to 6
- gene_counts: int32 [16], P('dp'), may hold values from 200 to 1023, as said below
- step_count: int32 [1], replicated, may hold values from 2 to 20
- norm_params: float32 [4, 1280], P(None, ('dp', 'mp')), may hold values from -0.3 to 1.4, as said below
- norm_first: float32 [4, 1280], P(None, ('dp', 'mp')), may hold values from -80 to 80
- norm_second: float32 [4, 1280], P(None, ('dp', 'mp')), may hold values from 425.984 to 6881.28
- attend_weight: float32 [3, 1280, 1280], P(None, 'dp', 'mp'), may hold values from -0.15625 to 0.15625
- attend_first: float32 [3, 1280, 1280], P(None, 'dp', 'mp'), may hold values from -80 to 80
- attend_second: float32 [3, 1280, 1280], P(None, 'dp', 'mp'), may hold values from 425.984 to 6881.28
- output_weight: float32 [1280, 1280], P('mp', 'dp'), may hold values from -4 to 4
- output_first: float32 [1280, 1280], P('mp', 'dp'), may hold values from -4 to 4
- output_second: float32 [1280, 1280], P('mp', 'dp'), may hold values from 0.8 to 13.44
- expand_weight: float32 [1280, 5120], P('dp', 'mp'), may hold values from -0.15625 to 0.15625
- expand_first: float32 [1280, 5120], P('dp', 'mp'), may hold values from -32 to 32
- expand_second: float32 [1280, 5120], P('dp', 'mp'), may hold values from 68.8128 to 1097.728
- reduce_weight: float32 [5120, 1280], P('mp', 'dp'), may hold values from -0.078125 to 0.078125
- reduce_first: float32 [5120, 1280], P('mp', 'dp'), may hold values from -48 to 48
- reduce_second: float32 [5120, 1280], P('mp', 'dp'), may hold values from 155.648 to 2457.6
Outputs:
- outputs: float32 [16, 1024, 1280], P('dp', 'mp')
- input_grad: float32 [16, 1024, 1280], P('dp', 'mp')
- norm_master: float32 [4, 1280], P(None, ('dp', 'mp'))
- norm_momentum: float32 [4, 1280], P(None, ('dp', 'mp'))
- norm_variance: float32 [2, 1280], P(None, ('dp', 'mp'))
- feed_variance: float32 [2, 1280], P(None, ('dp', 'mp'))
- attend_master: float32 [3, 1280, 1280], P(None, 'dp', 'mp')
- attend_momentum: float32 [3, 1280, 1280], P(None, 'dp', 'mp')
- attend_variance: float32 [3, 1280, 1280], P(None, 'dp', 'mp')
- output_master: float32 [1280, 1280], P('mp', 'dp')
- output_momentum: float32 [1280, 1280], P('mp', 'dp')
- output_variance: float32 [1280, 1280], P('mp', 'dp')
- expand_master: float32 [1280, 5120], P('dp', 'mp')
- expand_momentum: float32 [1280, 5120], P('dp', 'mp')
- expand_variance: float32 [1280, 5120], P('dp', 'mp')
- reduce_master: float32 [5120, 1280], P('mp', 'dp')
- reduce_momentum: float32 [5120, 1280], P('mp', 'dp')
- reduce_variance: float32 [5120, 1280], P('mp', 'dp')
The draws below stay inside these ranges and needn't reach their ends.
Inputs may be any that keep to these rules, and one draw needn't show every extreme that they name: `gene_counts`: genes of each cell; the cell holds that many tokens plus its CLS token, the rest of its 1024 slots are padding; the largest, 1023, occurs in every draw. `norm_params`: rows 0 and 2 are gains, rows 1 and 3 shifts.
All inputs are finite; a program needn't handle non-finite values.
Results may differ from the reference program's by a relative error of at most 0.012.
Values may be sent and summed in bfloat16 or wider, within the bound.
A program may use at most 256 MiB of HBM per device.

```python
import math
import jax
import jax.numpy as jnp
from jax import lax

D = 1280
HEADS = 20
HEAD_DIM = 64
FF = 5120
SEQ = 1024
MIN_GENES = 200
CELLS = 16


def draw_gene_counts(key, part):
    first_key = jax.random.fold_in(key, 11)
    second_key = jax.random.fold_in(key, 12)
    counts = jax.random.randint(first_key, (CELLS,), MIN_GENES, SEQ)
    largest_at = jax.random.randint(second_key, (), 0, CELLS)
    return counts.at[largest_at].set(SEQ - 1).astype(jnp.int32)


def draw_norm_params(key, part):
    gains = jax.random.uniform(jax.random.fold_in(key, 21), (2, D), jnp.float32, 0.6, 1.4)
    shifts = jax.random.uniform(jax.random.fold_in(key, 22), (2, D), jnp.float32, -0.3, 0.3)
    return jnp.stack([gains[0], shifts[0], gains[1], shifts[1]]).astype(jnp.float32)


def block_scale(rng, shape, split, low, largest):
    level, own = 1.0, jax.random.fold_in(rng, 6)
    for position, blocks in split:
        steps = jnp.exp(jax.random.uniform(jax.random.fold_in(own, position), (blocks,), jnp.float32, low / len(split), largest / len(split)))
        level = level * jnp.repeat(steps, shape[position] // blocks).reshape([-1 if axis == position else 1 for axis in range(len(shape))])
    return level


def normal_values(key, extent, deviation, bound, split=(), dtype=jnp.bfloat16):
    values = jax.random.normal(key, extent, jnp.float32) * deviation
    if len(split) > 0:
        values = block_scale(key, extent, split, -0.22, 0.18) * values
    return jnp.clip(values, min=-bound, max=bound).astype(dtype)


def setup_inputs(seed: int = 0) -> dict:
    arg_keys = jax.random.split(jax.random.key(seed), 20)
    return {
        "inputs": normal_values(arg_keys[0], (CELLS, SEQ, D), 1.0, 6.0, ((0, 8), (1, 4))),
        "cotangent": normal_values(arg_keys[1], (CELLS, SEQ, D), 1.0, 6.0, ((0, 8), (1, 4))),
        "gene_counts": draw_gene_counts(jax.random.fold_in(arg_keys[19], 71), 0),
        "step_count": jax.random.randint(arg_keys[3], (1,), 2, 21).astype(jnp.int32),
        "norm_params": draw_norm_params(jax.random.fold_in(arg_keys[19], 71), 0),
        "norm_first": normal_values(arg_keys[5], (4, D), (0.11 * (CELLS * SEQ) ** 0.5), 80.0, ((1, 32),), jnp.float32),
        "norm_second": jnp.clip(jnp.exp(math.log(6881.28) - 2.7821581 * jax.random.uniform(arg_keys[6], (4, D), jnp.float32) ** block_scale(arg_keys[6], (4, D), ((1, 32),), -0.2, 0.2)), 425.984, 6881.28),
        "attend_weight": normal_values(arg_keys[7], (3, D, D), D ** -0.5, 0.15625, ((1, 8), (2, 4)), jnp.float32),
        "attend_first": normal_values(arg_keys[8], (3, D, D), (0.11 * (CELLS * SEQ) ** 0.5), 80.0, ((1, 8), (2, 4)), jnp.float32),
        "attend_second": jnp.clip(jnp.exp(math.log(6881.28) - 2.7821581 * jax.random.uniform(arg_keys[9], (3, D, D), jnp.float32) ** block_scale(arg_keys[9], (3, D, D), ((1, 8), (2, 4)), -0.2, 0.2)), 425.984, 6881.28),
        "output_weight": normal_values(arg_keys[10], (D, D), (2 * D // SEQ) ** -0.5, 4.0, ((0, 4), (1, 8)), jnp.float32),
        "output_first": normal_values(arg_keys[11], (D, D), (0.16 * CELLS ** 0.5), 4.0, ((0, 4), (1, 8)), jnp.float32),
        "output_second": jnp.clip(jnp.exp(math.log(13.44) - 2.821379 * jax.random.uniform(arg_keys[12], (D, D), jnp.float32) ** block_scale(arg_keys[12], (D, D), ((0, 4), (1, 8)), -0.2, 0.2)), 0.8, 13.44),
        "expand_weight": normal_values(arg_keys[13], (D, FF), D ** -0.5, 0.15625, ((0, 8), (1, 4)), jnp.float32),
        "expand_first": normal_values(arg_keys[14], (D, FF), (0.044 * (CELLS * SEQ) ** 0.5), 32.0, ((0, 8), (1, 4)), jnp.float32),
        "expand_second": jnp.clip(jnp.exp(math.log(1097.728) - 2.7696082 * jax.random.uniform(arg_keys[15], (D, FF), jnp.float32) ** block_scale(arg_keys[15], (D, FF), ((0, 8), (1, 4)), -0.2, 0.2)), 68.8128, 1097.728),
        "reduce_weight": normal_values(arg_keys[16], (FF, D), FF ** -0.5, 0.078125, ((0, 4), (1, 8)), jnp.float32),
        "reduce_first": normal_values(arg_keys[17], (FF, D), (0.066 * (CELLS * SEQ) ** 0.5), 48.0, ((0, 4), (1, 8)), jnp.float32),
        "reduce_second": jnp.clip(jnp.exp(math.log(2457.6) - 2.7593436 * jax.random.uniform(arg_keys[18], (FF, D), jnp.float32) ** block_scale(arg_keys[18], (FF, D), ((0, 4), (1, 8)), -0.2, 0.2)), 155.648, 2457.6),
    }


eps_norm = 1e-05
masked_score = -1e+30
beta_one = 0.9
beta_two = 0.95
eps_adam = 1e-08
decay_rate = 0.1
norm_rate = 0.6

@jax.custom_vjp
def low(v):
    return lax.optimization_barrier(v.astype(jnp.bfloat16)).astype(jnp.float32)

@jax.custom_vjp
def low_back(v):
    return v

def low_keep(v):
    return (low(v), None)

def low_pass(kept, grad):
    return (grad,)

def back_keep(v):
    return (v, None)

def back_low(kept, grad):
    return (low(grad),)
low.defvjp(low_keep, low_pass)
low_back.defvjp(back_keep, back_low)

def layer_norm(token_rows, norm_gain, norm_shift):
    mean_row = lax.optimization_barrier(jnp.mean(token_rows, axis=-1, keepdims=True))
    centred = token_rows - mean_row
    variance = lax.optimization_barrier(jnp.mean(centred * centred, axis=-1, keepdims=True))
    return centred * lax.rsqrt(variance + eps_norm) * norm_gain + norm_shift

def adam_step(weight, first_moment, second_moment, gradient, rate, decay, step_number):
    first_new = beta_one * first_moment + (1.0 - beta_one) * gradient
    second_new = beta_two * second_moment + (1.0 - beta_two) * gradient * gradient
    corr_one = 1.0 - jnp.power(beta_one, step_number)
    corr_two = 1.0 - jnp.power(beta_two, step_number)
    update = first_new / corr_one / (jnp.sqrt(second_new / corr_two) + eps_adam)
    return (weight - rate * (update + decay * weight), first_new, second_new)

def reference(inputs, cotangent, gene_counts, step_count, norm_params, norm_first, norm_second, attend_weight, attend_first, attend_second, output_weight, output_first, output_second, expand_weight, expand_first, expand_second, reduce_weight, reduce_first, reduce_second):
    highest = lax.Precision.HIGHEST
    score_scale = HEAD_DIM ** (-0.5)

    def forward(rows_all, norms, attend_w, output_w, expand_w, reduce_w):
        attend_low = low(attend_w)
        output_low = low(output_w)
        expand_low = low(expand_w)
        reduce_low = low(reduce_w)

        def one_cell(token_rows, gene_total):
            key_valid = jnp.arange(SEQ) < 1 + gene_total
            normed = low(layer_norm(token_rows, norms[0], norms[1]))
            projected = low_back(low(jnp.einsum('sd,tde->tse', normed, attend_low, precision=highest)))
            projected = projected.reshape(3, SEQ, HEADS, HEAD_DIM)
            raw_scores = jnp.einsum('qhd,khd->hqk', projected[0], projected[1], precision=highest) * score_scale
            scores = low_back(jnp.where(key_valid[None, None, :], raw_scores, masked_score))
            exp_scores = jnp.exp(scores - lax.optimization_barrier(jnp.max(scores, axis=-1, keepdims=True)))
            probabilities = low(exp_scores / lax.optimization_barrier(jnp.sum(exp_scores, axis=-1, keepdims=True)))
            context = jnp.einsum('hqk,khd->qhd', probabilities, projected[2], precision=highest)
            context = low_back(low(context)).reshape(SEQ, D)
            middle = token_rows + low_back(jnp.dot(context, output_low, precision=highest))
            normed_two = low(layer_norm(middle, norms[2], norms[3]))
            hidden = low_back(jnp.dot(normed_two, expand_low, precision=highest))
            active = low(jax.nn.gelu(hidden, approximate=False))
            return middle + low_back(jnp.dot(active, reduce_low, precision=highest))
        cell_fn = jax.checkpoint(one_cell)

        def apply_cell(packed):
            return cell_fn(packed[0], packed[1])
        return lax.map(apply_cell, (rows_all, gene_counts))
    outputs, pullback = jax.vjp(forward, inputs.astype(jnp.float32), norm_params, attend_weight, output_weight, expand_weight, reduce_weight)
    gradients = pullback(cotangent.astype(jnp.float32))
    step_number = step_count[0].astype(jnp.float32)
    norm_new = adam_step(norm_params, norm_first, norm_second, gradients[1], norm_rate, 0.0, step_number)
    attend_new = adam_step(attend_weight, attend_first, attend_second, gradients[2], 2.0 * D ** (-0.5), decay_rate, step_number)
    output_new = adam_step(output_weight, output_first, output_second, gradients[3], 2.0 * (2 * D // SEQ) ** (-0.5), decay_rate, step_number)
    expand_new = adam_step(expand_weight, expand_first, expand_second, gradients[4], 2.0 * D ** (-0.5), decay_rate, step_number)
    reduce_new = adam_step(reduce_weight, reduce_first, reduce_second, gradients[5], 2.0 * FF ** (-0.5), decay_rate, step_number)
    return (outputs, gradients[0], norm_new[0], norm_new[1], norm_new[2][0:2], norm_new[2][2:4], attend_new[0], attend_new[1], attend_new[2], output_new[0], output_new[1], output_new[2], expand_new[0], expand_new[1], expand_new[2], reduce_new[0], reduce_new[1], reduce_new[2])
```

```python
import functools

import jax
import jax.numpy as jnp
from jax import lax
from jax.experimental import pallas as pl
from jax.experimental.pallas import tpu as pltpu
from jax.sharding import PartitionSpec as P

D = 1280
HEAD_DIM = 64
FF = 5120
SEQ = 1024

eps_norm = 1e-05
masked_score = -1e30
beta_one = 0.9
beta_two = 0.95
eps_adam = 1e-08
decay_rate = 0.1
norm_rate = 0.6

F32 = jnp.float32
BF16 = jnp.bfloat16
AXES = ("dp", "mp")


def exact_gelu(values):
    return jax.nn.gelu(values, approximate=False)


def mm(left, right, dims):
    return lax.dot_general(left, right, (dims, ((), ())), preferred_element_type=F32)


def mm_nn(left, right):
    return mm(left, right, ((1,), (0,)))


def mm_nt(left, right):
    return mm(left, right, ((1,), (1,)))


def mm_tn(left, right):
    return mm(left, right, ((0,), (0,)))


def normalize(token_rows, norm_gain, norm_shift):
    mean_row = jnp.mean(token_rows, axis=-1, keepdims=True)
    centred = token_rows - mean_row
    inv_std = lax.rsqrt(jnp.mean(centred * centred, axis=-1, keepdims=True) + eps_norm)
    scaled = centred * inv_std
    return (scaled * norm_gain + norm_shift, scaled, inv_std)


def normalize_back(grad_out, scaled, inv_std, norm_gain):
    grad_scaled = grad_out * norm_gain
    centre_part = jnp.mean(grad_scaled, axis=-1, keepdims=True)
    along_part = scaled * jnp.mean(grad_scaled * scaled, axis=-1, keepdims=True)
    grad_in = inv_std * (grad_scaled - centre_part - along_part)
    return (grad_in, jnp.sum(grad_out * scaled, axis=0), jnp.sum(grad_out, axis=0))


def adam_step(weight, first_moment, second_moment, gradient, rate, decay, step_number):
    first_new = beta_one * first_moment + (1.0 - beta_one) * gradient
    second_new = beta_two * second_moment + (1.0 - beta_two) * gradient * gradient
    corr_one = 1.0 - jnp.power(beta_one, step_number)
    corr_two = 1.0 - jnp.power(beta_two, step_number)
    update = first_new / corr_one / (jnp.sqrt(second_new / corr_two) + eps_adam)
    return (weight - rate * (update + decay * weight), first_new, second_new)


def attend_kernel(heads, block, bias_ref, q_ref, kv_ref, ctx_ref, lse_ref):
    width = heads * HEAD_DIM
    bias = bias_ref[...]
    for h in range(heads):
        lo = h * HEAD_DIM
        q = q_ref[0, :, lo : lo + HEAD_DIM] * jnp.asarray(HEAD_DIM**-0.5, BF16)
        k = kv_ref[0, :, width + lo : width + lo + HEAD_DIM]
        v = kv_ref[0, :, 2 * width + lo : 2 * width + lo + HEAD_DIM]
        s = mm_nt(q, k) + bias
        top = jnp.max(s, axis=-1, keepdims=True)
        e = jnp.exp(s - top)
        total = jnp.sum(e, axis=-1, keepdims=True)
        ctx = mm_nn(e.astype(BF16), v) / total
        ctx_ref[0, :, lo : lo + HEAD_DIM] = ctx.astype(BF16)
        lse_ref[0, :, h : h + 1] = top + jnp.log(total)


def attend(qkv, bias, heads):
    chunks, seq, _ = qkv.shape
    block = min(256, seq)
    width = heads * HEAD_DIM
    return pl.pallas_call(
        functools.partial(attend_kernel, heads, block),
        grid=(chunks, seq // block),
        in_specs=[
            pl.BlockSpec((1, seq), lambda i, j: (0, 0)),
            pl.BlockSpec((1, block, 3 * width), lambda i, j: (i, j, 0)),
            pl.BlockSpec((1, seq, 3 * width), lambda i, j: (i, 0, 0)),
        ],
        out_specs=[
            pl.BlockSpec((1, block, width), lambda i, j: (i, j, 0)),
            pl.BlockSpec((1, block, 8), lambda i, j: (i, j, 0)),
        ],
        out_shape=[
            jax.ShapeDtypeStruct((chunks, seq, width), BF16),
            jax.ShapeDtypeStruct((chunks, seq, 8), F32),
        ],
        cost_estimate=pl.CostEstimate(
            flops=16 * chunks * heads * seq * seq * HEAD_DIM,
            bytes_accessed=8 * chunks * seq * width,
            transcendentals=chunks * heads * seq * seq,
        ),
        name="attend",
    )(bias, qkv, qkv)


def attend_back_kernel(heads, bias_ref, q_ref, g_ref, o_ref, lse_ref, kv_ref, gq_ref, gkv_ref, acc_ref):
    width = heads * HEAD_DIM
    step = pl.program_id(1)
    scale = HEAD_DIM**-0.5

    @pl.when(step == 0)
    def _():
        acc_ref[...] = jnp.zeros_like(acc_ref)

    bias = bias_ref[...]
    lse_rows = lse_ref[0].T
    for h in range(heads):
        lo = h * HEAD_DIM
        q = q_ref[0, :, lo : lo + HEAD_DIM] * jnp.asarray(scale, BF16)
        g = g_ref[0, :, lo : lo + HEAD_DIM]
        o = o_ref[0, :, lo : lo + HEAD_DIM]
        k = kv_ref[0, :, width + lo : width + lo + HEAD_DIM]
        v = kv_ref[0, :, 2 * width + lo : 2 * width + lo + HEAD_DIM]
        delta = jnp.sum(g.astype(F32) * o.astype(F32), axis=-1, keepdims=True).T
        st = mm_nt(k, q) + bias
        pt = jnp.exp(st - lse_rows[h : h + 1, :])
        gpt = mm_nt(v, g)
        gst = (pt * (gpt - delta)).astype(BF16)
        acc_ref[:, width + lo : width + lo + HEAD_DIM] += mm_nn(pt.astype(BF16), g)
        acc_ref[:, lo : lo + HEAD_DIM] += mm_nn(gst, q)
        gq_ref[0, :, lo : lo + HEAD_DIM] = (mm_tn(gst, k) * scale).astype(BF16)

    @pl.when(step == pl.num_programs(1) - 1)
    def _():
        gkv_ref[0] = acc_ref[...].astype(BF16)


def attend_back(qkv, grad_ctx, ctx, lse, bias_col, heads):
    chunks, seq, _ = qkv.shape
    block = min(256, seq)
    width = heads * HEAD_DIM
    return pl.pallas_call(
        functools.partial(attend_back_kernel, heads),
        grid=(chunks, seq // block),
        in_specs=[
            pl.BlockSpec((seq, 1), lambda i, j: (0, 0)),
            pl.BlockSpec((1, block, 3 * width), lambda i, j: (i, j, 0)),
            pl.BlockSpec((1, block, width), lambda i, j: (i, j, 0)),
            pl.BlockSpec((1, block, width), lambda i, j: (i, j, 0)),
            pl.BlockSpec((1, block, 8), lambda i, j: (i, j, 0)),
            pl.BlockSpec((1, seq, 3 * width), lambda i, j: (i, 0, 0)),
        ],
        out_specs=[
            pl.BlockSpec((1, block, width), lambda i, j: (i, j, 0)),
            pl.BlockSpec((1, seq, 2 * width), lambda i, j: (i, 0, 0)),
        ],
        out_shape=[
            jax.ShapeDtypeStruct((chunks, seq, width), BF16),
            jax.ShapeDtypeStruct((chunks, seq, 2 * width), BF16),
        ],
        scratch_shapes=[pltpu.VMEM((seq, 2 * width), F32)],
        cost_estimate=pl.CostEstimate(
            flops=40 * chunks * heads * seq * seq * HEAD_DIM,
            bytes_accessed=20 * chunks * seq * width,
            transcendentals=chunks * heads * seq * seq,
        ),
        name="attend_back",
    )(bias_col, qkv, grad_ctx, ctx, lse, qkv)


class Routes:
    def __init__(self, dp_size, mp_size):
        self.dp, self.mp = dp_size, mp_size
        self.bits = (dp_size // 2).bit_length() - 1
        self.mp_bits = mp_size.bit_length() - 1

    def _pairs(self, target):
        pairs = []
        for d in range(self.dp):
            for m in range(self.mp):
                dest = target(d // 2, d % 2, m)
                pairs.append((d * self.mp + m, (dest[0] * 2 + dest[1]) * self.mp + dest[2]))
        return pairs

    def send(self, value, target, back=False):
        pairs = self._pairs(target)
        if back:
            pairs = [(b, a) for a, b in pairs]
        return lax.ppermute(value, AXES, pairs)

    def partner(self, value):
        return self.send(value, lambda p, c, m: (p, 1 - c, m))

    def pair_bit(self, value, bit):
        return self.send(value, lambda p, c, m: (p ^ (1 << bit), c, m))

    def mp_bit(self, value, bit):
        return self.send(value, lambda p, c, m: (p, c, m ^ (1 << bit)))

    def cell(self, value, k, back=False):
        return self.send(value, lambda p, c, m: (p, m // 2, 2 * c + ((m % 2) ^ k)), back)

    def shard(self, value, k, back=False):
        return self.send(value, lambda p, c, m: (p, m // 2, m ^ k ^ (2 * c)), back)


def gather_shards(routes, shard):
    got = [routes.shard(shard, k) for k in range(4)]
    chunks = []
    for half in range(2):
        own = jnp.stack([got[half], got[half + 2]])
        order = range(routes.bits) if half else reversed(range(routes.bits))
        pieces = {0: own}
        for bit in order:
            if routes.bits <= 2:
                pieces.update({r | (1 << bit): routes.pair_bit(v, bit) for r, v in list(pieces.items())})
            else:
                keys = sorted(pieces)
                cat = routes.pair_bit(jnp.stack([pieces[r] for r in keys]), bit)
                pieces.update({r | (1 << bit): cat[i] for i, r in enumerate(keys)})
        chunks.append(pieces)
    return chunks


def assemble(pieces, mask):
    count = len(pieces)
    _, rows, width = pieces[0].shape
    full = jnp.zeros((count * 2 * rows, width), pieces[0].dtype)
    for r in range(count):
        for e in range(2):
            full = lax.dynamic_update_slice(full, pieces[r][e], ((((2 * r + e) ^ mask)) * rows, 0))
    return full


def scatter_grads(routes, chunks, mask):
    partial = []
    for half in range(2):
        full = chunks[half]
        count = 1 << routes.bits
        rows = full.shape[0] // (2 * count)
        blocks = full.reshape(2 * count, rows, full.shape[1])
        pieces = {
            r: jnp.stack([lax.dynamic_index_in_dim(blocks, (2 * r + e) ^ mask, 0, keepdims=False) for e in range(2)])
            for r in range(count)
        }
        order = range(routes.bits) if not half else reversed(range(routes.bits))
        for bit in order:
            keys = sorted(r for r in pieces if not r & (1 << bit))
            sent = routes.pair_bit(jnp.stack([pieces[r | (1 << bit)] for r in keys]), bit)
            pieces = {
                r: (pieces[r].astype(F32) + sent[i].astype(F32)).astype(BF16) for i, r in enumerate(keys)
            }
        partial.append(pieces[0])
    total = None
    for k in range(4):
        got = routes.shard(partial[k % 2][k // 2], k, back=True).astype(F32)
        total = got if total is None else total + got
    return total


def gather_norms(routes, norm_params, d, m):
    cur = norm_params
    for bit in range(routes.mp_bits):
        got = routes.mp_bit(cur, bit)
        high = ((m >> bit) & 1) == 1
        cur = jnp.where(high, jnp.concatenate([got, cur], 1), jnp.concatenate([cur, got], 1))
    for bit in range(routes.bits + 1):
        got = routes.partner(cur) if bit == 0 else routes.pair_bit(cur, bit - 1)
        high = ((d >> bit) & 1) == 1
        cur = jnp.where(high, jnp.concatenate([got, cur], 1), jnp.concatenate([cur, got], 1))
    return cur


def scatter_norms(routes, grads, d, m):
    cur = grads
    for bit in reversed(range(routes.bits + 1)):
        low, up = jnp.split(cur, 2, axis=1)
        high = ((d >> bit) & 1) == 1
        give = jnp.where(high, low, up)
        got = routes.partner(give) if bit == 0 else routes.pair_bit(give, bit - 1)
        cur = jnp.where(high, up, low) + got
    for bit in reversed(range(routes.mp_bits)):
        low, up = jnp.split(cur, 2, axis=1)
        high = ((m >> bit) & 1) == 1
        cur = jnp.where(high, up, low) + routes.mp_bit(jnp.where(high, low, up), bit)
    return cur


def per_device(
    inputs, cotangent, gene_counts, step_count, norm_params, norm_first, norm_second,
    attend_weight, attend_first, attend_second, output_weight, output_first, output_second,
    expand_weight, expand_first, expand_second, reduce_weight, reduce_first, reduce_second,
):
    routes = Routes(lax.axis_size("dp"), lax.axis_size("mp"))
    d, m = lax.axis_index("dp"), lax.axis_index("mp")
    c = d % 2
    cells, quarter, _ = inputs.shape
    assert routes.mp == 4 and 2 * cells == routes.mp and routes.dp % 2 == 0
    half = 2 * quarter
    seq = 2 * half
    heads = attend_weight.shape[2] // HEAD_DIM
    width = heads * HEAD_DIM
    m_low, m_high = m % 2, m // 2
    mask = 2 * (d // 2) + ((c + m_high) % 2)

    norm_full = gather_norms(routes, norm_params, d, m)

    def to_cell(values):
        got = [
            routes.cell(lax.dynamic_index_in_dim(values, (m_low + k) % 2, 0, keepdims=False), k) for k in range(2)
        ]
        return jnp.concatenate(got, 0)

    def from_cell(rows):
        rows = rows.astype(BF16)
        got = [routes.cell(rows[k * quarter : (k + 1) * quarter], k, back=True) for k in range(2)]
        flip = m_low == 1
        return jnp.stack([jnp.where(flip, got[1], got[0]), jnp.where(flip, got[0], got[1])]).astype(F32)

    attend_shard = jnp.concatenate(
        [attend_weight[0], attend_weight[1], attend_weight[2], output_weight.T], axis=1
    ).astype(BF16)
    expand_shard = expand_weight.astype(BF16)
    reduce_shard = reduce_weight.T.astype(BF16)

    x_mine = to_cell(inputs).astype(F32)
    attend_w = [assemble(pieces, mask) for pieces in gather_shards(routes, attend_shard)]
    expand_w = [assemble(pieces, mask) for pieces in gather_shards(routes, expand_shard)]
    reduce_w = [assemble(pieces, mask) for pieces in gather_shards(routes, reduce_shard)]
    gy_mine = to_cell(cotangent)

    other_counts = routes.partner(gene_counts)
    mine = jnp.where(m_high == c, gene_counts, other_counts)
    count = jnp.where(m_low == 1, mine[1], mine[0])
    inside = jnp.arange(quarter)
    positions = jnp.concatenate(
        [
            h * half + b * quarter + inside
            for h, b in ((c, m_low), (c, 1 - m_low), (1 - c, m_low), (1 - c, 1 - m_low))
        ]
    )
    bias = jnp.where(positions < 1 + count, 0.0, masked_score).astype(F32)

    def both(rows):
        return jnp.concatenate([rows, routes.partner(rows)], 0)

    def fold(partial):
        return partial[:half] + routes.partner(partial[half:].astype(BF16)).astype(F32)

    normed, scaled_one, inv_one = normalize(x_mine, norm_full[0], norm_full[1])
    h1 = both(normed.astype(BF16))
    qkv = jnp.stack([mm_nn(h1, w[:, : 3 * width]).astype(BF16) for w in attend_w])
    ctx, lse = attend(qkv, bias[None, :], heads)
    branch = mm_nt(ctx[0], attend_w[0][:, 3 * width :]) + mm_nt(ctx[1], attend_w[1][:, 3 * width :])
    x2 = x_mine + fold(branch)
    normed, scaled_two, inv_two = normalize(x2, norm_full[2], norm_full[3])
    h2 = both(normed.astype(BF16))
    hidden = [mm_nn(h2, w) for w in expand_w]
    active = [exact_gelu(u).astype(BF16) for u in hidden]
    branch = mm_nt(active[0], reduce_w[0]) + mm_nt(active[1], reduce_w[1])
    outputs = from_cell(x2 + fold(branch))

    gy = both(gy_mine)
    reduce_grad = [mm_tn(gy, a).astype(BF16) for a in active]
    grad_hidden = [
        jax.vjp(exact_gelu, u)[1](mm_nn(gy, w))[0].astype(BF16) for u, w in zip(hidden, reduce_w)
    ]
    expand_grad = [mm_tn(h2, g).astype(BF16) for g in grad_hidden]
    gh2 = fold(mm_nt(grad_hidden[0], expand_w[0]) + mm_nt(grad_hidden[1], expand_w[1]))
    grad_in, gain_two, shift_two = normalize_back(gh2, scaled_two, inv_two, norm_full[2])
    gx2 = gy_mine.astype(F32) + grad_in
    gb = both(gx2.astype(BF16))
    grad_ctx = jnp.stack([mm_nn(gb, w[:, 3 * width :]).astype(BF16) for w in attend_w])
    gq, gkv = attend_back(qkv, grad_ctx, ctx, lse, bias[:, None], heads)
    attend_grad = [
        jnp.concatenate(
            [mm_tn(h1, gq[i]), mm_tn(h1, gkv[i]), mm_tn(gb, ctx[i])], axis=1
        ).astype(BF16)
        for i in range(2)
    ]
    gh1 = fold(
        sum(
            mm_nt(gq[i], attend_w[i][:, :width]) + mm_nt(gkv[i], attend_w[i][:, width : 3 * width])
            for i in range(2)
        )
    )
    grad_in, gain_one, shift_one = normalize_back(gh1, scaled_one, inv_one, norm_full[0])
    input_grad = from_cell(gx2 + grad_in)

    reduce_sum = scatter_grads(routes, reduce_grad, mask)
    expand_sum = scatter_grads(routes, expand_grad, mask)
    attend_sum = scatter_grads(routes, attend_grad, mask)
    norm_sum = scatter_norms(routes, jnp.stack([gain_one, shift_one, gain_two, shift_two]), d, m)

    step_number = step_count[0].astype(F32)
    norm_new = adam_step(norm_params, norm_first, norm_second, norm_sum, norm_rate, 0.0, step_number)
    attend_reduced = jnp.stack([attend_sum[:, i * width : (i + 1) * width] for i in range(3)])
    attend_new = adam_step(
        attend_weight, attend_first, attend_second, attend_reduced, 2.0 * D ** (-0.5), decay_rate, step_number
    )
    output_new = adam_step(
        output_weight, output_first, output_second, attend_sum[:, 3 * width :].T,
        2.0 * (2 * D // SEQ) ** (-0.5), decay_rate, step_number,
    )
    expand_new = adam_step(
        expand_weight, expand_first, expand_second, expand_sum, 2.0 * D ** (-0.5), decay_rate, step_number
    )
    reduce_new = adam_step(
        reduce_weight, reduce_first, reduce_second, reduce_sum.T, 2.0 * FF ** (-0.5), decay_rate, step_number
    )
    return (
        outputs, input_grad,
        norm_new[0], norm_new[1], norm_new[2][0:2], norm_new[2][2:4],
        *attend_new, *output_new, *expand_new, *reduce_new,
    )


def solution(mesh):
    norms = P(None, ("dp", "mp"))
    attend_spec, col, row = P(None, "dp", "mp"), P("mp", "dp"), P("dp", "mp")
    tokens = P("dp", "mp", None)
    return jax.shard_map(
        per_device,
        mesh=mesh,
        in_specs=(tokens, tokens, P("dp"), P(), norms, norms, norms)
        + (attend_spec,) * 3 + (col,) * 3 + (row,) * 3 + (col,) * 3,
        out_specs=(tokens, tokens, norms, norms, norms, norms)
        + (attend_spec,) * 3 + (col,) * 3 + (row,) * 3 + (col,) * 3,
        check_vma=False,
    )
```

```python
import functools

import jax
import jax.numpy as jnp
from jax import lax
from jax.experimental import pallas as pl
from jax.experimental.pallas import tpu as pltpu
from jax.sharding import PartitionSpec as P

D = 1280
HEAD_DIM = 64
FF = 5120
SEQ = 1024

eps_norm = 1e-05
masked_score = -1e30
beta_one = 0.9
beta_two = 0.95
eps_adam = 1e-08
decay_rate = 0.1
norm_rate = 0.6

F32 = jnp.float32
BF16 = jnp.bfloat16
AXES = ("dp", "mp")


def exact_gelu(values):
    return jax.nn.gelu(values, approximate=False)


def mm(left, right, dims):
    return lax.dot_general(left, right, (dims, ((), ())), preferred_element_type=F32)


def mm_nn(left, right):
    return mm(left, right, ((1,), (0,)))


def mm_nt(left, right):
    return mm(left, right, ((1,), (1,)))


def mm_tn(left, right):
    return mm(left, right, ((0,), (0,)))


def normalize(token_rows, norm_gain, norm_shift):
    mean_row = jnp.mean(token_rows, axis=-1, keepdims=True)
    centred = token_rows - mean_row
    inv_std = lax.rsqrt(jnp.mean(centred * centred, axis=-1, keepdims=True) + eps_norm)
    scaled = centred * inv_std
    return (scaled * norm_gain + norm_shift, scaled, inv_std)


def normalize_back(grad_out, scaled, inv_std, norm_gain):
    grad_scaled = grad_out * norm_gain
    centre_part = jnp.mean(grad_scaled, axis=-1, keepdims=True)
    along_part = scaled * jnp.mean(grad_scaled * scaled, axis=-1, keepdims=True)
    grad_in = inv_std * (grad_scaled - centre_part - along_part)
    return (grad_in, jnp.sum(grad_out * scaled, axis=0), jnp.sum(grad_out, axis=0))


def adam_step(weight, first_moment, second_moment, gradient, rate, decay, step_number):
    first_new = beta_one * first_moment + (1.0 - beta_one) * gradient
    second_new = beta_two * second_moment + (1.0 - beta_two) * gradient * gradient
    corr_one = 1.0 - jnp.power(beta_one, step_number)
    corr_two = 1.0 - jnp.power(beta_two, step_number)
    update = first_new / corr_one / (jnp.sqrt(second_new / corr_two) + eps_adam)
    return (weight - rate * (update + decay * weight), first_new, second_new)


def attend_kernel(heads, block, bias_ref, q_ref, kv_ref, ctx_ref, lse_ref):
    width = heads * HEAD_DIM
    bias = bias_ref[...]
    for h in range(heads):
        lo = h * HEAD_DIM
        q = q_ref[0, :, lo : lo + HEAD_DIM] * jnp.asarray(HEAD_DIM**-0.5, BF16)
        k = kv_ref[0, :, width + lo : width + lo + HEAD_DIM]
        v = kv_ref[0, :, 2 * width + lo : 2 * width + lo + HEAD_DIM]
        s = mm_nt(q, k) + bias
        top = jnp.max(s, axis=-1, keepdims=True)
        e = jnp.exp(s - top)
        total = jnp.sum(e, axis=-1, keepdims=True)
        ctx = mm_nn(e.astype(BF16), v) / total
        ctx_ref[0, :, lo : lo + HEAD_DIM] = ctx.astype(BF16)
        lse_ref[0, :, h : h + 1] = top + jnp.log(total)


def attend(qkv, bias, heads):
    chunks, seq, _ = qkv.shape
    block = min(256, seq)
    width = heads * HEAD_DIM
    return pl.pallas_call(
        functools.partial(attend_kernel, heads, block),
        grid=(chunks, seq // block),
        in_specs=[
            pl.BlockSpec((1, seq), lambda i, j: (0, 0)),
            pl.BlockSpec((1, block, 3 * width), lambda i, j: (i, j, 0)),
            pl.BlockSpec((1, seq, 3 * width), lambda i, j: (i, 0, 0)),
        ],
        out_specs=[
            pl.BlockSpec((1, block, width), lambda i, j: (i, j, 0)),
            pl.BlockSpec((1, block, 8), lambda i, j: (i, j, 0)),
        ],
        out_shape=[
            jax.ShapeDtypeStruct((chunks, seq, width), BF16),
            jax.ShapeDtypeStruct((chunks, seq, 8), F32),
        ],
        cost_estimate=pl.CostEstimate(
            flops=16 * chunks * heads * seq * seq * HEAD_DIM,
            bytes_accessed=8 * chunks * seq * width,
            transcendentals=chunks * heads * seq * seq,
        ),
        name="attend",
    )(bias, qkv, qkv)


def attend_back_kernel(heads, bias_ref, q_ref, g_ref, o_ref, lse_ref, kv_ref, gq_ref, gkv_ref, acc_ref):
    width = heads * HEAD_DIM
    step = pl.program_id(1)
    scale = HEAD_DIM**-0.5

    @pl.when(step == 0)
    def _():
        acc_ref[...] = jnp.zeros_like(acc_ref)

    bias = bias_ref[...]
    lse_rows = lse_ref[0].T
    for h in range(heads):
        lo = h * HEAD_DIM
        q = q_ref[0, :, lo : lo + HEAD_DIM] * jnp.asarray(scale, BF16)
        g = g_ref[0, :, lo : lo + HEAD_DIM]
        o = o_ref[0, :, lo : lo + HEAD_DIM]
        k = kv_ref[0, :, width + lo : width + lo + HEAD_DIM]
        v = kv_ref[0, :, 2 * width + lo : 2 * width + lo + HEAD_DIM]
        delta = jnp.sum(g.astype(F32) * o.astype(F32), axis=-1, keepdims=True).T
        st = mm_nt(k, q) + bias
        pt = jnp.exp(st - lse_rows[h : h + 1, :])
        gpt = mm_nt(v, g)
        gst = (pt * (gpt - delta)).astype(BF16)
        acc_ref[:, width + lo : width + lo + HEAD_DIM] += mm_nn(pt.astype(BF16), g)
        acc_ref[:, lo : lo + HEAD_DIM] += mm_nn(gst, q)
        gq_ref[0, :, lo : lo + HEAD_DIM] = (mm_tn(gst, k) * scale).astype(BF16)

    @pl.when(step == pl.num_programs(1) - 1)
    def _():
        gkv_ref[0] = acc_ref[...].astype(BF16)


def attend_back(qkv, grad_ctx, ctx, lse, bias_col, heads):
    chunks, seq, _ = qkv.shape
    block = min(256, seq)
    width = heads * HEAD_DIM
    return pl.pallas_call(
        functools.partial(attend_back_kernel, heads),
        grid=(chunks, seq // block),
        in_specs=[
            pl.BlockSpec((seq, 1), lambda i, j: (0, 0)),
            pl.BlockSpec((1, block, 3 * width), lambda i, j: (i, j, 0)),
            pl.BlockSpec((1, block, width), lambda i, j: (i, j, 0)),
            pl.BlockSpec((1, block, width), lambda i, j: (i, j, 0)),
            pl.BlockSpec((1, block, 8), lambda i, j: (i, j, 0)),
            pl.BlockSpec((1, seq, 3 * width), lambda i, j: (i, 0, 0)),
        ],
        out_specs=[
            pl.BlockSpec((1, block, width), lambda i, j: (i, j, 0)),
            pl.BlockSpec((1, seq, 2 * width), lambda i, j: (i, 0, 0)),
        ],
        out_shape=[
            jax.ShapeDtypeStruct((chunks, seq, width), BF16),
            jax.ShapeDtypeStruct((chunks, seq, 2 * width), BF16),
        ],
        scratch_shapes=[pltpu.VMEM((seq, 2 * width), F32)],
        cost_estimate=pl.CostEstimate(
            flops=40 * chunks * heads * seq * seq * HEAD_DIM,
            bytes_accessed=20 * chunks * seq * width,
            transcendentals=chunks * heads * seq * seq,
        ),
        name="attend_back",
    )(bias_col, qkv, grad_ctx, ctx, lse, qkv)


class Routes:
    def __init__(self, dp_size, mp_size):
        self.dp, self.mp = dp_size, mp_size
        self.bits = (dp_size // 2).bit_length() - 1
        self.mp_bits = mp_size.bit_length() - 1

    def _pairs(self, target):
        pairs = []
        for d in range(self.dp):
            for m in range(self.mp):
                dest = target(d // 2, d % 2, m)
                pairs.append((d * self.mp + m, (dest[0] * 2 + dest[1]) * self.mp + dest[2]))
        return pairs

    def send(self, value, target, back=False):
        pairs = self._pairs(target)
        if back:
            pairs = [(b, a) for a, b in pairs]
        return lax.ppermute(value, AXES, pairs)

    def partner(self, value):
        return self.send(value, lambda p, c, m: (p, 1 - c, m))

    def pair_bit(self, value, bit):
        return self.send(value, lambda p, c, m: (p ^ (1 << bit), c, m))

    def mp_bit(self, value, bit):
        return self.send(value, lambda p, c, m: (p, c, m ^ (1 << bit)))

    def cell(self, value, k, back=False):
        return self.send(value, lambda p, c, m: (p, m // 2, 2 * c + ((m % 2) ^ k)), back)

    def shard(self, value, k, back=False):
        return self.send(value, lambda p, c, m: (p, m // 2, m ^ k ^ (2 * c)), back)


def gather_shards(routes, shard):
    got = [routes.shard(shard, k) for k in range(4)]
    chunks = []
    for half in range(2):
        own = jnp.stack([got[half], got[half + 2]])
        order = range(routes.bits) if half else reversed(range(routes.bits))
        pieces = {0: own}
        for bit in order:
            if routes.bits <= 2:
                pieces.update({r | (1 << bit): routes.pair_bit(v, bit) for r, v in list(pieces.items())})
            else:
                keys = sorted(pieces)
                cat = routes.pair_bit(jnp.stack([pieces[r] for r in keys]), bit)
                pieces.update({r | (1 << bit): cat[i] for i, r in enumerate(keys)})
        chunks.append(pieces)
    return chunks


def assemble(pieces, mask):
    count = len(pieces)
    _, rows, width = pieces[0].shape
    full = jnp.zeros((count * 2 * rows, width), pieces[0].dtype)
    for r in range(count):
        for e in range(2):
            full = lax.dynamic_update_slice(full, pieces[r][e], ((((2 * r + e) ^ mask)) * rows, 0))
    return full


def scatter_grads(routes, chunks, mask):
    partial = []
    for half in range(2):
        full = chunks[half]
        count = 1 << routes.bits
        rows = full.shape[0] // (2 * count)
        blocks = full.reshape(2 * count, rows, full.shape[1])
        pieces = {
            r: jnp.stack([lax.dynamic_index_in_dim(blocks, (2 * r + e) ^ mask, 0, keepdims=False) for e in range(2)])
            for r in range(count)
        }
        order = range(routes.bits) if not half else reversed(range(routes.bits))
        for bit in order:
            keys = sorted(r for r in pieces if not r & (1 << bit))
            sent = routes.pair_bit(jnp.stack([pieces[r | (1 << bit)] for r in keys]), bit)
            pieces = {
                r: (pieces[r].astype(F32) + sent[i].astype(F32)).astype(BF16) for i, r in enumerate(keys)
            }
        partial.append(pieces[0])
    total = None
    for k in range(4):
        got = routes.shard(partial[k % 2][k // 2], k, back=True).astype(F32)
        total = got if total is None else total + got
    return total


MESH = pl.DeviceIdType.MESH


class Here:
    def __init__(self):
        self.d, self.m = lax.axis_index("dp"), lax.axis_index("mp")
        self.c = self.d % 2
        self.pair = self.d - self.c
        self.x = (self.d // 2) % 2
        self.y = self.d // 4
        self.t = self.m // 2
        self.b = self.m % 2
        self.over_x = {"dp": self.d + 2 - 4 * self.x, "mp": self.m}
        self.over_y = {"dp": self.d + 4 - 8 * self.y, "mp": self.m}
        self.partner = {"dp": self.d + 1 - 2 * self.c, "mp": self.m}
        self.home = self.t == self.c

    def at(self, core, m):
        return {"dp": self.pair + core, "mp": m}


def remote(src, dst, ssem, rsem, dev):
    return pltpu.make_async_remote_copy(
        src_ref=src, dst_ref=dst, send_sem=ssem, recv_sem=rsem, device_id=dev, device_id_type=MESH
    )


def arrived(dst, rsem, dev):
    remote(dst, dst, rsem, rsem, dev).wait_recv()


class Maybe:
    def __init__(self, src, dst, ssem, rsem, dev, own):
        self.args, self.dev, self.ssem, self.own = (src, dst), dev, ssem, own
        self.rsem = rsem

    def far(self):
        return remote(*self.args, self.ssem, self.rsem, self.dev)

    def start(self):
        pl.when(self.own)(lambda: pltpu.make_async_copy(*self.args, self.rsem).start())
        pl.when(jnp.logical_not(self.own))(lambda: self.far().start())

    def wait_send(self):
        pl.when(jnp.logical_not(self.own))(lambda: self.far().wait_send())


def greet(sources, count):
    barrier = pltpu.get_barrier_semaphore()

    def tell(dev):
        pl.semaphore_signal(barrier, inc=1, device_id=dev, device_id_type=MESH)

    for dev, own in sources:
        if own is None:
            tell(dev)
        else:
            pl.when(jnp.logical_not(own))(functools.partial(tell, dev))
    pl.semaphore_wait(barrier, count)


class Gather:
    def __init__(self, here, shard, full, sems):
        (self.send_z, self.got_z, self.send_x, self.send_y, self.got_x, self.got_y, self.send_r, self.got_r) = sems
        self.here, self.shard, self.full = here, shard, full
        self.rows = shard.shape[0]
        self.first = jnp.where(here.m > 2 * here.c, 1, 0)

    @staticmethod
    def scratch():
        dma = pltpu.SemaphoreType.DMA
        return [dma((4,)), dma((2, 2))] + [dma((2, 2))] * 6

    def plane(self, i):
        return (self.first + i) % 2

    def block(self, i, dp):
        return self.full.at[self.plane(i), pl.ds(dp * self.rows, self.rows), :]

    def z_copy(self, m):
        h = self.here
        dst = self.full.at[h.b, pl.ds(h.d * self.rows, self.rows), :]
        own = jnp.logical_and(h.home, h.m == m)
        return Maybe(self.shard, dst, self.send_z.at[m], self.got_z.at[h.b, h.c], h.at(h.t, m), own)

    def start_z(self):
        for m in range(4):
            self.z_copy(m).start()

    def own_copies(self, i, e):
        h = self.here
        ref = self.block(i, h.pair + e)
        return (
            remote(ref, ref, self.send_x.at[i, e], self.got_x.at[i, e], h.over_x),
            remote(ref, ref, self.send_y.at[i, e], self.got_y.at[i, e], h.over_y),
        )

    def spread(self, i):
        h = self.here
        for e in range(2):
            arrived(self.block(i, h.pair + e), self.got_z.at[self.plane(i), e], h.partner)
            for copy in self.own_copies(i, e):
                copy.start()

    def relay_copy(self, i, e):
        h = self.here
        if i == 0:
            ref, dev = self.block(i, h.over_y["dp"] - h.c + e), h.over_x
        else:
            ref, dev = self.block(i, h.over_x["dp"] - h.c + e), h.over_y
        return remote(ref, ref, self.send_r.at[i, e], self.got_r.at[i, e], dev)

    def relay(self, i):
        h = self.here
        for e in range(2):
            if i == 0:
                arrived(self.block(i, h.over_y["dp"] - h.c + e), self.got_y.at[i, e], h.over_y)
            else:
                arrived(self.block(i, h.over_x["dp"] - h.c + e), self.got_x.at[i, e], h.over_x)
            self.relay_copy(i, e).start()

    def finish(self):
        h = self.here
        diagonal = h.pair + 2 - 4 * h.x + 4 - 8 * h.y
        for i in range(2):
            for e in range(2):
                if i == 0:
                    arrived(self.block(i, h.over_x["dp"] - h.c + e), self.got_x.at[i, e], h.over_x)
                else:
                    arrived(self.block(i, h.over_y["dp"] - h.c + e), self.got_y.at[i, e], h.over_y)
                arrived(self.block(i, diagonal + e), self.got_r.at[i, e], h.over_x)
        for m in range(4):
            self.z_copy(m).wait_send()
        for i in range(2):
            for e in range(2):
                for copy in self.own_copies(i, e):
                    copy.wait_send()
                self.relay_copy(i, e).wait_send()


class ToCell:
    def __init__(self, here, source, rows, send, got):
        self.here, self.source, self.rows, self.send, self.got = here, source, rows, send, got

    def copy(self, s):
        h = self.here
        target = 2 * h.c + s
        own = jnp.logical_and(h.home, h.m == target)
        return Maybe(self.source.at[s], self.rows.at[h.b], self.send.at[s], self.got.at[h.b], h.at(h.t, target), own)

    def start(self):
        for s in range(2):
            self.copy(s).start()

    def wait(self):
        for b in range(2):
            arrived(self.rows.at[b], self.got.at[b], self.here.partner)

    def finish(self):
        for s in range(2):
            self.copy(s).wait_send()


def spread_ends(here):
    h = here
    takers = [(h.at(h.t, m), jnp.logical_and(h.home, h.m == m)) for m in range(4)]
    givers = [(h.at(e, 2 * h.c + b), jnp.logical_and(h.home, jnp.logical_and(h.b == b, h.c == e))) for e in range(2) for b in range(2)]
    return takers, givers


def greet_cross(here, sources, *others):
    others = [here.over_x, here.over_y, *others]
    greet(sources + [(dev, None) for dev in others], 4 + len(others) - here.home.astype(jnp.int32))


def norm_rows(values, gain, shift):
    mean_row = jnp.mean(values, axis=-1, keepdims=True)
    centred = values - mean_row
    inv_std = lax.rsqrt(jnp.mean(centred * centred, axis=-1, keepdims=True) + eps_norm)
    return centred * inv_std * gain + shift


def gather_first_kernel(x_ref, shard_ref, norm_ref, full_ref, h_ref, x_out, *sems):
    here = Here()
    send_x, got_x, send_h, got_h = sems[:4]
    greet_cross(here, spread_ends(here)[1], here.partner)
    block = Gather(here, shard_ref, full_ref, sems[4:])
    cell = ToCell(here, x_ref, x_out, send_x, got_x)
    block.start_z()
    cell.start()
    block.spread(0)
    block.spread(1)
    cell.wait()
    quarter = x_out.shape[1]
    for b in range(2):
        h_ref[0, pl.ds(b * quarter, quarter), :] = norm_rows(
            x_out[b].astype(F32), norm_ref[0:1, :], norm_ref[1:2, :]
        ).astype(BF16)
    swap = remote(h_ref.at[0], h_ref.at[1], send_h, got_h, here.partner)
    swap.start()
    block.relay(0)
    block.relay(1)
    block.finish()
    cell.finish()
    swap.wait()


ANY = pl.BlockSpec(memory_space=pl.ANY)
VMEM = pl.BlockSpec(memory_space=pltpu.VMEM)


def gather_first(inputs, shard, norms, collective):
    cells, quarter, width = inputs.shape
    rows = shard.shape[0]
    dma = pltpu.SemaphoreType.DMA
    return pl.pallas_call(
        gather_first_kernel,
        out_shape=[
            jax.ShapeDtypeStruct((2, 8 * rows, width), BF16),
            jax.ShapeDtypeStruct((2, 2 * quarter, width), BF16),
            jax.ShapeDtypeStruct((2, quarter, width), BF16),
        ],
        in_specs=[VMEM, VMEM, VMEM],
        out_specs=[ANY, VMEM, VMEM],
        scratch_shapes=[dma((2,)), dma((2,)), dma, dma] + Gather.scratch(),
        compiler_params=pltpu.CompilerParams(collective_id=collective, has_side_effects=True),
        name="gather_first",
    )(inputs, shard, norms)


def gather_rest_kernel(gy_ref, shard_one, shard_two, full_one, full_two, gy_out, *sems):
    here = Here()
    send_g, got_g = sems[:2]
    greet_cross(here, spread_ends(here)[1])
    blocks = [Gather(here, shard_one, full_one, sems[2:10]), Gather(here, shard_two, full_two, sems[10:18])]
    cell = ToCell(here, gy_ref, gy_out, send_g, got_g)
    for block in blocks:
        block.start_z()
    cell.start()
    for block in blocks:
        block.spread(0)
        block.spread(1)
        block.relay(0)
        block.relay(1)
    for block in blocks:
        block.finish()
    cell.wait()
    cell.finish()


def gather_rest(cotangent, shard_one, shard_two, collective):
    cells, quarter, width = cotangent.shape
    rows = shard_one.shape[0]
    dma = pltpu.SemaphoreType.DMA
    return pl.pallas_call(
        gather_rest_kernel,
        out_shape=[jax.ShapeDtypeStruct((2, 8 * rows, width), BF16)] * 2
        + [jax.ShapeDtypeStruct((2, quarter, width), BF16)],
        in_specs=[VMEM] * 3,
        out_specs=[ANY] * 3,
        scratch_shapes=[dma((2,)), dma((2,))] + Gather.scratch() * 2,
        compiler_params=pltpu.CompilerParams(collective_id=collective, has_side_effects=True),
        name="gather_rest",
    )(cotangent, shard_one, shard_two)


class Reduce:
    def __init__(self, here, grads, bufs, sems):
        self.here, self.grads = here, grads
        self.own, self.one, self.two, self.part, self.last = bufs
        self.sem_own, self.send_one, self.got_one, self.send_two, self.got_two, self.send_z, self.got_z = sems
        self.piece = self.own.shape[3]

    @staticmethod
    def scratch(rows, width):
        r = rows // 2
        dma = pltpu.SemaphoreType.DMA
        return [
            pltpu.VMEM((2, 2, 4, r, width), BF16),
            pltpu.VMEM((2, 2, 4, r, width), BF16),
            pltpu.VMEM((2, 4, r, width), BF16),
            pltpu.VMEM((2, 4, r, width), BF16),
            pltpu.VMEM((4, 2, r, width), BF16),
        ], [dma((2, 2, 4)), dma((2, 2, 4)), dma((2, 2, 4)), dma((2, 4)), dma((2, 4)), dma((2, 4)), dma((4, 2))]

    def rows_of(self, role, dp, j):
        return self.grads.at[role, pl.ds(dp * 2 * self.piece + j * self.piece, self.piece), :]

    def pair_at(self, role, n, far):
        h = self.here
        dx, dy = 2 - 4 * h.x, 4 - 8 * h.y
        first, second = (dx, dy) if role == 0 else (dy, dx)
        return h.pair + (first if far else 0) + (second if n == 0 else 0)

    def load(self, role, n, j):
        return pltpu.make_async_copy(
            self.rows_of(role, self.pair_at(role, n, False), j), self.own.at[role, n, j], self.sem_own.at[role, n, j]
        )

    def copy_one(self, role, n, j):
        dev = self.here.over_x if role == 0 else self.here.over_y
        return remote(
            self.rows_of(role, self.pair_at(role, n, True), j), self.one.at[role, n, j],
            self.send_one.at[role, n, j], self.got_one.at[role, n, j], dev,
        )

    def copy_two(self, role, j):
        dev = self.here.over_y if role == 0 else self.here.over_x
        return remote(
            self.own.at[role, 0, j], self.two.at[role, j], self.send_two.at[role, j], self.got_two.at[role, j], dev
        )

    def copy_z(self, role, j):
        h = self.here
        core, target = j // 2, 2 * h.c + role
        own = jnp.logical_and(h.c == core, h.m == target)
        return Maybe(
            self.part.at[role, j], self.last.at[h.m, j % 2], self.send_z.at[role, j], self.got_z.at[h.m, j % 2],
            h.at(core, target), own,
        )

    def start(self):
        for j in range(4):
            for n in range(2):
                for role in range(2):
                    self.copy_one(role, n, j).start()
                    self.load(role, n, j).start()

    def add_one(self, role, j):
        h = self.here
        for n in range(2):
            self.load(role, n, j).wait()
            arrived(self.one.at[role, n, j], self.got_one.at[role, n, j], h.over_x)
            total = self.own[role, n, j].astype(F32) + self.one[role, n, j].astype(F32)
            self.own[role, n, j] = total.astype(BF16)
            if n == 0:
                self.copy_two(role, j).start()

    def add_two(self, role, j):
        arrived(self.two.at[role, j], self.got_two.at[role, j], self.here.over_x)
        total = self.own[role, 1, j].astype(F32) + self.two[role, j].astype(F32)
        self.part[role, j] = total.astype(BF16)
        self.copy_z(role, j).start()

    def finish(self, out_ref):
        h = self.here
        for s in range(2):
            for m in range(4):
                arrived(self.last.at[m, s], self.got_z.at[m, s], h.partner)
            total = self.last[0, s].astype(F32)
            for m in range(1, 4):
                total = total + self.last[m, s].astype(F32)
            out_ref[pl.ds(s * self.piece, self.piece), :] = total
        for role in range(2):
            for j in range(4):
                for n in range(2):
                    self.copy_one(role, n, j).wait_send()
                self.copy_two(role, j).wait_send()
                self.copy_z(role, j).wait_send()


def reduce_kernel(grads_ref, out_ref, *scratch):
    here = Here()
    greet_cross(here, spread_ends(here)[0])
    block = Reduce(here, grads_ref, scratch[:5], scratch[5:])
    block.start()
    for j in range(4):
        for role in range(2):
            block.add_one(role, j)
        if j >= 1:
            for role in range(2):
                block.add_two(role, j - 1)
    for role in range(2):
        block.add_two(role, 3)
    block.finish(out_ref)


def reduce_block(grads, collective):
    _, full, width = grads.shape
    rows = full // 8
    bufs, sems = Reduce.scratch(rows, width)
    return pl.pallas_call(
        reduce_kernel,
        out_shape=jax.ShapeDtypeStruct((rows, width), F32),
        in_specs=[ANY],
        out_specs=VMEM,
        scratch_shapes=bufs + sems,
        compiler_params=pltpu.CompilerParams(collective_id=collective, has_side_effects=True),
        name="reduce_block",
    )(grads)


def gather_norms(routes, norm_params, d, m):
    cur = norm_params
    for bit in range(routes.mp_bits):
        got = routes.mp_bit(cur, bit)
        high = ((m >> bit) & 1) == 1
        cur = jnp.where(high, jnp.concatenate([got, cur], 1), jnp.concatenate([cur, got], 1))
    for bit in range(routes.bits + 1):
        got = routes.partner(cur) if bit == 0 else routes.pair_bit(cur, bit - 1)
        high = ((d >> bit) & 1) == 1
        cur = jnp.where(high, jnp.concatenate([got, cur], 1), jnp.concatenate([cur, got], 1))
    return cur


def scatter_norms(routes, grads, d, m):
    cur = grads
    for bit in reversed(range(routes.bits + 1)):
        low, up = jnp.split(cur, 2, axis=1)
        high = ((d >> bit) & 1) == 1
        give = jnp.where(high, low, up)
        got = routes.partner(give) if bit == 0 else routes.pair_bit(give, bit - 1)
        cur = jnp.where(high, up, low) + got
    for bit in reversed(range(routes.mp_bits)):
        low, up = jnp.split(cur, 2, axis=1)
        high = ((m >> bit) & 1) == 1
        cur = jnp.where(high, up, low) + routes.mp_bit(jnp.where(high, low, up), bit)
    return cur


def per_device(
    inputs, cotangent, gene_counts, step_count, norm_params, norm_first, norm_second,
    attend_weight, attend_first, attend_second, output_weight, output_first, output_second,
    expand_weight, expand_first, expand_second, reduce_weight, reduce_first, reduce_second,
):
    routes = Routes(lax.axis_size("dp"), lax.axis_size("mp"))
    d, m = lax.axis_index("dp"), lax.axis_index("mp")
    c = d % 2
    cells, quarter, _ = inputs.shape
    assert routes.mp == 4 and 2 * cells == routes.mp and routes.dp % 2 == 0
    half = 2 * quarter
    seq = 2 * half
    heads = attend_weight.shape[2] // HEAD_DIM
    width = heads * HEAD_DIM
    m_low, m_high = m % 2, m // 2
    mask = 2 * (d // 2) + ((c + m_high) % 2)

    norm_full = gather_norms(routes, norm_params, d, m)

    def to_cell(values):
        got = [
            routes.cell(lax.dynamic_index_in_dim(values, (m_low + k) % 2, 0, keepdims=False), k) for k in range(2)
        ]
        return jnp.concatenate(got, 0)

    def from_cell(rows):
        rows = rows.astype(BF16)
        if kernels:
            flip_rows = jnp.concatenate([rows[quarter:], rows[:quarter]], 0)
            rows = jnp.where(m_low == 1, flip_rows, rows)
        got = [routes.cell(rows[k * quarter : (k + 1) * quarter], k, back=True) for k in range(2)]
        flip = m_low == 1
        return jnp.stack([jnp.where(flip, got[1], got[0]), jnp.where(flip, got[0], got[1])]).astype(F32)

    attend_shard = jnp.concatenate(
        [attend_weight[0], attend_weight[1], attend_weight[2], output_weight.T], axis=1
    ).astype(BF16)
    expand_shard = expand_weight.astype(BF16)
    reduce_shard = reduce_weight.T.astype(BF16)

    kernels = routes.dp == 8 and routes.mp == 4
    if kernels:
        attend_w, h1, x_mine = gather_first(inputs, attend_shard, norm_full[0:2], 1)
        x_mine = x_mine.reshape(half, -1).astype(F32)
        expand_w, reduce_w, gy_mine = gather_rest(cotangent, expand_shard, reduce_shard, 2)
        gy_mine = gy_mine.reshape(half, -1)
    else:
        x_mine = to_cell(inputs).astype(F32)
        attend_w = [assemble(pieces, mask) for pieces in gather_shards(routes, attend_shard)]
        expand_w = [assemble(pieces, mask) for pieces in gather_shards(routes, expand_shard)]
        reduce_w = [assemble(pieces, mask) for pieces in gather_shards(routes, reduce_shard)]
        gy_mine = to_cell(cotangent)

    other_counts = routes.partner(gene_counts)
    mine = jnp.where(m_high == c, gene_counts, other_counts)
    count = jnp.where(m_low == 1, mine[1], mine[0])
    inside = jnp.arange(quarter)
    first = 0 if kernels else m_low
    positions = jnp.concatenate(
        [h * half + b * quarter + inside for h, b in ((c, first), (c, 1 - first), (1 - c, first), (1 - c, 1 - first))]
    )
    bias = jnp.where(positions < 1 + count, 0.0, masked_score).astype(F32)

    def both(rows):
        return jnp.concatenate([rows, routes.partner(rows)], 0)

    def fold(partial):
        return partial[:half] + routes.partner(partial[half:].astype(BF16)).astype(F32)

    normed, scaled_one, inv_one = normalize(x_mine, norm_full[0], norm_full[1])
    h1 = h1.reshape(seq, -1) if kernels else both(normed.astype(BF16))
    qkv = jnp.stack([mm_nn(h1, w[:, : 3 * width]).astype(BF16) for w in attend_w])
    ctx, lse = attend(qkv, bias[None, :], heads)
    branch = mm_nt(ctx[0], attend_w[0][:, 3 * width :]) + mm_nt(ctx[1], attend_w[1][:, 3 * width :])
    x2 = x_mine + fold(branch)
    normed, scaled_two, inv_two = normalize(x2, norm_full[2], norm_full[3])
    h2 = both(normed.astype(BF16))
    hidden = [mm_nn(h2, w) for w in expand_w]
    active = [exact_gelu(u).astype(BF16) for u in hidden]
    branch = mm_nt(active[0], reduce_w[0]) + mm_nt(active[1], reduce_w[1])
    outputs = from_cell(x2 + fold(branch))

    gy = both(gy_mine)
    reduce_grad = [mm_tn(gy, a).astype(BF16) for a in active]
    grad_hidden = [
        jax.vjp(exact_gelu, u)[1](mm_nn(gy, w))[0].astype(BF16) for u, w in zip(hidden, reduce_w)
    ]
    expand_grad = [mm_tn(h2, g).astype(BF16) for g in grad_hidden]
    gh2 = fold(mm_nt(grad_hidden[0], expand_w[0]) + mm_nt(grad_hidden[1], expand_w[1]))
    grad_in, gain_two, shift_two = normalize_back(gh2, scaled_two, inv_two, norm_full[2])
    gx2 = gy_mine.astype(F32) + grad_in
    gb = both(gx2.astype(BF16))
    grad_ctx = jnp.stack([mm_nn(gb, w[:, 3 * width :]).astype(BF16) for w in attend_w])
    gq, gkv = attend_back(qkv, grad_ctx, ctx, lse, bias[:, None], heads)
    attend_grad = [
        jnp.concatenate(
            [mm_tn(h1, gq[i]), mm_tn(h1, gkv[i]), mm_tn(gb, ctx[i])], axis=1
        ).astype(BF16)
        for i in range(2)
    ]
    gh1 = fold(
        sum(
            mm_nt(gq[i], attend_w[i][:, :width]) + mm_nt(gkv[i], attend_w[i][:, width : 3 * width])
            for i in range(2)
        )
    )
    grad_in, gain_one, shift_one = normalize_back(gh1, scaled_one, inv_one, norm_full[0])
    input_grad = from_cell(gx2 + grad_in)

    if kernels:
        reduce_sum = reduce_block(jnp.stack(reduce_grad), 3)
        expand_sum = reduce_block(jnp.stack(expand_grad), 3)
        attend_sum = reduce_block(jnp.stack(attend_grad), 3)
    else:
        reduce_sum = scatter_grads(routes, reduce_grad, mask)
        expand_sum = scatter_grads(routes, expand_grad, mask)
        attend_sum = scatter_grads(routes, attend_grad, mask)
    norm_sum = scatter_norms(routes, jnp.stack([gain_one, shift_one, gain_two, shift_two]), d, m)

    step_number = step_count[0].astype(F32)
    norm_new = adam_step(norm_params, norm_first, norm_second, norm_sum, norm_rate, 0.0, step_number)
    attend_reduced = jnp.stack([attend_sum[:, i * width : (i + 1) * width] for i in range(3)])
    attend_new = adam_step(
        attend_weight, attend_first, attend_second, attend_reduced, 2.0 * D ** (-0.5), decay_rate, step_number
    )
    output_new = adam_step(
        output_weight, output_first, output_second, attend_sum[:, 3 * width :].T,
        2.0 * (2 * D // SEQ) ** (-0.5), decay_rate, step_number,
    )
    expand_new = adam_step(
        expand_weight, expand_first, expand_second, expand_sum, 2.0 * D ** (-0.5), decay_rate, step_number
    )
    reduce_new = adam_step(
        reduce_weight, reduce_first, reduce_second, reduce_sum.T, 2.0 * FF ** (-0.5), decay_rate, step_number
    )
    return (
        outputs, input_grad,
        norm_new[0], norm_new[1], norm_new[2][0:2], norm_new[2][2:4],
        *attend_new, *output_new, *expand_new, *reduce_new,
    )


def solution(mesh):
    norms = P(None, ("dp", "mp"))
    attend_spec, col, row = P(None, "dp", "mp"), P("mp", "dp"), P("dp", "mp")
    tokens = P("dp", "mp", None)
    return jax.shard_map(
        per_device,
        mesh=mesh,
        in_specs=(tokens, tokens, P("dp"), P(), norms, norms, norms)
        + (attend_spec,) * 3 + (col,) * 3 + (row,) * 3 + (col,) * 3,
        out_specs=(tokens, tokens, norms, norms, norms, norms)
        + (attend_spec,) * 3 + (col,) * 3 + (row,) * 3 + (col,) * 3,
        check_vma=False,
    )
```

```python
import functools

import jax
import jax.numpy as jnp
from jax import lax
from jax.experimental import pallas as pl
from jax.experimental.pallas import tpu as pltpu
from jax.sharding import PartitionSpec as P

D = 1280
HEAD_DIM = 64
FF = 5120
SEQ = 1024

eps_norm = 1e-05
masked_score = -1e30
beta_one = 0.9
beta_two = 0.95
eps_adam = 1e-08
decay_rate = 0.1
norm_rate = 0.6

F32 = jnp.float32
BF16 = jnp.bfloat16
AXES = ("dp", "mp")


def exact_gelu(values):
    return jax.nn.gelu(values, approximate=False)


def mm(left, right, dims):
    return lax.dot_general(left, right, (dims, ((), ())), preferred_element_type=F32)


def mm_nn(left, right):
    return mm(left, right, ((1,), (0,)))


def mm_nt(left, right):
    return mm(left, right, ((1,), (1,)))


def mm_tn(left, right):
    return mm(left, right, ((0,), (0,)))


def normalize(token_rows, norm_gain, norm_shift):
    mean_row = jnp.mean(token_rows, axis=-1, keepdims=True)
    centred = token_rows - mean_row
    inv_std = lax.rsqrt(jnp.mean(centred * centred, axis=-1, keepdims=True) + eps_norm)
    scaled = centred * inv_std
    return (scaled * norm_gain + norm_shift, scaled, inv_std)


def normalize_back(grad_out, scaled, inv_std, norm_gain):
    grad_scaled = grad_out * norm_gain
    centre_part = jnp.mean(grad_scaled, axis=-1, keepdims=True)
    along_part = scaled * jnp.mean(grad_scaled * scaled, axis=-1, keepdims=True)
    grad_in = inv_std * (grad_scaled - centre_part - along_part)
    return (grad_in, jnp.sum(grad_out * scaled, axis=0), jnp.sum(grad_out, axis=0))


def adam_step(weight, first_moment, second_moment, gradient, rate, decay, step_number):
    first_new = beta_one * first_moment + (1.0 - beta_one) * gradient
    second_new = beta_two * second_moment + (1.0 - beta_two) * gradient * gradient
    corr_one = 1.0 - jnp.power(beta_one, step_number)
    corr_two = 1.0 - jnp.power(beta_two, step_number)
    update = first_new / corr_one / (jnp.sqrt(second_new / corr_two) + eps_adam)
    return (weight - rate * (update + decay * weight), first_new, second_new)


def attend_kernel(heads, block, bias_ref, q_ref, kv_ref, ctx_ref, lse_ref):
    width = heads * HEAD_DIM
    bias = bias_ref[...]
    for h in range(heads):
        lo = h * HEAD_DIM
        q = q_ref[0, :, lo : lo + HEAD_DIM] * jnp.asarray(HEAD_DIM**-0.5, BF16)
        k = kv_ref[0, :, width + lo : width + lo + HEAD_DIM]
        v = kv_ref[0, :, 2 * width + lo : 2 * width + lo + HEAD_DIM]
        s = mm_nt(q, k) + bias
        top = jnp.max(s, axis=-1, keepdims=True)
        e = jnp.exp(s - top)
        total = jnp.sum(e, axis=-1, keepdims=True)
        ctx = mm_nn(e.astype(BF16), v) / total
        ctx_ref[0, :, lo : lo + HEAD_DIM] = ctx.astype(BF16)
        lse_ref[0, :, h : h + 1] = top + jnp.log(total)


def attend(qkv, bias, heads):
    chunks, seq, _ = qkv.shape
    block = min(256, seq)
    width = heads * HEAD_DIM
    return pl.pallas_call(
        functools.partial(attend_kernel, heads, block),
        grid=(chunks, seq // block),
        in_specs=[
            pl.BlockSpec((1, seq), lambda i, j: (0, 0)),
            pl.BlockSpec((1, block, 3 * width), lambda i, j: (i, j, 0)),
            pl.BlockSpec((1, seq, 3 * width), lambda i, j: (i, 0, 0)),
        ],
        out_specs=[
            pl.BlockSpec((1, block, width), lambda i, j: (i, j, 0)),
            pl.BlockSpec((1, block, 8), lambda i, j: (i, j, 0)),
        ],
        out_shape=[
            jax.ShapeDtypeStruct((chunks, seq, width), BF16),
            jax.ShapeDtypeStruct((chunks, seq, 8), F32),
        ],
        cost_estimate=pl.CostEstimate(
            flops=16 * chunks * heads * seq * seq * HEAD_DIM,
            bytes_accessed=8 * chunks * seq * width,
            transcendentals=chunks * heads * seq * seq,
        ),
        name="attend",
    )(bias, qkv, qkv)


def attend_back_kernel(heads, bias_ref, q_ref, g_ref, o_ref, lse_ref, kv_ref, gq_ref, gkv_ref, acc_ref):
    width = heads * HEAD_DIM
    step = pl.program_id(1)
    scale = HEAD_DIM**-0.5

    @pl.when(step == 0)
    def _():
        acc_ref[...] = jnp.zeros_like(acc_ref)

    bias = bias_ref[...]
    lse_rows = lse_ref[0].T
    for h in range(heads):
        lo = h * HEAD_DIM
        q = q_ref[0, :, lo : lo + HEAD_DIM] * jnp.asarray(scale, BF16)
        g = g_ref[0, :, lo : lo + HEAD_DIM]
        o = o_ref[0, :, lo : lo + HEAD_DIM]
        k = kv_ref[0, :, width + lo : width + lo + HEAD_DIM]
        v = kv_ref[0, :, 2 * width + lo : 2 * width + lo + HEAD_DIM]
        delta = jnp.sum(g.astype(F32) * o.astype(F32), axis=-1, keepdims=True).T
        st = mm_nt(k, q) + bias
        pt = jnp.exp(st - lse_rows[h : h + 1, :])
        gpt = mm_nt(v, g)
        gst = (pt * (gpt - delta)).astype(BF16)
        acc_ref[:, width + lo : width + lo + HEAD_DIM] += mm_nn(pt.astype(BF16), g)
        acc_ref[:, lo : lo + HEAD_DIM] += mm_nn(gst, q)
        gq_ref[0, :, lo : lo + HEAD_DIM] = (mm_tn(gst, k) * scale).astype(BF16)

    @pl.when(step == pl.num_programs(1) - 1)
    def _():
        gkv_ref[0] = acc_ref[...].astype(BF16)


def attend_back(qkv, grad_ctx, ctx, lse, bias_col, heads):
    chunks, seq, _ = qkv.shape
    block = min(256, seq)
    width = heads * HEAD_DIM
    return pl.pallas_call(
        functools.partial(attend_back_kernel, heads),
        grid=(chunks, seq // block),
        in_specs=[
            pl.BlockSpec((seq, 1), lambda i, j: (0, 0)),
            pl.BlockSpec((1, block, 3 * width), lambda i, j: (i, j, 0)),
            pl.BlockSpec((1, block, width), lambda i, j: (i, j, 0)),
            pl.BlockSpec((1, block, width), lambda i, j: (i, j, 0)),
            pl.BlockSpec((1, block, 8), lambda i, j: (i, j, 0)),
            pl.BlockSpec((1, seq, 3 * width), lambda i, j: (i, 0, 0)),
        ],
        out_specs=[
            pl.BlockSpec((1, block, width), lambda i, j: (i, j, 0)),
            pl.BlockSpec((1, seq, 2 * width), lambda i, j: (i, 0, 0)),
        ],
        out_shape=[
            jax.ShapeDtypeStruct((chunks, seq, width), BF16),
            jax.ShapeDtypeStruct((chunks, seq, 2 * width), BF16),
        ],
        scratch_shapes=[pltpu.VMEM((seq, 2 * width), F32)],
        cost_estimate=pl.CostEstimate(
            flops=40 * chunks * heads * seq * seq * HEAD_DIM,
            bytes_accessed=20 * chunks * seq * width,
            transcendentals=chunks * heads * seq * seq,
        ),
        name="attend_back",
    )(bias_col, qkv, grad_ctx, ctx, lse, qkv)


class Routes:
    def __init__(self, dp_size, mp_size):
        self.dp, self.mp = dp_size, mp_size
        self.bits = (dp_size // 2).bit_length() - 1
        self.mp_bits = mp_size.bit_length() - 1

    def _pairs(self, target):
        pairs = []
        for d in range(self.dp):
            for m in range(self.mp):
                dest = target(d // 2, d % 2, m)
                pairs.append((d * self.mp + m, (dest[0] * 2 + dest[1]) * self.mp + dest[2]))
        return pairs

    def send(self, value, target, back=False):
        pairs = self._pairs(target)
        if back:
            pairs = [(b, a) for a, b in pairs]
        return lax.ppermute(value, AXES, pairs)

    def partner(self, value):
        return self.send(value, lambda p, c, m: (p, 1 - c, m))

    def pair_bit(self, value, bit):
        return self.send(value, lambda p, c, m: (p ^ (1 << bit), c, m))

    def mp_bit(self, value, bit):
        return self.send(value, lambda p, c, m: (p, c, m ^ (1 << bit)))

    def cell(self, value, k, back=False):
        return self.send(value, lambda p, c, m: (p, m // 2, 2 * c + ((m % 2) ^ k)), back)

    def shard(self, value, k, back=False):
        return self.send(value, lambda p, c, m: (p, m // 2, m ^ k ^ (2 * c)), back)


def gather_shards(routes, shard):
    got = [routes.shard(shard, k) for k in range(4)]
    chunks = []
    for half in range(2):
        own = jnp.stack([got[half], got[half + 2]])
        order = range(routes.bits) if half else reversed(range(routes.bits))
        pieces = {0: own}
        for bit in order:
            if routes.bits <= 2:
                pieces.update({r | (1 << bit): routes.pair_bit(v, bit) for r, v in list(pieces.items())})
            else:
                keys = sorted(pieces)
                cat = routes.pair_bit(jnp.stack([pieces[r] for r in keys]), bit)
                pieces.update({r | (1 << bit): cat[i] for i, r in enumerate(keys)})
        chunks.append(pieces)
    return chunks


def assemble(pieces, mask):
    count = len(pieces)
    _, rows, width = pieces[0].shape
    full = jnp.zeros((count * 2 * rows, width), pieces[0].dtype)
    for r in range(count):
        for e in range(2):
            full = lax.dynamic_update_slice(full, pieces[r][e], ((((2 * r + e) ^ mask)) * rows, 0))
    return full


def scatter_grads(routes, chunks, mask):
    partial = []
    for half in range(2):
        full = chunks[half]
        count = 1 << routes.bits
        rows = full.shape[0] // (2 * count)
        blocks = full.reshape(2 * count, rows, full.shape[1])
        pieces = {
            r: jnp.stack([lax.dynamic_index_in_dim(blocks, (2 * r + e) ^ mask, 0, keepdims=False) for e in range(2)])
            for r in range(count)
        }
        order = range(routes.bits) if not half else reversed(range(routes.bits))
        for bit in order:
            keys = sorted(r for r in pieces if not r & (1 << bit))
            sent = routes.pair_bit(jnp.stack([pieces[r | (1 << bit)] for r in keys]), bit)
            pieces = {
                r: (pieces[r].astype(F32) + sent[i].astype(F32)).astype(BF16) for i, r in enumerate(keys)
            }
        partial.append(pieces[0])
    total = None
    for k in range(4):
        got = routes.shard(partial[k % 2][k // 2], k, back=True).astype(F32)
        total = got if total is None else total + got
    return total


MESH = pl.DeviceIdType.MESH


class Here:
    def __init__(self):
        self.d, self.m = lax.axis_index("dp"), lax.axis_index("mp")
        self.c = self.d % 2
        self.pair = self.d - self.c
        self.x = (self.d // 2) % 2
        self.y = self.d // 4
        self.t = self.m // 2
        self.b = self.m % 2
        self.over_x = {"dp": self.d + 2 - 4 * self.x, "mp": self.m}
        self.over_y = {"dp": self.d + 4 - 8 * self.y, "mp": self.m}
        self.partner = {"dp": self.d + 1 - 2 * self.c, "mp": self.m}
        self.home = self.t == self.c

    def at(self, core, m):
        return {"dp": self.pair + core, "mp": m}


def remote(src, dst, ssem, rsem, dev):
    return pltpu.make_async_remote_copy(
        src_ref=src, dst_ref=dst, send_sem=ssem, recv_sem=rsem, device_id=dev, device_id_type=MESH
    )


def arrived(dst, rsem, dev):
    remote(dst, dst, rsem, rsem, dev).wait_recv()


class Maybe:
    def __init__(self, src, dst, ssem, rsem, dev, own):
        self.args, self.dev, self.ssem, self.own = (src, dst), dev, ssem, own
        self.rsem = rsem

    def far(self):
        return remote(*self.args, self.ssem, self.rsem, self.dev)

    def start(self):
        pl.when(self.own)(lambda: pltpu.make_async_copy(*self.args, self.rsem).start())
        pl.when(jnp.logical_not(self.own))(lambda: self.far().start())

    def wait_send(self):
        pl.when(jnp.logical_not(self.own))(lambda: self.far().wait_send())


def greet(sources, count):
    barrier = pltpu.get_barrier_semaphore()

    def tell(dev):
        pl.semaphore_signal(barrier, inc=1, device_id=dev, device_id_type=MESH)

    for dev, own in sources:
        if own is None:
            tell(dev)
        else:
            pl.when(jnp.logical_not(own))(functools.partial(tell, dev))
    pl.semaphore_wait(barrier, count)


class Gather:
    def __init__(self, here, shard, full, sems):
        (self.send_z, self.got_z, self.send_x, self.send_y, self.got_x, self.got_y, self.send_r, self.got_r) = sems
        self.here, self.shard, self.full = here, shard, full
        self.rows = shard.shape[0]
        self.first = jnp.where(here.m > 2 * here.c, 1, 0)

    @staticmethod
    def scratch():
        dma = pltpu.SemaphoreType.DMA
        return [dma((4,)), dma((2, 2))] + [dma((2, 2))] * 6

    def plane(self, i):
        return (self.first + i) % 2

    def block(self, i, dp):
        return self.full.at[self.plane(i), pl.ds(dp * self.rows, self.rows), :]

    def z_copy(self, m):
        h = self.here
        dst = self.full.at[h.b, pl.ds(h.d * self.rows, self.rows), :]
        own = jnp.logical_and(h.home, h.m == m)
        return Maybe(self.shard, dst, self.send_z.at[m], self.got_z.at[h.b, h.c], h.at(h.t, m), own)

    def start_z(self):
        for m in range(4):
            self.z_copy(m).start()

    def own_copies(self, i, e):
        h = self.here
        ref = self.block(i, h.pair + e)
        return (
            remote(ref, ref, self.send_x.at[i, e], self.got_x.at[i, e], h.over_x),
            remote(ref, ref, self.send_y.at[i, e], self.got_y.at[i, e], h.over_y),
        )

    def spread(self, i):
        h = self.here
        for e in range(2):
            arrived(self.block(i, h.pair + e), self.got_z.at[self.plane(i), e], h.partner)
            for copy in self.own_copies(i, e):
                copy.start()

    def relay_copy(self, i, e):
        h = self.here
        if i == 0:
            ref, dev = self.block(i, h.over_y["dp"] - h.c + e), h.over_x
        else:
            ref, dev = self.block(i, h.over_x["dp"] - h.c + e), h.over_y
        return remote(ref, ref, self.send_r.at[i, e], self.got_r.at[i, e], dev)

    def relay(self, i):
        h = self.here
        for e in range(2):
            if i == 0:
                arrived(self.block(i, h.over_y["dp"] - h.c + e), self.got_y.at[i, e], h.over_y)
            else:
                arrived(self.block(i, h.over_x["dp"] - h.c + e), self.got_x.at[i, e], h.over_x)
            self.relay_copy(i, e).start()

    def finish(self):
        self.arrive()
        self.sent()

    def arrive(self):
        h = self.here
        diagonal = h.pair + 2 - 4 * h.x + 4 - 8 * h.y
        for i in range(2):
            for e in range(2):
                if i == 0:
                    arrived(self.block(i, h.over_x["dp"] - h.c + e), self.got_x.at[i, e], h.over_x)
                else:
                    arrived(self.block(i, h.over_y["dp"] - h.c + e), self.got_y.at[i, e], h.over_y)
                arrived(self.block(i, diagonal + e), self.got_r.at[i, e], h.over_x)

    def sent(self):
        for m in range(4):
            self.z_copy(m).wait_send()
        for i in range(2):
            for e in range(2):
                for copy in self.own_copies(i, e):
                    copy.wait_send()
                self.relay_copy(i, e).wait_send()


class ToCell:
    def __init__(self, here, source, rows, send, got):
        self.here, self.source, self.rows, self.send, self.got = here, source, rows, send, got

    def copy(self, s):
        h = self.here
        target = 2 * h.c + s
        own = jnp.logical_and(h.home, h.m == target)
        return Maybe(self.source.at[s], self.rows.at[h.b], self.send.at[s], self.got.at[h.b], h.at(h.t, target), own)

    def start(self):
        for s in range(2):
            self.copy(s).start()

    def wait(self):
        for b in range(2):
            arrived(self.rows.at[b], self.got.at[b], self.here.partner)

    def finish(self):
        for s in range(2):
            self.copy(s).wait_send()


def spread_ends(here):
    h = here
    takers = [(h.at(h.t, m), jnp.logical_and(h.home, h.m == m)) for m in range(4)]
    givers = [(h.at(e, 2 * h.c + b), jnp.logical_and(h.home, jnp.logical_and(h.b == b, h.c == e))) for e in range(2) for b in range(2)]
    return takers, givers


def greet_cross(here, sources, *others):
    others = [here.over_x, here.over_y, *others]
    greet(sources + [(dev, None) for dev in others], 4 + len(others) - here.home.astype(jnp.int32))


def norm_rows(values, gain, shift):
    mean_row = jnp.mean(values, axis=-1, keepdims=True)
    centred = values - mean_row
    inv_std = lax.rsqrt(jnp.mean(centred * centred, axis=-1, keepdims=True) + eps_norm)
    return centred * inv_std * gain + shift


ANY = pl.BlockSpec(memory_space=pl.ANY)
VMEM = pl.BlockSpec(memory_space=pltpu.VMEM)


def rows_at(start, size):
    return pl.ds(start * size, size)


def exact_gelu_both(u):
    below = 0.5 * (1.0 + lax.erf(u * (0.5**0.5)))
    density = jnp.exp(-0.5 * u * u) * ((2.0 * jnp.pi) ** -0.5)
    return u * below, below + u * density


class Stores:
    def __init__(self, sems):
        self.sems, self.made = sems, []

    def put(self, src, dst):
        copy = pltpu.make_async_copy(src, dst, self.sems.at[len(self.made)])
        copy.start()
        self.made.append((src, dst))

    def finish(self):
        for i, (src, dst) in enumerate(self.made):
            pltpu.make_async_copy(src, dst, self.sems.at[i]).wait()


def attend_rows(bias, qkv_ref, ctx_ref, lse_ref, chunk, start, block, heads):
    width = heads * HEAD_DIM
    spare = qkv_ref.shape[2] - 3 * width
    rows = pl.ds(start, block)
    stats = []
    for h in range(heads):
        lo = spare + h * HEAD_DIM
        q = qkv_ref[chunk, rows, lo : lo + HEAD_DIM] * jnp.asarray(HEAD_DIM**-0.5, BF16)
        k = qkv_ref[chunk, :, width + lo : width + lo + HEAD_DIM]
        v = qkv_ref[chunk, :, 2 * width + lo : 2 * width + lo + HEAD_DIM]
        s = mm_nt(q, k) + bias
        top = jnp.max(s, axis=-1, keepdims=True)
        e = jnp.exp(s - top)
        total = jnp.sum(e, axis=-1, keepdims=True)
        ctx = mm_nn(e.astype(BF16), v) / total
        ctx_ref[chunk, rows, h * HEAD_DIM : (h + 1) * HEAD_DIM] = ctx.astype(BF16)
        stats.append(top + jnp.log(total))
    stats += [jnp.zeros_like(stats[0])] * (8 - heads)
    lse_ref[chunk, :, rows] = jnp.concatenate(stats, axis=1).T


def forward_kernel(heads, *refs):
    (x_ref, gy_ref, shard_a, shard_1, shard_2, norm_ref, bias_ref) = refs[:7]
    (full_a, full_1, full_2, h1_out, qkv_out, ctx_out, lse_out, x_out, x2_out, h2_out, act_out, slope_out, gy_out,
     grad_out) = refs[7:21]
    (weight, x_in, gy_in, h1, qkv, ctx, lse, fold_out, fold_in, x2, h2, act, slope, gy, stage) = refs[21:36]
    sems = refs[36:]
    (cell_sems, swap_send, swap_got, load_sem, store_sems, stage_sems) = (
        sems[:4], sems[4], sems[5], sems[6], sems[7], sems[8]
    )
    here = Here()
    half, width = x2.shape
    seq = 2 * half
    quarter = half // 2
    inner = heads * HEAD_DIM
    greet_cross(here, spread_ends(here)[1], here.partner)
    per = len(Gather.scratch())
    block_a, block_1, block_2 = (
        Gather(here, shard, full, sems[9 + per * i : 9 + per * (i + 1)])
        for i, (shard, full) in enumerate(((shard_a, full_a), (shard_1, full_1), (shard_2, full_2)))
    )
    cell_x = ToCell(here, x_ref, x_in, cell_sems[0], cell_sems[1])
    cell_g = ToCell(here, gy_ref, gy_in, cell_sems[2], cell_sems[3])
    stores = Stores(store_sems)

    def swap(n, src, dst):
        return remote(src, dst, swap_send.at[n], swap_got.at[n], here.partner)

    def load(full):
        copies = [pltpu.make_async_copy(full.at[b], weight.at[b], load_sem.at[b]) for b in range(2)]
        for copy in copies:
            copy.start()
        for copy in copies:
            copy.wait()

    own, other = pl.ds(0, half), pl.ds(half, half)
    block_a.start_z()
    block_a.spread(0)
    cell_x.start()
    block_a.spread(1)
    block_a.relay(0)
    block_a.relay(1)
    cell_x.wait()
    block_1.start_z()

    step = 128
    per_quarter = quarter // step

    @pl.loop(0, half // step)
    def _(i):
        rows = pl.ds(pl.multiple_of((i % per_quarter) * step, step), step)
        h1[pl.ds(pl.multiple_of(i * step, step), step), :] = norm_rows(
            x_in[i // per_quarter, rows, :].astype(F32), norm_ref[0:1, :], norm_ref[1:2, :]
        ).astype(BF16)

    swap_h1 = swap(0, h1.at[own], h1.at[other])
    swap_h1.start()
    stores.put(x_in, x_out)
    block_a.arrive()
    load(full_a)
    swap_h1.wait_recv()
    stores.put(h1, h1_out)

    first = 4 * inner - qkv.shape[2]

    @pl.loop(0, 2)
    def _(b):
        for n in range(0, qkv.shape[2], 512):
            qkv[b, :, n : n + 512] = mm_nn(h1[...], weight[b, :, first + n : first + n + 512]).astype(BF16)

    stores.put(qkv, qkv_out)
    bias = bias_ref[...]
    q_block = 256
    per_chunk = seq // q_block

    @pl.loop(0, 2 * per_chunk)
    def _(i):
        pl.when(i == 2)(lambda: block_1.spread(0))
        pl.when(i == 6)(lambda: block_1.spread(1))
        pl.when(i == 6)(lambda: block_2.start_z())
        pl.when(i == 7)(lambda: block_1.relay(0))
        attend_rows(
            bias, qkv, ctx, lse, i // per_chunk, pl.multiple_of((i % per_chunk) * q_block, q_block), q_block, heads
        )

    stores.put(ctx, ctx_out)
    stores.put(lse, lse_out)

    def branch_tile(rows, n):
        cols = pl.ds(pl.multiple_of(n * 256, 256), 256)
        return mm_nt(ctx[0, rows, :], weight[0, cols, 0:inner]) + mm_nt(ctx[1, rows, :], weight[1, cols, 0:inner]), cols

    @pl.loop(0, width // 256)
    def _(n):
        part, cols = branch_tile(other, n)
        fold_out[:, cols] = part.astype(BF16)

    swap_fold = swap(1, fold_out, fold_in)
    swap_fold.start()

    @pl.loop(0, width // 256)
    def _(n):
        part, cols = branch_tile(own, n)
        for b in range(2):
            rows = pl.ds(b * quarter, quarter)
            x2[rows, cols] = x_in[b, :, cols].astype(F32) + part[b * quarter : (b + 1) * quarter]

    block_1.relay(1)
    swap_fold.wait_recv()

    @pl.loop(0, half // step)
    def _(i):
        rows = pl.ds(pl.multiple_of(i * step, step), step)
        middle = x2[rows, :] + fold_in[rows, :].astype(F32)
        x2[rows, :] = middle
        h2[rows, :] = norm_rows(middle, norm_ref[2:3, :], norm_ref[3:4, :]).astype(BF16)

    swap_h2 = swap(2, h2.at[own], h2.at[other])
    swap_h2.start()
    stores.put(x2, x2_out)
    block_1.arrive()
    load(full_1)
    block_2.spread(0)
    swap_h2.wait_recv()
    stores.put(h2, h2_out)
    per_unit = width // 256

    @pl.loop(0, 2 * per_unit)
    def _(i):
        pl.when(i == 3)(lambda: block_2.spread(1))
        pl.when(i == 3)(lambda: cell_g.start())
        pl.when(i == 6)(lambda: block_2.relay(0))
        b, cols = i // per_unit, pl.ds(pl.multiple_of((i % per_unit) * 256, 256), 256)
        value, grad = exact_gelu_both(mm_nn(h2[...], weight[b, :, cols]))
        act[b, :, cols] = value.astype(BF16)
        slope[b, :, cols] = grad.astype(BF16)

    stores.put(act, act_out)
    stores.put(slope, slope_out)
    block_2.relay(1)
    cell_g.wait()

    @pl.loop(0, 2)
    def _(b):
        gy[pl.ds(pl.multiple_of(b * quarter, quarter), quarter), :] = gy_in[b]

    swap_gy = swap(3, gy.at[own], gy.at[other])
    swap_gy.start()
    swap_gy.wait_recv()
    stores.put(gy, gy_out)

    def stage_copy(i):
        slot = i % 2
        return pltpu.make_async_copy(
            stage.at[slot], grad_out.at[:, pl.ds(pl.multiple_of(i * 256, 256), 256), :], stage_sems.at[slot]
        )

    @pl.loop(0, width // 256)
    def _(i):
        pl.when(i >= 2)(lambda: stage_copy(i - 2).wait())
        left = gy[:, pl.ds(pl.multiple_of(i * 256, 256), 256)].T
        for b in range(2):
            stage[i % 2, b] = mm_nn(left, act[b]).astype(BF16)
        stage_copy(i).start()

    for i in range(width // 256 - 2, width // 256):
        stage_copy(i).wait()
    block_2.arrive()
    for block in (block_a, block_1, block_2):
        block.sent()
    cell_x.finish()
    cell_g.finish()
    for n, (src, dst) in enumerate(((h1.at[own], h1.at[other]), (fold_out, fold_in), (h2.at[own], h2.at[other]), (gy.at[own], gy.at[other]))):
        swap(n, src, dst).wait_send()
    stores.finish()


def forward(inputs, cotangent, shards, norms, bias, heads, collective):
    cells, quarter, width = inputs.shape
    rows, wide = shards[0].shape
    half, seq, inner = 2 * quarter, 4 * quarter, heads * HEAD_DIM
    part = (3 * inner + 255) // 256 * 256
    dma = pltpu.SemaphoreType.DMA
    full = ((2, 8 * rows, wide), BF16)
    kept = [
        ((seq, width), BF16), ((2, seq, part), BF16), ((2, seq, inner), BF16), ((2, 8, seq), F32),
        ((2, quarter, width), BF16), ((half, width), F32), ((seq, width), BF16), ((2, seq, wide), BF16),
        ((2, seq, wide), BF16), ((seq, width), BF16), ((2, width, wide), BF16),
    ]
    buffers = [
        full, ((2, quarter, width), BF16), ((2, quarter, width), BF16), kept[0], kept[1], kept[2], kept[3],
        ((half, width), BF16), ((half, width), BF16), kept[5], kept[6], kept[7], kept[8], kept[9],
        ((2, 2, 256, wide), BF16),
    ]
    return pl.pallas_call(
        functools.partial(forward_kernel, heads),
        out_shape=[jax.ShapeDtypeStruct(*s) for s in [full] * 3 + kept],
        in_specs=[VMEM] * 7,
        out_specs=[ANY] * 14,
        scratch_shapes=[pltpu.VMEM(*s) for s in buffers]
        + [dma((2,))] * 4 + [dma((4,)), dma((4,)), dma((2,)), dma((10,)), dma((2,))]
        + Gather.scratch() * 3,
        compiler_params=pltpu.CompilerParams(
            collective_id=collective, has_side_effects=True, vmem_limit_bytes=67043328
        ),
        name="forward",
    )(inputs, cotangent, *shards, norms, bias)


class Reduce:
    def __init__(self, here, grads, bufs, sems):
        self.here, self.grads = here, grads
        self.own, self.one, self.two, self.part, self.last = bufs
        self.sem_own, self.send_one, self.got_one, self.send_two, self.got_two, self.send_z, self.got_z = sems
        self.piece = self.own.shape[3]

    @staticmethod
    def scratch(rows, width):
        r = rows // 2
        dma = pltpu.SemaphoreType.DMA
        return [
            pltpu.VMEM((2, 2, 4, r, width), BF16),
            pltpu.VMEM((2, 2, 4, r, width), BF16),
            pltpu.VMEM((2, 4, r, width), BF16),
            pltpu.VMEM((2, 4, r, width), BF16),
            pltpu.VMEM((4, 2, r, width), BF16),
        ], [dma((2, 2, 4)), dma((2, 2, 4)), dma((2, 2, 4)), dma((2, 4)), dma((2, 4)), dma((2, 4)), dma((4, 2))]

    def rows_of(self, role, dp, j):
        return self.grads.at[role, pl.ds(dp * 2 * self.piece + j * self.piece, self.piece), :]

    def pair_at(self, role, n, far):
        h = self.here
        dx, dy = 2 - 4 * h.x, 4 - 8 * h.y
        first, second = (dx, dy) if role == 0 else (dy, dx)
        return h.pair + (first if far else 0) + (second if n == 0 else 0)

    def load(self, role, n, j):
        return pltpu.make_async_copy(
            self.rows_of(role, self.pair_at(role, n, False), j), self.own.at[role, n, j], self.sem_own.at[role, n, j]
        )

    def copy_one(self, role, n, j):
        dev = self.here.over_x if role == 0 else self.here.over_y
        return remote(
            self.rows_of(role, self.pair_at(role, n, True), j), self.one.at[role, n, j],
            self.send_one.at[role, n, j], self.got_one.at[role, n, j], dev,
        )

    def copy_two(self, role, j):
        dev = self.here.over_y if role == 0 else self.here.over_x
        return remote(
            self.own.at[role, 0, j], self.two.at[role, j], self.send_two.at[role, j], self.got_two.at[role, j], dev
        )

    def copy_z(self, role, j):
        h = self.here
        core, target = j // 2, 2 * h.c + role
        own = jnp.logical_and(h.c == core, h.m == target)
        return Maybe(
            self.part.at[role, j], self.last.at[h.m, j % 2], self.send_z.at[role, j], self.got_z.at[h.m, j % 2],
            h.at(core, target), own,
        )

    def start(self):
        for j in range(4):
            for n in range(2):
                for role in range(2):
                    self.copy_one(role, n, j).start()
                    self.load(role, n, j).start()

    def add_one(self, role, j):
        h = self.here
        for n in range(2):
            self.load(role, n, j).wait()
            arrived(self.one.at[role, n, j], self.got_one.at[role, n, j], h.over_x)
            total = self.own[role, n, j].astype(F32) + self.one[role, n, j].astype(F32)
            self.own[role, n, j] = total.astype(BF16)
            if n == 0:
                self.copy_two(role, j).start()

    def add_two(self, role, j):
        arrived(self.two.at[role, j], self.got_two.at[role, j], self.here.over_x)
        total = self.own[role, 1, j].astype(F32) + self.two[role, j].astype(F32)
        self.part[role, j] = total.astype(BF16)
        self.copy_z(role, j).start()

    def finish(self, out_ref):
        h = self.here
        for s in range(2):
            for m in range(4):
                arrived(self.last.at[m, s], self.got_z.at[m, s], h.partner)
            total = self.last[0, s].astype(F32)
            for m in range(1, 4):
                total = total + self.last[m, s].astype(F32)
            out_ref[pl.ds(s * self.piece, self.piece), :] = total
        for role in range(2):
            for j in range(4):
                for n in range(2):
                    self.copy_one(role, n, j).wait_send()
                self.copy_two(role, j).wait_send()
                self.copy_z(role, j).wait_send()


def reduce_kernel(grads_ref, out_ref, *scratch):
    here = Here()
    greet_cross(here, spread_ends(here)[0])
    block = Reduce(here, grads_ref, scratch[:5], scratch[5:])
    block.start()
    for j in range(4):
        for role in range(2):
            block.add_one(role, j)
        if j >= 1:
            for role in range(2):
                block.add_two(role, j - 1)
    for role in range(2):
        block.add_two(role, 3)
    block.finish(out_ref)


def reduce_block(grads, collective):
    _, full, width = grads.shape
    rows = full // 8
    bufs, sems = Reduce.scratch(rows, width)
    return pl.pallas_call(
        reduce_kernel,
        out_shape=jax.ShapeDtypeStruct((rows, width), F32),
        in_specs=[ANY],
        out_specs=VMEM,
        scratch_shapes=bufs + sems,
        compiler_params=pltpu.CompilerParams(collective_id=collective, has_side_effects=True),
        name="reduce_block",
    )(grads)


def gather_norms(routes, norm_params, d, m):
    cur = norm_params
    for bit in range(routes.mp_bits):
        got = routes.mp_bit(cur, bit)
        high = ((m >> bit) & 1) == 1
        cur = jnp.where(high, jnp.concatenate([got, cur], 1), jnp.concatenate([cur, got], 1))
    for bit in range(routes.bits + 1):
        got = routes.partner(cur) if bit == 0 else routes.pair_bit(cur, bit - 1)
        high = ((d >> bit) & 1) == 1
        cur = jnp.where(high, jnp.concatenate([got, cur], 1), jnp.concatenate([cur, got], 1))
    return cur


def scatter_norms(routes, grads, d, m):
    cur = grads
    for bit in reversed(range(routes.bits + 1)):
        low, up = jnp.split(cur, 2, axis=1)
        high = ((d >> bit) & 1) == 1
        give = jnp.where(high, low, up)
        got = routes.partner(give) if bit == 0 else routes.pair_bit(give, bit - 1)
        cur = jnp.where(high, up, low) + got
    for bit in reversed(range(routes.mp_bits)):
        low, up = jnp.split(cur, 2, axis=1)
        high = ((m >> bit) & 1) == 1
        cur = jnp.where(high, up, low) + routes.mp_bit(jnp.where(high, low, up), bit)
    return cur


def update(
    outputs, input_grad, norm_sum, attend_sum, expand_sum, reduce_sum, step_count, norm_params, norm_first, norm_second,
    attend_weight, attend_first, attend_second, output_weight, output_first, output_second,
    expand_weight, expand_first, expand_second, reduce_weight, reduce_first, reduce_second,
):
    width = attend_weight.shape[2]
    step_number = step_count[0].astype(F32)
    norm_new = adam_step(norm_params, norm_first, norm_second, norm_sum, norm_rate, 0.0, step_number)
    attend_reduced = jnp.stack([attend_sum[:, i * width : (i + 1) * width] for i in range(1, 4)])
    attend_new = adam_step(
        attend_weight, attend_first, attend_second, attend_reduced, 2.0 * D ** (-0.5), decay_rate, step_number
    )
    output_new = adam_step(
        output_weight, output_first, output_second, attend_sum[:, :width].T,
        2.0 * (2 * D // SEQ) ** (-0.5), decay_rate, step_number,
    )
    expand_new = adam_step(
        expand_weight, expand_first, expand_second, expand_sum, 2.0 * D ** (-0.5), decay_rate, step_number
    )
    reduce_new = adam_step(
        reduce_weight, reduce_first, reduce_second, reduce_sum.T, 2.0 * FF ** (-0.5), decay_rate, step_number
    )
    return (
        outputs, input_grad,
        norm_new[0], norm_new[1], norm_new[2][0:2], norm_new[2][2:4],
        *attend_new, *output_new, *expand_new, *reduce_new,
    )


def per_device_plain(
    inputs, cotangent, gene_counts, step_count, norm_params, norm_first, norm_second,
    attend_weight, attend_first, attend_second, output_weight, output_first, output_second,
    expand_weight, expand_first, expand_second, reduce_weight, reduce_first, reduce_second,
):
    routes = Routes(lax.axis_size("dp"), lax.axis_size("mp"))
    d, m = lax.axis_index("dp"), lax.axis_index("mp")
    c = d % 2
    cells, quarter, _ = inputs.shape
    assert routes.mp == 4 and 2 * cells == routes.mp and routes.dp % 2 == 0
    half = 2 * quarter
    seq = 2 * half
    heads = attend_weight.shape[2] // HEAD_DIM
    width = heads * HEAD_DIM
    m_low, m_high = m % 2, m // 2
    mask = 2 * (d // 2) + ((c + m_high) % 2)

    norm_full = gather_norms(routes, norm_params, d, m)

    def to_cell(values):
        got = [
            routes.cell(lax.dynamic_index_in_dim(values, (m_low + k) % 2, 0, keepdims=False), k) for k in range(2)
        ]
        return jnp.concatenate(got, 0)

    def from_cell(rows):
        rows = rows.astype(BF16)
        got = [routes.cell(rows[k * quarter : (k + 1) * quarter], k, back=True) for k in range(2)]
        flip = m_low == 1
        return jnp.stack([jnp.where(flip, got[1], got[0]), jnp.where(flip, got[0], got[1])]).astype(F32)

    attend_shard = jnp.concatenate(
        [output_weight.T, attend_weight[0], attend_weight[1], attend_weight[2]], axis=1
    ).astype(BF16)
    expand_shard = expand_weight.astype(BF16)
    reduce_shard = reduce_weight.T.astype(BF16)

    x_mine = to_cell(inputs).astype(F32)
    attend_w = [assemble(pieces, mask) for pieces in gather_shards(routes, attend_shard)]
    expand_w = [assemble(pieces, mask) for pieces in gather_shards(routes, expand_shard)]
    reduce_w = [assemble(pieces, mask) for pieces in gather_shards(routes, reduce_shard)]
    gy_mine = to_cell(cotangent)

    other_counts = routes.partner(gene_counts)
    mine = jnp.where(m_high == c, gene_counts, other_counts)
    count = jnp.where(m_low == 1, mine[1], mine[0])
    inside = jnp.arange(quarter)
    first = m_low
    positions = jnp.concatenate(
        [h * half + b * quarter + inside for h, b in ((c, first), (c, 1 - first), (1 - c, first), (1 - c, 1 - first))]
    )
    bias = jnp.where(positions < 1 + count, 0.0, masked_score).astype(F32)

    def both(rows):
        return jnp.concatenate([rows, routes.partner(rows)], 0)

    def fold(partial):
        return partial[:half] + routes.partner(partial[half:].astype(BF16)).astype(F32)

    normed, scaled_one, inv_one = normalize(x_mine, norm_full[0], norm_full[1])
    h1 = both(normed.astype(BF16))
    qkv = jnp.stack([mm_nn(h1, w[:, width:]).astype(BF16) for w in attend_w])
    ctx, lse = attend(qkv, bias[None, :], heads)
    branch = mm_nt(ctx[0], attend_w[0][:, :width]) + mm_nt(ctx[1], attend_w[1][:, :width])
    x2 = x_mine + fold(branch)
    normed, scaled_two, inv_two = normalize(x2, norm_full[2], norm_full[3])
    h2 = both(normed.astype(BF16))
    hidden = [mm_nn(h2, w) for w in expand_w]
    active = [exact_gelu(u).astype(BF16) for u in hidden]
    branch = mm_nt(active[0], reduce_w[0]) + mm_nt(active[1], reduce_w[1])
    outputs = from_cell(x2 + fold(branch))

    gy = both(gy_mine)
    reduce_grad = [mm_tn(gy, a).astype(BF16) for a in active]
    grad_hidden = [
        jax.vjp(exact_gelu, u)[1](mm_nn(gy, w))[0].astype(BF16) for u, w in zip(hidden, reduce_w)
    ]
    expand_grad = [mm_tn(h2, g).astype(BF16) for g in grad_hidden]
    gh2 = fold(mm_nt(grad_hidden[0], expand_w[0]) + mm_nt(grad_hidden[1], expand_w[1]))
    grad_in, gain_two, shift_two = normalize_back(gh2, scaled_two, inv_two, norm_full[2])
    gx2 = gy_mine.astype(F32) + grad_in
    gb = both(gx2.astype(BF16))
    grad_ctx = jnp.stack([mm_nn(gb, w[:, :width]).astype(BF16) for w in attend_w])
    gq, gkv = attend_back(qkv, grad_ctx, ctx, lse, bias[:, None], heads)
    attend_grad = [
        jnp.concatenate(
            [mm_tn(gb, ctx[i]), mm_tn(h1, gq[i]), mm_tn(h1, gkv[i])], axis=1
        ).astype(BF16)
        for i in range(2)
    ]
    gh1 = fold(
        sum(
            mm_nt(gq[i], attend_w[i][:, width : 2 * width]) + mm_nt(gkv[i], attend_w[i][:, 2 * width :])
            for i in range(2)
        )
    )
    grad_in, gain_one, shift_one = normalize_back(gh1, scaled_one, inv_one, norm_full[0])
    input_grad = from_cell(gx2 + grad_in)

    reduce_sum = scatter_grads(routes, reduce_grad, mask)
    expand_sum = scatter_grads(routes, expand_grad, mask)
    attend_sum = scatter_grads(routes, attend_grad, mask)
    norm_sum = scatter_norms(routes, jnp.stack([gain_one, shift_one, gain_two, shift_two]), d, m)

    return update(
        outputs, input_grad, norm_sum, attend_sum, expand_sum, reduce_sum, step_count, norm_params, norm_first,
        norm_second, attend_weight, attend_first, attend_second, output_weight, output_first, output_second,
        expand_weight, expand_first, expand_second, reduce_weight, reduce_first, reduce_second,
    )


def per_device(
    inputs, cotangent, gene_counts, step_count, norm_params, norm_first, norm_second,
    attend_weight, attend_first, attend_second, output_weight, output_first, output_second,
    expand_weight, expand_first, expand_second, reduce_weight, reduce_first, reduce_second,
):
    routes = Routes(lax.axis_size("dp"), lax.axis_size("mp"))
    d, m = lax.axis_index("dp"), lax.axis_index("mp")
    c = d % 2
    cells, quarter, _ = inputs.shape
    assert routes.mp == 4 and 2 * cells == routes.mp and routes.dp == 8
    half = 2 * quarter
    seq = 2 * half
    heads = attend_weight.shape[2] // HEAD_DIM
    width = heads * HEAD_DIM
    m_low, m_high = m % 2, m // 2

    norm_full = gather_norms(routes, norm_params, d, m)
    shards = (
        jnp.concatenate([output_weight.T, attend_weight[0], attend_weight[1], attend_weight[2]], axis=1).astype(BF16),
        expand_weight.astype(BF16),
        reduce_weight.T.astype(BF16),
    )
    other_counts = routes.partner(gene_counts)
    mine = jnp.where(m_high == c, gene_counts, other_counts)
    count = jnp.where(m_low == 1, mine[1], mine[0])
    inside = jnp.arange(half)
    positions = jnp.concatenate([c * half + inside, (1 - c) * half + inside])
    bias = jnp.where(positions < 1 + count, 0.0, masked_score).astype(F32)

    (attend_w, expand_w, reduce_w, h1, qkv, ctx, lse, x_mine, x2, h2, act, slope, gy, reduce_grad) = forward(
        inputs, cotangent, shards, norm_full, bias[None, :], heads, 1
    )

    def both(rows):
        return jnp.concatenate([rows, routes.partner(rows)], 0)

    def fold(partial):
        return partial[:half] + routes.partner(partial[half:].astype(BF16)).astype(F32)

    def from_cell(rows):
        rows = rows.astype(BF16)
        flip_rows = jnp.concatenate([rows[quarter:], rows[:quarter]], 0)
        rows = jnp.where(m_low == 1, flip_rows, rows)
        got = [routes.cell(rows[k * quarter : (k + 1) * quarter], k, back=True) for k in range(2)]
        flip = m_low == 1
        return jnp.stack([jnp.where(flip, got[1], got[0]), jnp.where(flip, got[0], got[1])]).astype(F32)

    _, scaled_one, inv_one = normalize(x_mine.reshape(half, -1).astype(F32), norm_full[0], norm_full[1])
    _, scaled_two, inv_two = normalize(x2, norm_full[2], norm_full[3])
    outputs = from_cell(x2 + fold(mm_nt(act[0], reduce_w[0]) + mm_nt(act[1], reduce_w[1])))
    reduce_sum = reduce_block(reduce_grad, 3)
    grad_hidden = [(mm_nn(gy, reduce_w[i]) * slope[i].astype(F32)).astype(BF16) for i in range(2)]
    expand_grad = [mm_tn(h2, g).astype(BF16) for g in grad_hidden]
    gh2 = fold(mm_nt(grad_hidden[0], expand_w[0]) + mm_nt(grad_hidden[1], expand_w[1]))
    grad_in, gain_two, shift_two = normalize_back(gh2, scaled_two, inv_two, norm_full[2])
    gx2 = gy[:half].astype(F32) + grad_in
    gb = both(gx2.astype(BF16))
    grad_ctx = jnp.stack([mm_nn(gb, attend_w[i][:, :width]).astype(BF16) for i in range(2)])
    gq, gkv = attend_back(qkv[:, :, -3 * width :], grad_ctx, ctx, lse.transpose(0, 2, 1), bias[:, None], heads)
    attend_grad = [
        jnp.concatenate([mm_tn(gb, ctx[i]), mm_tn(h1, gq[i]), mm_tn(h1, gkv[i])], axis=1).astype(BF16) for i in range(2)
    ]
    gh1 = fold(
        sum(
            mm_nt(gq[i], attend_w[i][:, width : 2 * width]) + mm_nt(gkv[i], attend_w[i][:, 2 * width :])
            for i in range(2)
        )
    )
    grad_in, gain_one, shift_one = normalize_back(gh1, scaled_one, inv_one, norm_full[0])
    input_grad = from_cell(gx2 + grad_in)
    expand_sum = reduce_block(jnp.stack(expand_grad), 3)
    attend_sum = reduce_block(jnp.stack(attend_grad), 3)
    norm_sum = scatter_norms(routes, jnp.stack([gain_one, shift_one, gain_two, shift_two]), d, m)
    return update(
        outputs, input_grad, norm_sum, attend_sum, expand_sum, reduce_sum, step_count, norm_params, norm_first,
        norm_second, attend_weight, attend_first, attend_second, output_weight, output_first, output_second,
        expand_weight, expand_first, expand_second, reduce_weight, reduce_first, reduce_second,
    )


def solution(mesh):
    norms = P(None, ("dp", "mp"))
    attend_spec, col, row = P(None, "dp", "mp"), P("mp", "dp"), P("dp", "mp")
    tokens = P("dp", "mp", None)
    return jax.shard_map(
        per_device if mesh.shape["dp"] == 8 else per_device_plain,
        mesh=mesh,
        in_specs=(tokens, tokens, P("dp"), P(), norms, norms, norms)
        + (attend_spec,) * 3 + (col,) * 3 + (row,) * 3 + (col,) * 3,
        out_specs=(tokens, tokens, norms, norms, norms, norms)
        + (attend_spec,) * 3 + (col,) * 3 + (row,) * 3 + (col,) * 3,
        check_vma=False,
    )
```

```python
import functools

import jax
import jax.numpy as jnp
from jax import lax
from jax.experimental import pallas as pl
from jax.experimental.pallas import tpu as pltpu
from jax.sharding import PartitionSpec as P

D = 1280
HEAD_DIM = 64
FF = 5120
SEQ = 1024

eps_norm = 1e-05
masked_score = -1e30
beta_one = 0.9
beta_two = 0.95
eps_adam = 1e-08
decay_rate = 0.1
norm_rate = 0.6

F32 = jnp.float32
BF16 = jnp.bfloat16
AXES = ("dp", "mp")


def exact_gelu(values):
    return jax.nn.gelu(values, approximate=False)


def mm(left, right, dims):
    return lax.dot_general(left, right, (dims, ((), ())), preferred_element_type=F32)


def mm_nn(left, right):
    return mm(left, right, ((1,), (0,)))


def mm_nt(left, right):
    return mm(left, right, ((1,), (1,)))


def mm_tn(left, right):
    return mm(left, right, ((0,), (0,)))


def normalize(token_rows, norm_gain, norm_shift):
    mean_row = jnp.mean(token_rows, axis=-1, keepdims=True)
    centred = token_rows - mean_row
    inv_std = lax.rsqrt(jnp.mean(centred * centred, axis=-1, keepdims=True) + eps_norm)
    scaled = centred * inv_std
    return (scaled * norm_gain + norm_shift, scaled, inv_std)


def normalize_back(grad_out, scaled, inv_std, norm_gain):
    grad_scaled = grad_out * norm_gain
    centre_part = jnp.mean(grad_scaled, axis=-1, keepdims=True)
    along_part = scaled * jnp.mean(grad_scaled * scaled, axis=-1, keepdims=True)
    grad_in = inv_std * (grad_scaled - centre_part - along_part)
    return (grad_in, jnp.sum(grad_out * scaled, axis=0), jnp.sum(grad_out, axis=0))


def adam_step(weight, first_moment, second_moment, gradient, rate, decay, step_number):
    first_new = beta_one * first_moment + (1.0 - beta_one) * gradient
    second_new = beta_two * second_moment + (1.0 - beta_two) * gradient * gradient
    corr_one = 1.0 - jnp.power(beta_one, step_number)
    corr_two = 1.0 - jnp.power(beta_two, step_number)
    update = first_new / corr_one / (jnp.sqrt(second_new / corr_two) + eps_adam)
    return (weight - rate * (update + decay * weight), first_new, second_new)


def attend_kernel(heads, block, bias_ref, q_ref, kv_ref, ctx_ref, lse_ref):
    width = heads * HEAD_DIM
    bias = bias_ref[...]
    for h in range(heads):
        lo = h * HEAD_DIM
        q = q_ref[0, :, lo : lo + HEAD_DIM] * jnp.asarray(HEAD_DIM**-0.5, BF16)
        k = kv_ref[0, :, width + lo : width + lo + HEAD_DIM]
        v = kv_ref[0, :, 2 * width + lo : 2 * width + lo + HEAD_DIM]
        s = mm_nt(q, k) + bias
        top = jnp.max(s, axis=-1, keepdims=True)
        e = jnp.exp(s - top)
        total = jnp.sum(e, axis=-1, keepdims=True)
        ctx = mm_nn(e.astype(BF16), v) / total
        ctx_ref[0, :, lo : lo + HEAD_DIM] = ctx.astype(BF16)
        lse_ref[0, :, h : h + 1] = top + jnp.log(total)


def attend(qkv, bias, heads):
    chunks, seq, _ = qkv.shape
    block = min(256, seq)
    width = heads * HEAD_DIM
    return pl.pallas_call(
        functools.partial(attend_kernel, heads, block),
        grid=(chunks, seq // block),
        in_specs=[
            pl.BlockSpec((1, seq), lambda i, j: (0, 0)),
            pl.BlockSpec((1, block, 3 * width), lambda i, j: (i, j, 0)),
            pl.BlockSpec((1, seq, 3 * width), lambda i, j: (i, 0, 0)),
        ],
        out_specs=[
            pl.BlockSpec((1, block, width), lambda i, j: (i, j, 0)),
            pl.BlockSpec((1, block, 8), lambda i, j: (i, j, 0)),
        ],
        out_shape=[
            jax.ShapeDtypeStruct((chunks, seq, width), BF16),
            jax.ShapeDtypeStruct((chunks, seq, 8), F32),
        ],
        cost_estimate=pl.CostEstimate(
            flops=16 * chunks * heads * seq * seq * HEAD_DIM,
            bytes_accessed=8 * chunks * seq * width,
            transcendentals=chunks * heads * seq * seq,
        ),
        name="attend",
    )(bias, qkv, qkv)


def attend_back_kernel(heads, bias_ref, q_ref, g_ref, o_ref, lse_ref, kv_ref, gq_ref, gkv_ref, acc_ref):
    width = heads * HEAD_DIM
    step = pl.program_id(1)
    scale = HEAD_DIM**-0.5

    @pl.when(step == 0)
    def _():
        acc_ref[...] = jnp.zeros_like(acc_ref)

    bias = bias_ref[...]
    lse_rows = lse_ref[0].T
    for h in range(heads):
        lo = h * HEAD_DIM
        q = q_ref[0, :, lo : lo + HEAD_DIM] * jnp.asarray(scale, BF16)
        g = g_ref[0, :, lo : lo + HEAD_DIM]
        o = o_ref[0, :, lo : lo + HEAD_DIM]
        k = kv_ref[0, :, width + lo : width + lo + HEAD_DIM]
        v = kv_ref[0, :, 2 * width + lo : 2 * width + lo + HEAD_DIM]
        delta = jnp.sum(g.astype(F32) * o.astype(F32), axis=-1, keepdims=True).T
        st = mm_nt(k, q) + bias
        pt = jnp.exp(st - lse_rows[h : h + 1, :])
        gpt = mm_nt(v, g)
        gst = (pt * (gpt - delta)).astype(BF16)
        acc_ref[:, width + lo : width + lo + HEAD_DIM] += mm_nn(pt.astype(BF16), g)
        acc_ref[:, lo : lo + HEAD_DIM] += mm_nn(gst, q)
        gq_ref[0, :, lo : lo + HEAD_DIM] = (mm_tn(gst, k) * scale).astype(BF16)

    @pl.when(step == pl.num_programs(1) - 1)
    def _():
        gkv_ref[0] = acc_ref[...].astype(BF16)


def attend_back(qkv, grad_ctx, ctx, lse, bias_col, heads):
    chunks, seq, _ = qkv.shape
    block = min(256, seq)
    width = heads * HEAD_DIM
    return pl.pallas_call(
        functools.partial(attend_back_kernel, heads),
        grid=(chunks, seq // block),
        in_specs=[
            pl.BlockSpec((seq, 1), lambda i, j: (0, 0)),
            pl.BlockSpec((1, block, 3 * width), lambda i, j: (i, j, 0)),
            pl.BlockSpec((1, block, width), lambda i, j: (i, j, 0)),
            pl.BlockSpec((1, block, width), lambda i, j: (i, j, 0)),
            pl.BlockSpec((1, block, 8), lambda i, j: (i, j, 0)),
            pl.BlockSpec((1, seq, 3 * width), lambda i, j: (i, 0, 0)),
        ],
        out_specs=[
            pl.BlockSpec((1, block, width), lambda i, j: (i, j, 0)),
            pl.BlockSpec((1, seq, 2 * width), lambda i, j: (i, 0, 0)),
        ],
        out_shape=[
            jax.ShapeDtypeStruct((chunks, seq, width), BF16),
            jax.ShapeDtypeStruct((chunks, seq, 2 * width), BF16),
        ],
        scratch_shapes=[pltpu.VMEM((seq, 2 * width), F32)],
        cost_estimate=pl.CostEstimate(
            flops=40 * chunks * heads * seq * seq * HEAD_DIM,
            bytes_accessed=20 * chunks * seq * width,
            transcendentals=chunks * heads * seq * seq,
        ),
        name="attend_back",
    )(bias_col, qkv, grad_ctx, ctx, lse, qkv)


class Routes:
    def __init__(self, dp_size, mp_size):
        self.dp, self.mp = dp_size, mp_size
        self.bits = (dp_size // 2).bit_length() - 1
        self.mp_bits = mp_size.bit_length() - 1

    def _pairs(self, target):
        pairs = []
        for d in range(self.dp):
            for m in range(self.mp):
                dest = target(d // 2, d % 2, m)
                pairs.append((d * self.mp + m, (dest[0] * 2 + dest[1]) * self.mp + dest[2]))
        return pairs

    def send(self, value, target, back=False):
        pairs = self._pairs(target)
        if back:
            pairs = [(b, a) for a, b in pairs]
        return lax.ppermute(value, AXES, pairs)

    def partner(self, value):
        return self.send(value, lambda p, c, m: (p, 1 - c, m))

    def pair_bit(self, value, bit):
        return self.send(value, lambda p, c, m: (p ^ (1 << bit), c, m))

    def mp_bit(self, value, bit):
        return self.send(value, lambda p, c, m: (p, c, m ^ (1 << bit)))

    def cell(self, value, k, back=False):
        return self.send(value, lambda p, c, m: (p, m // 2, 2 * c + ((m % 2) ^ k)), back)

    def shard(self, value, k, back=False):
        return self.send(value, lambda p, c, m: (p, m // 2, m ^ k ^ (2 * c)), back)


def gather_shards(routes, shard):
    got = [routes.shard(shard, k) for k in range(4)]
    chunks = []
    for half in range(2):
        own = jnp.stack([got[half], got[half + 2]])
        order = range(routes.bits) if half else reversed(range(routes.bits))
        pieces = {0: own}
        for bit in order:
            if routes.bits <= 2:
                pieces.update({r | (1 << bit): routes.pair_bit(v, bit) for r, v in list(pieces.items())})
            else:
                keys = sorted(pieces)
                cat = routes.pair_bit(jnp.stack([pieces[r] for r in keys]), bit)
                pieces.update({r | (1 << bit): cat[i] for i, r in enumerate(keys)})
        chunks.append(pieces)
    return chunks


def assemble(pieces, mask):
    count = len(pieces)
    _, rows, width = pieces[0].shape
    full = jnp.zeros((count * 2 * rows, width), pieces[0].dtype)
    for r in range(count):
        for e in range(2):
            full = lax.dynamic_update_slice(full, pieces[r][e], ((((2 * r + e) ^ mask)) * rows, 0))
    return full


def scatter_grads(routes, chunks, mask):
    partial = []
    for half in range(2):
        full = chunks[half]
        count = 1 << routes.bits
        rows = full.shape[0] // (2 * count)
        blocks = full.reshape(2 * count, rows, full.shape[1])
        pieces = {
            r: jnp.stack([lax.dynamic_index_in_dim(blocks, (2 * r + e) ^ mask, 0, keepdims=False) for e in range(2)])
            for r in range(count)
        }
        order = range(routes.bits) if not half else reversed(range(routes.bits))
        for bit in order:
            keys = sorted(r for r in pieces if not r & (1 << bit))
            sent = routes.pair_bit(jnp.stack([pieces[r | (1 << bit)] for r in keys]), bit)
            pieces = {
                r: (pieces[r].astype(F32) + sent[i].astype(F32)).astype(BF16) for i, r in enumerate(keys)
            }
        partial.append(pieces[0])
    total = None
    for k in range(4):
        got = routes.shard(partial[k % 2][k // 2], k, back=True).astype(F32)
        total = got if total is None else total + got
    return total


MESH = pl.DeviceIdType.MESH


class Here:
    def __init__(self):
        self.d, self.m = lax.axis_index("dp"), lax.axis_index("mp")
        self.c = self.d % 2
        self.pair = self.d - self.c
        self.x = (self.d // 2) % 2
        self.y = self.d // 4
        self.t = self.m // 2
        self.b = self.m % 2
        self.over_x = {"dp": self.d + 2 - 4 * self.x, "mp": self.m}
        self.over_y = {"dp": self.d + 4 - 8 * self.y, "mp": self.m}
        self.partner = {"dp": self.d + 1 - 2 * self.c, "mp": self.m}
        self.home = self.t == self.c

    def at(self, core, m):
        return {"dp": self.pair + core, "mp": m}


def remote(src, dst, ssem, rsem, dev):
    return pltpu.make_async_remote_copy(
        src_ref=src, dst_ref=dst, send_sem=ssem, recv_sem=rsem, device_id=dev, device_id_type=MESH
    )


def arrived(dst, rsem, dev):
    remote(dst, dst, rsem, rsem, dev).wait_recv()


class Maybe:
    def __init__(self, src, dst, ssem, rsem, dev, own):
        self.args, self.dev, self.ssem, self.own = (src, dst), dev, ssem, own
        self.rsem = rsem

    def far(self):
        return remote(*self.args, self.ssem, self.rsem, self.dev)

    def start(self):
        pl.when(self.own)(lambda: pltpu.make_async_copy(*self.args, self.rsem).start())
        pl.when(jnp.logical_not(self.own))(lambda: self.far().start())

    def wait_send(self):
        pl.when(jnp.logical_not(self.own))(lambda: self.far().wait_send())


def greet(here):
    barrier = pltpu.get_barrier_semaphore()

    def tell(dev):
        pl.semaphore_signal(barrier, inc=1, device_id=dev, device_id_type=MESH)

    for core in range(2):
        for m in range(4):
            other = jnp.logical_or(here.c != core, here.m != m)
            pl.when(other)(functools.partial(tell, here.at(core, m)))
    tell(here.over_x)
    tell(here.over_y)
    pl.semaphore_wait(barrier, 9)


class Gather:
    def __init__(self, here, shard, full, sems, relayed):
        self.relayed = relayed
        (self.send_z, self.got_z, self.send_f, self.send_x, self.send_y, self.got_x, self.got_y, self.send_r, self.got_r) = sems
        self.here, self.shard, self.full = here, shard, full
        self.rows = shard.shape[0]
        self.first = jnp.where(here.m > 2 * here.c, 1, 0)

    @staticmethod
    def scratch():
        dma = pltpu.SemaphoreType.DMA
        return [dma((5,))] + [dma((2, 2))] * 8

    def plane(self, i):
        return (self.first + i) % 2

    def block(self, i, dp):
        return self.full.at[self.plane(i), pl.ds(dp * self.rows, self.rows), :]

    def z_copies(self):
        h = self.here
        dst = self.full.at[h.b, pl.ds(h.d * self.rows, self.rows), :]
        got = self.got_z.at[h.b, h.c]
        if self.relayed:
            far = [(h.m < 3, (h.m + 1) % 4), (h.m > 0, (h.m + 3) % 4)]
        else:
            far = [(h.m != m, m) for m in range(4)]
        copies = [
            (there, remote(self.shard, dst, self.send_z.at[n], got, h.at(h.t, m))) for n, (there, m) in enumerate(far)
        ]
        return Maybe(self.shard, dst, self.send_z.at[4], got, h.at(h.t, h.m), h.home), copies

    def start_near(self):
        self.z_copies()[0].start()

    def start_far(self):
        for there, copy in self.z_copies()[1]:
            pl.when(there)(copy.start)

    def onward(self, i, e):
        h = self.here
        source = 2 * h.c + self.plane(i)
        up = source < h.m
        there = jnp.logical_or(jnp.logical_and(up, h.m < 3), jnp.logical_and(source > h.m, h.m > 0))
        ref = self.block(i, h.pair + e)
        target = (h.m + 3 - 2 * up.astype(jnp.int32)) % 4
        return there, remote(ref, ref, self.send_f.at[i, e], self.got_z.at[self.plane(i), e], h.at(h.c, target))

    def own_copies(self, i, e):
        h = self.here
        ref = self.block(i, h.pair + e)
        return (
            remote(ref, ref, self.send_x.at[i, e], self.got_x.at[i, e], h.over_x),
            remote(ref, ref, self.send_y.at[i, e], self.got_y.at[i, e], h.over_y),
        )

    def spread(self, i):
        h = self.here
        for e in range(2):
            arrived(self.block(i, h.pair + e), self.got_z.at[self.plane(i), e], h.partner)
            if self.relayed:
                there, copy = self.onward(i, e)
                pl.when(there)(copy.start)
            for copy in self.own_copies(i, e):
                copy.start()

    def relay_copy(self, i, e):
        h = self.here
        if i == 0:
            ref, dev = self.block(i, h.over_y["dp"] - h.c + e), h.over_x
        else:
            ref, dev = self.block(i, h.over_x["dp"] - h.c + e), h.over_y
        return remote(ref, ref, self.send_r.at[i, e], self.got_r.at[i, e], dev)

    def relay(self, i):
        h = self.here
        for e in range(2):
            if i == 0:
                arrived(self.block(i, h.over_y["dp"] - h.c + e), self.got_y.at[i, e], h.over_y)
            else:
                arrived(self.block(i, h.over_x["dp"] - h.c + e), self.got_x.at[i, e], h.over_x)
            self.relay_copy(i, e).start()

    def finish(self):
        self.arrive()
        self.sent()

    def arrive(self):
        h = self.here
        diagonal = h.pair + 2 - 4 * h.x + 4 - 8 * h.y
        for i in range(2):
            for e in range(2):
                if i == 0:
                    arrived(self.block(i, h.over_x["dp"] - h.c + e), self.got_x.at[i, e], h.over_x)
                else:
                    arrived(self.block(i, h.over_y["dp"] - h.c + e), self.got_y.at[i, e], h.over_y)
                arrived(self.block(i, diagonal + e), self.got_r.at[i, e], h.over_x)

    def sent(self):
        near, far = self.z_copies()
        near.wait_send()
        for there, copy in far:
            pl.when(there)(copy.wait_send)
        for i in range(2):
            for e in range(2):
                if self.relayed:
                    there, copy = self.onward(i, e)
                    pl.when(there)(copy.wait_send)
                for copy in self.own_copies(i, e):
                    copy.wait_send()
                self.relay_copy(i, e).wait_send()


class ToCell:
    def __init__(self, here, source, rows, send, got):
        self.here, self.source, self.rows, self.send, self.got = here, source, rows, send, got

    def copy(self, s):
        h = self.here
        target = 2 * h.c + s
        own = jnp.logical_and(h.home, h.m == target)
        return Maybe(self.source.at[s], self.rows.at[h.b], self.send.at[s], self.got.at[h.b], h.at(h.t, target), own)

    def start(self):
        for s in range(2):
            self.copy(s).start()

    def wait(self):
        for b in range(2):
            arrived(self.rows.at[b], self.got.at[b], self.here.partner)

    def finish(self):
        for s in range(2):
            self.copy(s).wait_send()


class Norms:
    def __init__(self, here, slot, slots, sems):
        self.here, self.slot, self.slots = here, slot, slots
        self.send_z, self.got_z, self.send, self.got = sems

    @staticmethod
    def scratch():
        dma = pltpu.SemaphoreType.DMA
        return [dma((4,)), dma((4,)), dma((3,)), dma((3,))]

    def span(self, d, count):
        return self.slots.at[pl.ds(d * 4 // count * count, count)]

    def z_copy(self, m):
        h = self.here
        return Maybe(self.slot, self.slots.at[h.d * 4 + h.m], self.send_z.at[m], self.got_z.at[h.m], {"dp": h.d, "mp": m}, h.m == m)

    def copy(self, k):
        h = self.here
        ref = self.span(h.d, 4 << k)
        return remote(ref, ref, self.send.at[k], self.got.at[k], (h.partner, h.over_x, h.over_y)[k])

    def start_z(self):
        for m in range(4):
            self.z_copy(m).start()

    def wait_z(self):
        h = self.here
        for m in range(4):
            arrived(self.slots.at[h.d * 4 + m], self.got_z.at[m], h.partner)

    def start(self, k):
        self.copy(k).start()

    def wait(self, k):
        h = self.here
        dev = (h.partner, h.over_x, h.over_y)[k]
        arrived(self.span(dev["dp"], 4 << k), self.got.at[k], dev)

    def sent(self):
        for m in range(4):
            self.z_copy(m).wait_send()
        for k in range(3):
            self.copy(k).wait_send()


def norm_rows(values, gain, shift):
    mean_row = jnp.mean(values, axis=-1, keepdims=True)
    centred = values - mean_row
    inv_std = lax.rsqrt(jnp.mean(centred * centred, axis=-1, keepdims=True) + eps_norm)
    return centred * inv_std * gain + shift


ANY = pl.BlockSpec(memory_space=pl.ANY)
VMEM = pl.BlockSpec(memory_space=pltpu.VMEM)


def rows_at(start, size):
    return pl.ds(start * size, size)


def exact_gelu_both(u):
    below = 0.5 * (1.0 + lax.erf(u * (0.5**0.5)))
    density = jnp.exp(-0.5 * u * u) * ((2.0 * jnp.pi) ** -0.5)
    return u * below, below + u * density


class Stores:
    def __init__(self, sems):
        self.sems, self.made = sems, []

    def put(self, src, dst):
        copy = pltpu.make_async_copy(src, dst, self.sems.at[len(self.made)])
        copy.start()
        self.made.append((src, dst))

    def finish(self):
        for i, (src, dst) in enumerate(self.made):
            pltpu.make_async_copy(src, dst, self.sems.at[i]).wait()


def attend_rows(bias, qkv_ref, ctx_ref, lse_ref, chunk, start, block, heads):
    width = heads * HEAD_DIM
    spare = qkv_ref.shape[2] - 3 * width
    rows = pl.ds(start, block)
    stats = []
    for h in range(heads):
        lo = spare + h * HEAD_DIM
        q = qkv_ref[chunk, rows, lo : lo + HEAD_DIM] * jnp.asarray(HEAD_DIM**-0.5, BF16)
        k = qkv_ref[chunk, :, width + lo : width + lo + HEAD_DIM]
        v = qkv_ref[chunk, :, 2 * width + lo : 2 * width + lo + HEAD_DIM]
        s = mm_nt(q, k) + bias
        top = jnp.max(s, axis=-1, keepdims=True)
        e = jnp.exp(s - top)
        total = jnp.sum(e, axis=-1, keepdims=True)
        ctx = mm_nn(e.astype(BF16), v) / total
        ctx_ref[chunk, rows, h * HEAD_DIM : (h + 1) * HEAD_DIM] = ctx.astype(BF16)
        stats.append(top + jnp.log(total))
    stats += [jnp.zeros_like(stats[0])] * (8 - heads)
    lse_ref[chunk, :, rows] = jnp.concatenate(stats, axis=1).T


def forward_kernel(heads, *refs):
    (x_ref, gy_ref, shard_a, shard_1, shard_2, slot_ref) = refs[:6]
    (full_a, full_1, full_2, h1_out, qkv_out, ctx_out, lse_out, x_out, x2_out, h2_out, act_out, slope_out, gy_out,
     grad_out, norm_ref, count_ref) = refs[6:22]
    (weight, x_in, gy_in, h1, qkv, ctx, lse, fold_out, fold_in, x2, h2, act, slope, gy, stage, slots) = refs[22:38]
    sems = refs[38:]
    (cell_sems, swap_send, swap_got, load_sem, store_sems, stage_sems) = (
        sems[:4], sems[4], sems[5], sems[6], sems[7], sems[8]
    )
    here = Here()
    half, width = x2.shape
    seq = 2 * half
    quarter = half // 2
    inner = heads * HEAD_DIM
    greet(here)
    per = len(Gather.scratch())
    norms = Norms(here, slot_ref, slots, sems[9 + 3 * per :])
    block_a, block_1, block_2 = (
        Gather(here, shard, full, sems[9 + per * i : 9 + per * (i + 1)], i == 0)
        for i, (shard, full) in enumerate(((shard_a, full_a), (shard_1, full_1), (shard_2, full_2)))
    )
    cell_x = ToCell(here, x_ref, x_in, cell_sems[0], cell_sems[1])
    cell_g = ToCell(here, gy_ref, gy_in, cell_sems[2], cell_sems[3])
    stores = Stores(store_sems)

    def swap(n, src, dst):
        return remote(src, dst, swap_send.at[n], swap_got.at[n], here.partner)

    def load(full):
        copies = [pltpu.make_async_copy(full.at[b], weight.at[b], load_sem.at[b]) for b in range(2)]
        for copy in copies:
            copy.start()
        for copy in copies:
            copy.wait()

    own, other = pl.ds(0, half), pl.ds(half, half)
    away = jnp.logical_not(here.home)
    norms.start_z()
    block_a.start_far()
    for block in (block_a, block_1, block_2):
        block.start_near()
    block_a.spread(0)
    norms.wait_z()
    norms.start(0)
    block_a.relay(0)
    norms.wait(0)
    norms.start(1)
    cell_x.start()
    block_a.spread(1)
    norms.wait(1)
    norms.start(2)
    block_a.relay(1)
    pl.when(here.home)(lambda: block_1.spread(0))
    block_1.start_far()
    norms.wait(2)
    columns = norm_ref.shape[1] // 32
    for n in range(32):
        norm_ref[:, n * columns : (n + 1) * columns] = slots[n, 0:4, 0:columns]
    lanes = lax.broadcasted_iota(jnp.int32, (1, 128), 1)
    count_row = slots[(here.pair + here.t) * 4 + here.m, 4:5, :]
    count = jnp.sum(jnp.where(lanes == here.b, count_row, 0.0), axis=1, keepdims=True)
    count_ref[...] = jnp.broadcast_to(count, count_ref.shape)
    cell_x.wait()

    step = 128
    per_quarter = quarter // step

    @pl.loop(0, half // step)
    def _(i):
        rows = pl.ds(pl.multiple_of((i % per_quarter) * step, step), step)
        h1[pl.ds(pl.multiple_of(i * step, step), step), :] = norm_rows(
            x_in[i // per_quarter, rows, :].astype(F32), norm_ref[0:1, :], norm_ref[1:2, :]
        ).astype(BF16)

    swap_h1 = swap(0, h1.at[own], h1.at[other])
    swap_h1.start()
    stores.put(x_in, x_out)
    pl.when(away)(lambda: block_1.spread(0))
    block_a.arrive()
    pl.when(here.home)(lambda: block_1.relay(0))
    pl.when(here.home)(lambda: block_2.spread(0))
    load(full_a)
    swap_h1.wait_recv()
    stores.put(h1, h1_out)

    first = 4 * inner - qkv.shape[2]

    @pl.loop(0, 2)
    def _(b):
        for n in range(0, qkv.shape[2], 512):
            qkv[b, :, n : n + 512] = mm_nn(h1[...], weight[b, :, first + n : first + n + 512]).astype(BF16)

    stores.put(qkv, qkv_out)
    bias = key_bias(here, count, lax.broadcasted_iota(jnp.int32, (1, seq), 1), half)
    q_block = 256
    per_chunk = seq // q_block

    @pl.loop(0, 2 * per_chunk)
    def _(i):
        pl.when(jnp.logical_and(i == 1, away))(lambda: block_1.relay(0))
        pl.when(i == 4)(lambda: block_1.spread(1))
        pl.when(i == 4)(lambda: block_2.start_far())
        pl.when(jnp.logical_and(i == 5, here.home))(lambda: block_2.relay(0))
        pl.when(i == 7)(lambda: block_1.relay(1))
        attend_rows(
            bias, qkv, ctx, lse, i // per_chunk, pl.multiple_of((i % per_chunk) * q_block, q_block), q_block, heads
        )

    stores.put(ctx, ctx_out)
    stores.put(lse, lse_out)

    def branch_tile(rows, n):
        cols = pl.ds(pl.multiple_of(n * 256, 256), 256)
        return mm_nt(ctx[0, rows, :], weight[0, cols, 0:inner]) + mm_nt(ctx[1, rows, :], weight[1, cols, 0:inner]), cols

    @pl.loop(0, width // 256)
    def _(n):
        part, cols = branch_tile(other, n)
        fold_out[:, cols] = part.astype(BF16)

    swap_fold = swap(1, fold_out, fold_in)
    swap_fold.start()

    @pl.loop(0, width // 256)
    def _(n):
        part, cols = branch_tile(own, n)
        for b in range(2):
            rows = pl.ds(b * quarter, quarter)
            x2[rows, cols] = x_in[b, :, cols].astype(F32) + part[b * quarter : (b + 1) * quarter]

    pl.when(away)(lambda: block_2.spread(0))
    swap_fold.wait_recv()

    @pl.loop(0, half // step)
    def _(i):
        rows = pl.ds(pl.multiple_of(i * step, step), step)
        middle = x2[rows, :] + fold_in[rows, :].astype(F32)
        x2[rows, :] = middle
        h2[rows, :] = norm_rows(middle, norm_ref[2:3, :], norm_ref[3:4, :]).astype(BF16)

    swap_h2 = swap(2, h2.at[own], h2.at[other])
    swap_h2.start()
    stores.put(x2, x2_out)
    cell_g.start()
    block_1.arrive()
    load(full_1)
    swap_h2.wait_recv()
    stores.put(h2, h2_out)
    per_unit = width // 256

    @pl.loop(0, 2 * per_unit)
    def _(i):
        pl.when(jnp.logical_and(i == 0, away))(lambda: block_2.relay(0))
        pl.when(i == 3)(lambda: block_2.spread(1))
        pl.when(i == 9)(lambda: block_2.relay(1))
        b, cols = i // per_unit, pl.ds(pl.multiple_of((i % per_unit) * 256, 256), 256)
        value, grad = exact_gelu_both(mm_nn(h2[...], weight[b, :, cols]))
        act[b, :, cols] = value.astype(BF16)
        slope[b, :, cols] = grad.astype(BF16)

    stores.put(act, act_out)
    stores.put(slope, slope_out)
    cell_g.wait()

    @pl.loop(0, 2)
    def _(b):
        gy[pl.ds(pl.multiple_of(b * quarter, quarter), quarter), :] = gy_in[b]

    swap_gy = swap(3, gy.at[own], gy.at[other])
    swap_gy.start()
    swap_gy.wait_recv()
    stores.put(gy, gy_out)

    def stage_copy(i):
        slot = i % 2
        return pltpu.make_async_copy(
            stage.at[slot], grad_out.at[:, pl.ds(pl.multiple_of(i * 256, 256), 256), :], stage_sems.at[slot]
        )

    @pl.loop(0, width // 256)
    def _(i):
        pl.when(i >= 2)(lambda: stage_copy(i - 2).wait())
        left = gy[:, pl.ds(pl.multiple_of(i * 256, 256), 256)].T
        for b in range(2):
            stage[i % 2, b] = mm_nn(left, act[b]).astype(BF16)
        stage_copy(i).start()

    for i in range(width // 256 - 2, width // 256):
        stage_copy(i).wait()
    block_2.arrive()
    for block in (block_a, block_1, block_2):
        block.sent()
    cell_x.finish()
    cell_g.finish()
    norms.sent()
    for n, (src, dst) in enumerate(((h1.at[own], h1.at[other]), (fold_out, fold_in), (h2.at[own], h2.at[other]), (gy.at[own], gy.at[other]))):
        swap(n, src, dst).wait_send()
    stores.finish()


def key_bias(here, count, index, half):
    position = jnp.where(index < half, here.c * half + index, (1 - here.c) * half + index - half)
    return jnp.where(position.astype(F32) < 1.0 + count, 0.0, masked_score)


def forward(inputs, cotangent, shards, slot, heads, collective):
    cells, quarter, width = inputs.shape
    rows, wide = shards[0].shape
    half, seq, inner = 2 * quarter, 4 * quarter, heads * HEAD_DIM
    part = (3 * inner + 255) // 256 * 256
    dma = pltpu.SemaphoreType.DMA
    full = ((2, 8 * rows, wide), BF16)
    kept = [
        ((seq, width), BF16), ((2, seq, part), BF16), ((2, seq, inner), BF16), ((2, 8, seq), F32),
        ((2, quarter, width), BF16), ((half, width), F32), ((seq, width), BF16), ((2, seq, wide), BF16),
        ((2, seq, wide), BF16), ((seq, width), BF16), ((2, width, wide), BF16),
    ]
    buffers = [
        full, ((2, quarter, width), BF16), ((2, quarter, width), BF16), kept[0], kept[1], kept[2], kept[3],
        ((half, width), BF16), ((half, width), BF16), kept[5], kept[6], kept[7], kept[8], kept[9],
        ((2, 2, 256, wide), BF16), ((32, 8, 128), F32),
    ]
    return pl.pallas_call(
        functools.partial(forward_kernel, heads),
        out_shape=[jax.ShapeDtypeStruct(*s) for s in [full] * 3 + kept + [((4, width), F32), ((8, 128), F32)]],
        in_specs=[VMEM] * 6,
        out_specs=[ANY] * 14 + [VMEM] * 2,
        scratch_shapes=[pltpu.VMEM(*s) for s in buffers]
        + [dma((2,))] * 4 + [dma((4,)), dma((4,)), dma((2,)), dma((10,)), dma((2,))]
        + Gather.scratch() * 3 + Norms.scratch(),
        compiler_params=pltpu.CompilerParams(
            collective_id=collective, has_side_effects=True, vmem_limit_bytes=67043328
        ),
        name="forward",
    )(inputs, cotangent, *shards, slot)


class Reduce:
    def __init__(self, here, grads, bufs, sems):
        self.here, self.grads = here, grads
        self.own, self.one, self.two, self.far, self.last, self.part = bufs
        (self.sem_own, self.send_one, self.got_one, self.send_two, self.got_two, self.send_z, self.got_far, self.got_z) = sems
        self.piece = self.own.shape[2]
        self.before = None
        self.away = jnp.logical_not(here.home)
        self.outer = here.m % 3 == 0

    @staticmethod
    def scratch(rows, width):
        r = rows // 2
        dma = pltpu.SemaphoreType.DMA
        four = pltpu.VMEM((2, 4, r, width), BF16)
        landing = [pltpu.VMEM((2, 2, 4, r, width), BF16), four, four, pltpu.VMEM((3, 2, r, width), BF16)]
        sems = [dma((2, 2, 4)), dma((2, 2, 4)), dma((2, 4)), dma((2, 4)), dma((2, 4)), dma((2, 4)), dma((3, 2))]
        return pltpu.VMEM((2, 2, r, width), BF16), four, landing, sems

    def rows_of(self, role, dp, j):
        return self.grads.at[role, pl.ds(dp * 2 * self.piece + j * self.piece, self.piece), :]

    def pair_at(self, role, n, far):
        h = self.here
        dx, dy = 2 - 4 * h.x, 4 - 8 * h.y
        first, second = (dx, dy) if role == 0 else (dy, dx)
        return h.pair + (first if far else 0) + (second if n == 0 else 0)

    def copy_one(self, role, n, j):
        dev = self.here.over_x if role == 0 else self.here.over_y
        return remote(
            self.rows_of(role, self.pair_at(role, n, True), j), self.one.at[role, n, j],
            self.send_one.at[role, n, j], self.got_one.at[role, n, j], dev,
        )

    def copy_two(self, role, j):
        dev = self.here.over_y if role == 0 else self.here.over_x
        return remote(
            self.one.at[role, 0, j], self.two.at[role, j], self.send_two.at[role, j], self.got_two.at[role, j], dev
        )

    def to_inner(self, role, j):
        h = self.here
        return remote(
            self.part.at[role, j], self.far.at[role, j], self.send_z.at[role, j], self.got_far.at[role, j],
            h.at(h.c, h.m + 1 - 2 * h.b),
        )

    def to_owner(self, role, j):
        h = self.here
        target = 2 * h.c + role
        slot = jnp.where(self.away, 2, (h.m + target) % 2)
        return remote(
            self.part.at[role, j], self.last.at[slot, j % 2], self.send_z.at[role, j], self.got_z.at[slot, j % 2],
            h.at(j // 2, target),
        )

    def mine(self, role, j):
        return jnp.logical_and(self.here.c == j // 2, self.here.m == 2 * self.here.c + role)

    def direct(self, role, j):
        return jnp.logical_and(self.here.home, jnp.logical_not(self.mine(role, j)))

    def start_one(self, j):
        for n in range(2):
            for role in range(2):
                self.copy_one(role, n, j).start()

    def start(self):
        for j in range(3):
            self.start_one(j)
        for role in range(2):
            for n in range(2):
                self.load_piece(role, n, 0).start()

    def load_piece(self, role, n, j):
        return pltpu.make_async_copy(
            self.rows_of(role, self.pair_at(role, n, False), j), self.own.at[role, n], self.sem_own.at[role, n]
        )

    def add_one(self, role, j):
        h = self.here
        for n in range(2):
            self.load_piece(role, n, j).wait()
            arrived(self.one.at[role, n, j], self.got_one.at[role, n, j], h.over_x)
            total = self.own[role, n].astype(F32) + self.one[role, n, j].astype(F32)
            self.one[role, n, j] = total.astype(BF16)
            if n == 0:
                self.copy_two(role, j).start()
            if j < 3:
                self.load_piece(role, n, j + 1).start()

    def add_two(self, role, j):
        arrived(self.two.at[role, j], self.got_two.at[role, j], self.here.over_x)
        total = (self.one[role, 1, j].astype(F32) + self.two[role, j].astype(F32)).astype(BF16)
        if self.before is not None:
            self.before.z_sent(role, j)

        @pl.when(self.mine(role, j))
        def _():
            self.last[0, j % 2] = total

        @pl.when(jnp.logical_not(self.mine(role, j)))
        def _():
            self.part[role, j] = total

        pl.when(self.direct(role, j))(lambda: self.to_owner(role, j).start())
        pl.when(jnp.logical_and(self.away, self.outer))(lambda: self.to_inner(role, j).start())

    def pass_on(self, role, j):
        @pl.when(jnp.logical_and(self.away, jnp.logical_not(self.outer)))
        def _():
            arrived(self.far.at[role, j], self.got_far.at[role, j], self.here.partner)
            total = self.part[role, j].astype(F32) + self.far[role, j].astype(F32)
            self.part[role, j] = total.astype(BF16)
            self.to_owner(role, j).start()

    def step(self, j):
        for role in range(2):
            if j < 4:
                self.add_one(role, j)
        if j == 0:
            self.start_one(3)
        for role in range(2):
            if 1 <= j <= 4:
                self.add_two(role, j - 1)
        for role in range(2):
            if j >= 2:
                self.pass_on(role, j - 2)

    def z_sent(self, role, j):
        inner = jnp.logical_and(self.away, jnp.logical_not(self.outer))
        pl.when(jnp.logical_or(self.direct(role, j), inner))(lambda: self.to_owner(role, j).wait_send())
        pl.when(jnp.logical_and(self.away, self.outer))(lambda: self.to_inner(role, j).wait_send())

    def finish(self, total, out_ref, sem):
        h = self.here
        for s in range(2):
            pl.when(self.away)(functools.partial(arrived, self.last.at[0, s], self.got_z.at[0, s], h.partner))
            for n in range(1, 3):
                arrived(self.last.at[n, s], self.got_z.at[n, s], h.partner)
            rows = self.last[0, s].astype(F32)
            for n in range(1, 3):
                rows = rows + self.last[n, s].astype(F32)
            total[pl.ds(s * self.piece, self.piece), :] = rows
        copy = pltpu.make_async_copy(total, out_ref, sem)
        copy.start()
        for role in range(2):
            for j in range(4):
                for n in range(2):
                    self.copy_one(role, n, j).wait_send()
                self.copy_two(role, j).wait_send()
        copy.wait()


class FromCell:
    def __init__(self, here, rows, landing, send, got):
        self.here, self.rows, self.landing, self.send, self.got = here, rows, landing, send, got

    def copy(self, b):
        h = self.here
        target = 2 * h.c + b
        own = jnp.logical_and(h.home, h.m == target)
        return Maybe(self.rows.at[b], self.landing.at[h.b], self.send.at[b], self.got.at[h.b], h.at(h.t, target), own)

    def start(self):
        for b in range(2):
            self.copy(b).start()

    def sent(self):
        for b in range(2):
            self.copy(b).wait_send()

    def arrive(self):
        for s in range(2):
            arrived(self.landing.at[s], self.got.at[s], self.here.partner)


def norm_rows_back(values, grad_out, gain):
    mean_row = jnp.mean(values, axis=-1, keepdims=True)
    centred = values - mean_row
    inv_std = lax.rsqrt(jnp.mean(centred * centred, axis=-1, keepdims=True) + eps_norm)
    scaled = centred * inv_std
    grad_scaled = grad_out * gain
    centre_part = jnp.mean(grad_scaled, axis=-1, keepdims=True)
    along_part = scaled * jnp.mean(grad_scaled * scaled, axis=-1, keepdims=True)
    grad_in = inv_std * (grad_scaled - centre_part - along_part)
    return grad_in, jnp.sum(grad_out * scaled, axis=0, keepdims=True), jnp.sum(grad_out, axis=0, keepdims=True)


def attend_rows_back(bias, qkv_ref, gctx_ref, ctx_ref, lse_ref, grad_ref, acc_ref, chunk, start, block, heads):
    width = heads * HEAD_DIM
    spare = -3 * width % 256
    half = acc_ref.shape[0]
    rows = pl.ds(start, block)
    scale = HEAD_DIM**-0.5
    for h in range(heads):
        at = slice(h * HEAD_DIM, (h + 1) * HEAD_DIM)
        lo = spare + h * HEAD_DIM
        q = qkv_ref[chunk, rows, lo : lo + HEAD_DIM] * jnp.asarray(scale, BF16)
        k = qkv_ref[chunk, :, width + lo : width + lo + HEAD_DIM]
        v = qkv_ref[chunk, :, 2 * width + lo : 2 * width + lo + HEAD_DIM]
        g = gctx_ref[chunk, rows, at]
        delta = jnp.sum(g.astype(F32) * ctx_ref[chunk, rows, at].astype(F32), axis=-1, keepdims=True).T
        pt = jnp.exp(mm_nt(k, q) + bias - lse_ref[chunk, h : h + 1, rows])
        gst = (pt * (mm_nt(v, g) - delta)).astype(BF16)
        gk = mm_nn(gst, q)
        gv = mm_nn(pt.astype(BF16), g)
        for n, part in enumerate((gk[:half], gk[half:], gv[:half], gv[half:])):
            acc_ref[:, n * width + h * HEAD_DIM : n * width + (h + 1) * HEAD_DIM] += part
        grad_ref[chunk, rows, lo : lo + HEAD_DIM] = (mm_tn(gst, k) * scale).astype(BF16)


def backward_kernel(heads, *refs):
    (norm_ref, count_ref, full_a, full_1, full_2, h1_in, qkv_in, ctx_in, lse_in, x_src, x2_src, h2_in, act_in, slope_in,
     gy_src, grad_2) = refs[:16]
    (out_ref, gx_ref, sum_a, sum_1, sum_2, norm_out, grad_1, grad_a) = refs[16:24]
    (weight, gy, slope, act, h2, x2, fold_out, fold_in, gctx, ctx, lse, acc, stage, own, part) = refs[24:39]
    landings = [refs[39 + 4 * i : 43 + 4 * i] for i in range(3)]
    sums, sums_in = refs[51:53]
    sems = refs[53:]
    send_rows = stage
    (load_sems, swap_send, swap_got, cell_sems, stage_sems, own_sem, total_sem) = (
        sems[:10], sems[10], sems[11], sems[12:16], sems[16], sems[17], sems[18]
    )
    per = 7
    here = Here()
    half, width = x2.shape
    seq, quarter, inner = 2 * half, half // 2, heads * HEAD_DIM
    part_width = (3 * inner + 255) // 256 * 256
    first = 4 * inner - part_width
    spare = part_width - 3 * inner
    greet(here)
    blocks = [
        Reduce(here, grads, (own, *landings[i], part), (own_sem, *sems[19 + per * i : 19 + per * (i + 1)]))
        for i, grads in enumerate((grad_2, grad_1, grad_a))
    ]
    block_2, block_1, block_a = blocks
    own_rows, other_rows = pl.ds(0, half), pl.ds(half, half)

    def load(n, src, dst):
        return pltpu.make_async_copy(src, dst, load_sems[n])

    copies = {
        "w2": load(0, full_2, weight), "gy": load(1, gy_src, gy), "slope": load(2, slope_in, slope),
        "act": load(3, act_in, act), "h2": load(4, h2_in, h2), "x2": load(5, x2_src, x2), "ctx": load(6, ctx_in, ctx),
        "lse": load(7, lse_in, lse),
    }
    block_2.start()
    for copy in copies.values():
        copy.start()

    def fetch(src, dst):
        copy = load(9, src, dst)
        copy.start()
        return copy

    def swap(n, src, dst):
        return remote(src, dst, swap_send.at[n], swap_got.at[n], here.partner)

    def tile(n):
        return pl.ds(pl.multiple_of(n * 256, 256), 256)

    tiles = width // 256
    per_unit = width // 256

    copies["w2"].wait()
    copies["act"].wait()

    @pl.loop(0, tiles)
    def _(n):
        cols = tile(n)
        fold_out[:, cols] = (
            mm_nt(act[0, other_rows, :], weight[0, cols, :]) + mm_nt(act[1, other_rows, :], weight[1, cols, :])
        ).astype(BF16)

    swaps = [(fold_out, fold_in.at[0]), (fold_out, fold_in.at[1]), (h2.at[own_rows], h2.at[other_rows]), (fold_out, fold_in.at[0])]
    swap(0, *swaps[0]).start()

    for name in ("gy", "slope"):
        copies[name].wait()

    @pl.loop(0, 2 * per_unit)
    def _(i):
        pl.when(i == 4)(lambda: block_2.step(0))
        b, cols = i // per_unit, tile(i % per_unit)
        grad = mm_nn(gy[...], weight[b, :, cols])
        slope[b, :, cols] = (grad * slope[b, :, cols].astype(F32)).astype(BF16)

    block_2.step(1)
    copies["h2"].wait()

    def stage_copy(grads, i, b):
        return pltpu.make_async_copy(stage.at[b], grads.at[b, tile(i), :], stage_sems.at[b])

    @pl.loop(0, tiles)
    def _(i):
        left = h2[:, tile(i)].T
        for b in range(2):
            pl.when(i >= 1)(lambda: stage_copy(grad_1, i - 1, b).wait())
            stage[b] = mm_nn(left, slope[b]).astype(BF16)
            stage_copy(grad_1, i, b).start()
        pl.when(i == 1)(lambda: block_2.step(2))

    for b in range(2):
        stage_copy(grad_1, tiles - 1, b).wait()
    block_2.step(3)
    block_1.start()
    copies["x2"].wait()
    swap(0, *swaps[0]).wait_recv()

    @pl.loop(0, tiles)
    def _(n):
        cols = tile(n)
        mine = mm_nt(act[0, own_rows, :], weight[0, cols, :]) + mm_nt(act[1, own_rows, :], weight[1, cols, :])
        mine = (mine + x2[:, cols] + fold_in[0, :, cols].astype(F32)).astype(BF16)
        for b in range(2):
            send_rows[b, :, cols] = mine[b * quarter : (b + 1) * quarter]

    cell_out = FromCell(here, send_rows, out_ref, cell_sems[0], cell_sems[1])
    cell_out.start()
    fetch(full_1, weight).wait()
    fetched = fetch(qkv_in, act.at[:, :, 0:part_width])
    swap(0, *swaps[0]).wait_send()

    @pl.loop(0, tiles)
    def _(n):
        cols = tile(n)
        fold_out[:, cols] = (
            mm_nt(slope[0, other_rows, :], weight[0, cols, :]) + mm_nt(slope[1, other_rows, :], weight[1, cols, :])
        ).astype(BF16)

    swap(1, *swaps[1]).start()

    @pl.loop(0, tiles)
    def _(n):
        cols = tile(n)
        acc[:, cols] = mm_nt(slope[0, own_rows, :], weight[0, cols, :]) + mm_nt(slope[1, own_rows, :], weight[1, cols, :])

    fetched.wait()
    fetched = fetch(full_a, weight)
    swap(1, *swaps[1]).wait_recv()
    step = 128
    sums[0] = jnp.zeros(sums.shape[1:], F32)

    @pl.loop(0, half // step)
    def _(i):
        rows = pl.ds(pl.multiple_of(i * step, step), step)
        grad_in, gain_sum, shift_sum = norm_rows_back(
            x2[rows, :], acc[rows, :] + fold_in[1, rows, :].astype(F32), norm_ref[2:3, :]
        )
        sums[0, 2:3, :] += gain_sum
        sums[0, 3:4, :] += shift_sum
        grad_in = gy[rows, :].astype(F32) + grad_in
        x2[rows, :] = grad_in
        h2[rows, :] = grad_in.astype(BF16)

    swap(2, *swaps[2]).start()
    fetched.wait()
    fetched = fetch(h1_in, gy)
    block_2.step(4)
    block_1.before, block_a.before = block_2, block_1
    copies["ctx"].wait()
    copies["lse"].wait()
    swap(2, *swaps[2]).wait_recv()

    for b in range(2):
        gctx[b] = mm_nn(h2[...], weight[b, :, 0:inner]).astype(BF16)
        slope[b, :, 0:spare] = jnp.zeros((seq, spare), BF16)
    bias = key_bias(here, count_ref[0:1, 0:1], lax.broadcasted_iota(jnp.int32, (seq, 1), 0), half)
    q_block = 256
    per_chunk = seq // q_block

    @pl.loop(0, 2 * per_chunk)
    def _(i):
        b, j = i // per_chunk, i % per_chunk

        @pl.when(j == 0)
        def _():
            acc[...] = jnp.zeros_like(acc)

        attend_rows_back(
            bias, act, gctx, ctx, lse, slope, acc, b, pl.multiple_of(j * q_block, q_block), q_block, heads
        )

        @pl.when(j == per_chunk - 1)
        def _():
            for n in range(4):
                lo = spare + (1 + n // 2) * inner
                slope[b, pl.ds((n % 2) * half, half), lo : lo + inner] = acc[:, n * inner : (n + 1) * inner].astype(BF16)

        pl.when(i == 0)(lambda: block_1.step(0))
        pl.when(i == 1)(lambda: block_2.step(5))
        pl.when(i == 2)(lambda: block_1.step(1))
        pl.when(i == 4)(lambda: block_1.step(2))
        pl.when(i == 6)(lambda: block_1.step(3))

    fetched.wait()

    cell_out.sent()
    cell_out.arrive()

    @pl.loop(0, tiles)
    def _(i):
        left = gy[:, tile(i)].T
        left_out = h2[:, tile(i)].T
        for b in range(2):
            pl.when(i >= 1)(lambda: stage_copy(grad_a, i - 1, b).wait())
            stage[b, :, first:] = mm_nn(left, slope[b, :, 0:part_width]).astype(BF16)
            stage[b, :, 0:inner] = mm_nn(left_out, ctx[b]).astype(BF16)
            stage_copy(grad_a, i, b).start()

    for b in range(2):
        stage_copy(grad_a, tiles - 1, b).wait()
    fetched = fetch(x_src, stage)
    block_a.start()
    block_1.step(4)
    total = acc.at[0 : sum_2.shape[0], :]
    swap(1, *swaps[1]).wait_send()

    @pl.loop(0, tiles)
    def _(n):
        cols = tile(n)
        fold_out[:, cols] = sum(
            mm_nt(slope[b, other_rows, 0:part_width], weight[b, cols, first:]) for b in range(2)
        ).astype(BF16)

    swap(3, *swaps[3]).start()
    block_2.finish(total, sum_2, total_sem)
    block_1.step(5)

    @pl.loop(0, tiles)
    def _(n):
        cols = tile(n)
        acc[:, cols] = sum(mm_nt(slope[b, own_rows, 0:part_width], weight[b, cols, first:]) for b in range(2))

    fetched.wait()
    block_a.step(0)
    swap(3, *swaps[3]).wait_recv()
    per_quarter = quarter // step

    @pl.loop(0, half // step)
    def _(i):
        b, inside = i // per_quarter, pl.ds(pl.multiple_of((i % per_quarter) * step, step), step)
        rows = pl.ds(pl.multiple_of(i * step, step), step)
        grad_in, gain_sum, shift_sum = norm_rows_back(
            stage[b, inside, :].astype(F32), acc[rows, :] + fold_in[0, rows, :].astype(F32), norm_ref[0:1, :]
        )
        sums[0, 0:1, :] += gain_sum
        sums[0, 1:2, :] += shift_sum
        send_rows[b, inside, :] = (x2[rows, :] + grad_in).astype(BF16)

    cell_gx = FromCell(here, send_rows, gx_ref, cell_sems[2], cell_sems[3])
    cell_gx.start()
    peers = (
        here.partner, here.over_x, here.over_y, {"dp": here.d, "mp": here.m + 1 - 2 * here.b},
        {"dp": here.d, "mp": here.m + 2 - 4 * here.t},
    )
    sum_send, sum_got = sems[-2:]

    def share(k):
        return remote(sums.at[k], sums_in.at[k], sum_send.at[k], sum_got.at[k], peers[k])

    def add_sums(k):
        share(k).wait_recv()
        sums[k + 1] = sums[k] + sums_in[k]
        if k < 4:
            share(k + 1).start()

    share(0).start()
    add_sums(0)
    add_sums(1)
    block_a.step(1)
    add_sums(2)
    block_1.finish(total, sum_1, total_sem)
    add_sums(3)
    block_a.step(2)
    add_sums(4)
    norm_out[...] = sums[5]
    block_a.step(3)
    block_a.step(4)
    block_a.step(5)
    for k in range(5):
        share(k).wait_send()
    cell_gx.arrive()
    block_a.finish(total, sum_a, total_sem)
    for role in range(2):
        for j in range(4):
            block_a.z_sent(role, j)
    cell_gx.sent()
    for n in (2, 3):
        swap(n, *swaps[n]).wait_send()


def backward(kept, heads, collective):
    kept, (norms, count) = kept[:14], kept[14:]
    (full_a, full_1, full_2, h1, qkv, ctx, lse, x_in, x2, h2, act, slope, gy, grad_2) = kept
    half, width = x2.shape
    quarter, seq = half // 2, 2 * half
    wide = act.shape[2]
    rows = width // 8
    inner = heads * HEAD_DIM
    dma = pltpu.SemaphoreType.DMA
    buffers = [
        (full_a.shape, BF16), (gy.shape, BF16), (slope.shape, BF16), (act.shape, BF16), (h2.shape, BF16), (x2.shape, F32),
        ((half, width), BF16), ((2, half, width), BF16), (ctx.shape, BF16), (ctx.shape, BF16), (lse.shape, F32),
        ((half, width), F32), (x_in.shape, BF16),
    ]
    own, part, landing, reduce_sems = Reduce.scratch(rows, wide)
    return pl.pallas_call(
        functools.partial(backward_kernel, heads),
        out_shape=[jax.ShapeDtypeStruct(x_in.shape, BF16)] * 2
        + [jax.ShapeDtypeStruct((rows, wide), F32)] * 3
        + [jax.ShapeDtypeStruct((4, width), F32)]
        + [jax.ShapeDtypeStruct(grad_2.shape, BF16)] * 2,
        in_specs=[VMEM] * 2 + [ANY] * 14,
        out_specs=[ANY] * 5 + [VMEM] + [ANY] * 2,
        scratch_shapes=[pltpu.VMEM(*s) for s in buffers]
        + [own, part] + landing * 3
        + [pltpu.VMEM((6, 4, width), F32), pltpu.VMEM((5, 4, width), F32)]
        + [dma] * 10 + [dma((4,)), dma((4,))] + [dma((2,))] * 4 + [dma((2,)), dma((2, 2)), dma]
        + reduce_sems * 3 + [dma((5,))] * 2,
        compiler_params=pltpu.CompilerParams(
            collective_id=collective, has_side_effects=True, vmem_limit_bytes=67043328
        ),
        name="backward",
    )(norms, count, *kept)


def gather_norms(routes, norm_params, d, m):
    cur = norm_params
    for bit in range(routes.mp_bits):
        got = routes.mp_bit(cur, bit)
        high = ((m >> bit) & 1) == 1
        cur = jnp.where(high, jnp.concatenate([got, cur], 1), jnp.concatenate([cur, got], 1))
    for bit in range(routes.bits + 1):
        got = routes.partner(cur) if bit == 0 else routes.pair_bit(cur, bit - 1)
        high = ((d >> bit) & 1) == 1
        cur = jnp.where(high, jnp.concatenate([got, cur], 1), jnp.concatenate([cur, got], 1))
    return cur


def scatter_norms(routes, grads, d, m):
    cur = grads
    for bit in reversed(range(routes.bits + 1)):
        low, up = jnp.split(cur, 2, axis=1)
        high = ((d >> bit) & 1) == 1
        give = jnp.where(high, low, up)
        got = routes.partner(give) if bit == 0 else routes.pair_bit(give, bit - 1)
        cur = jnp.where(high, up, low) + got
    for bit in reversed(range(routes.mp_bits)):
        low, up = jnp.split(cur, 2, axis=1)
        high = ((m >> bit) & 1) == 1
        cur = jnp.where(high, up, low) + routes.mp_bit(jnp.where(high, low, up), bit)
    return cur


def update(
    outputs, input_grad, norm_sum, attend_sum, expand_sum, reduce_sum, step_count, norm_params, norm_first, norm_second,
    attend_weight, attend_first, attend_second, output_weight, output_first, output_second,
    expand_weight, expand_first, expand_second, reduce_weight, reduce_first, reduce_second,
):
    width = attend_weight.shape[2]
    step_number = step_count[0].astype(F32)
    norm_new = adam_step(norm_params, norm_first, norm_second, norm_sum, norm_rate, 0.0, step_number)
    attend_reduced = jnp.stack([attend_sum[:, i * width : (i + 1) * width] for i in range(1, 4)])
    attend_new = adam_step(
        attend_weight, attend_first, attend_second, attend_reduced, 2.0 * D ** (-0.5), decay_rate, step_number
    )
    output_new = adam_step(
        output_weight, output_first, output_second, attend_sum[:, :width].T,
        2.0 * (2 * D // SEQ) ** (-0.5), decay_rate, step_number,
    )
    expand_new = adam_step(
        expand_weight, expand_first, expand_second, expand_sum, 2.0 * D ** (-0.5), decay_rate, step_number
    )
    reduce_new = adam_step(
        reduce_weight, reduce_first, reduce_second, reduce_sum.T, 2.0 * FF ** (-0.5), decay_rate, step_number
    )
    return (
        outputs, input_grad,
        norm_new[0], norm_new[1], norm_new[2][0:2], norm_new[2][2:4],
        *attend_new, *output_new, *expand_new, *reduce_new,
    )


def per_device_plain(
    inputs, cotangent, gene_counts, step_count, norm_params, norm_first, norm_second,
    attend_weight, attend_first, attend_second, output_weight, output_first, output_second,
    expand_weight, expand_first, expand_second, reduce_weight, reduce_first, reduce_second,
):
    routes = Routes(lax.axis_size("dp"), lax.axis_size("mp"))
    d, m = lax.axis_index("dp"), lax.axis_index("mp")
    c = d % 2
    cells, quarter, _ = inputs.shape
    assert routes.mp == 4 and 2 * cells == routes.mp and routes.dp % 2 == 0
    half = 2 * quarter
    seq = 2 * half
    heads = attend_weight.shape[2] // HEAD_DIM
    width = heads * HEAD_DIM
    m_low, m_high = m % 2, m // 2
    mask = 2 * (d // 2) + ((c + m_high) % 2)

    norm_full = gather_norms(routes, norm_params, d, m)

    def to_cell(values):
        got = [
            routes.cell(lax.dynamic_index_in_dim(values, (m_low + k) % 2, 0, keepdims=False), k) for k in range(2)
        ]
        return jnp.concatenate(got, 0)

    def from_cell(rows):
        rows = rows.astype(BF16)
        got = [routes.cell(rows[k * quarter : (k + 1) * quarter], k, back=True) for k in range(2)]
        flip = m_low == 1
        return jnp.stack([jnp.where(flip, got[1], got[0]), jnp.where(flip, got[0], got[1])]).astype(F32)

    attend_shard = jnp.concatenate(
        [output_weight.T, attend_weight[0], attend_weight[1], attend_weight[2]], axis=1
    ).astype(BF16)
    expand_shard = expand_weight.astype(BF16)
    reduce_shard = reduce_weight.T.astype(BF16)

    x_mine = to_cell(inputs).astype(F32)
    attend_w = [assemble(pieces, mask) for pieces in gather_shards(routes, attend_shard)]
    expand_w = [assemble(pieces, mask) for pieces in gather_shards(routes, expand_shard)]
    reduce_w = [assemble(pieces, mask) for pieces in gather_shards(routes, reduce_shard)]
    gy_mine = to_cell(cotangent)

    other_counts = routes.partner(gene_counts)
    mine = jnp.where(m_high == c, gene_counts, other_counts)
    count = jnp.where(m_low == 1, mine[1], mine[0])
    inside = jnp.arange(quarter)
    first = m_low
    positions = jnp.concatenate(
        [h * half + b * quarter + inside for h, b in ((c, first), (c, 1 - first), (1 - c, first), (1 - c, 1 - first))]
    )
    bias = jnp.where(positions < 1 + count, 0.0, masked_score).astype(F32)

    def both(rows):
        return jnp.concatenate([rows, routes.partner(rows)], 0)

    def fold(partial):
        return partial[:half] + routes.partner(partial[half:].astype(BF16)).astype(F32)

    normed, scaled_one, inv_one = normalize(x_mine, norm_full[0], norm_full[1])
    h1 = both(normed.astype(BF16))
    qkv = jnp.stack([mm_nn(h1, w[:, width:]).astype(BF16) for w in attend_w])
    ctx, lse = attend(qkv, bias[None, :], heads)
    branch = mm_nt(ctx[0], attend_w[0][:, :width]) + mm_nt(ctx[1], attend_w[1][:, :width])
    x2 = x_mine + fold(branch)
    normed, scaled_two, inv_two = normalize(x2, norm_full[2], norm_full[3])
    h2 = both(normed.astype(BF16))
    hidden = [mm_nn(h2, w) for w in expand_w]
    active = [exact_gelu(u).astype(BF16) for u in hidden]
    branch = mm_nt(active[0], reduce_w[0]) + mm_nt(active[1], reduce_w[1])
    outputs = from_cell(x2 + fold(branch))

    gy = both(gy_mine)
    reduce_grad = [mm_tn(gy, a).astype(BF16) for a in active]
    grad_hidden = [
        jax.vjp(exact_gelu, u)[1](mm_nn(gy, w))[0].astype(BF16) for u, w in zip(hidden, reduce_w)
    ]
    expand_grad = [mm_tn(h2, g).astype(BF16) for g in grad_hidden]
    gh2 = fold(mm_nt(grad_hidden[0], expand_w[0]) + mm_nt(grad_hidden[1], expand_w[1]))
    grad_in, gain_two, shift_two = normalize_back(gh2, scaled_two, inv_two, norm_full[2])
    gx2 = gy_mine.astype(F32) + grad_in
    gb = both(gx2.astype(BF16))
    grad_ctx = jnp.stack([mm_nn(gb, w[:, :width]).astype(BF16) for w in attend_w])
    gq, gkv = attend_back(qkv, grad_ctx, ctx, lse, bias[:, None], heads)
    attend_grad = [
        jnp.concatenate(
            [mm_tn(gb, ctx[i]), mm_tn(h1, gq[i]), mm_tn(h1, gkv[i])], axis=1
        ).astype(BF16)
        for i in range(2)
    ]
    gh1 = fold(
        sum(
            mm_nt(gq[i], attend_w[i][:, width : 2 * width]) + mm_nt(gkv[i], attend_w[i][:, 2 * width :])
            for i in range(2)
        )
    )
    grad_in, gain_one, shift_one = normalize_back(gh1, scaled_one, inv_one, norm_full[0])
    input_grad = from_cell(gx2 + grad_in)

    reduce_sum = scatter_grads(routes, reduce_grad, mask)
    expand_sum = scatter_grads(routes, expand_grad, mask)
    attend_sum = scatter_grads(routes, attend_grad, mask)
    norm_sum = scatter_norms(routes, jnp.stack([gain_one, shift_one, gain_two, shift_two]), d, m)

    return update(
        outputs, input_grad, norm_sum, attend_sum, expand_sum, reduce_sum, step_count, norm_params, norm_first,
        norm_second, attend_weight, attend_first, attend_second, output_weight, output_first, output_second,
        expand_weight, expand_first, expand_second, reduce_weight, reduce_first, reduce_second,
    )


def per_device(
    inputs, cotangent, gene_counts, step_count, norm_params, norm_first, norm_second,
    attend_weight, attend_first, attend_second, output_weight, output_first, output_second,
    expand_weight, expand_first, expand_second, reduce_weight, reduce_first, reduce_second,
):
    d, m, mp_size = lax.axis_index("dp"), lax.axis_index("mp"), lax.axis_size("mp")
    cells = inputs.shape[0]
    assert mp_size == 4 and 2 * cells == mp_size and lax.axis_size("dp") == 8
    heads = attend_weight.shape[2] // HEAD_DIM
    shards = (
        jnp.concatenate([output_weight.T, attend_weight[0], attend_weight[1], attend_weight[2]], axis=1).astype(BF16),
        expand_weight.astype(BF16),
        reduce_weight.T.astype(BF16),
    )
    slot = jnp.zeros((8, 128), F32)
    slot = slot.at[0:4, 0 : norm_params.shape[1]].set(norm_params).at[4, 0:cells].set(gene_counts.astype(F32))
    kept = forward(inputs, cotangent, shards, slot, heads, 1)
    outputs, input_grad, attend_sum, expand_sum, reduce_sum, norm_part, _, _ = backward(kept, heads, 2)
    outputs, input_grad = outputs.astype(F32), input_grad.astype(F32)
    columns = norm_params.shape[1]
    norm_sum = lax.dynamic_slice(norm_part, (0, (d * mp_size + m) * columns), (4, columns))
    return update(
        outputs, input_grad, norm_sum, attend_sum, expand_sum, reduce_sum, step_count, norm_params, norm_first,
        norm_second, attend_weight, attend_first, attend_second, output_weight, output_first, output_second,
        expand_weight, expand_first, expand_second, reduce_weight, reduce_first, reduce_second,
    )


def solution(mesh):
    norms = P(None, ("dp", "mp"))
    attend_spec, col, row = P(None, "dp", "mp"), P("mp", "dp"), P("dp", "mp")
    tokens = P("dp", "mp", None)
    return jax.shard_map(
        per_device if mesh.shape["dp"] == 8 else per_device_plain,
        mesh=mesh,
        in_specs=(tokens, tokens, P("dp"), P(), norms, norms, norms)
        + (attend_spec,) * 3 + (col,) * 3 + (row,) * 3 + (col,) * 3,
        out_specs=(tokens, tokens, norms, norms, norms, norms)
        + (attend_spec,) * 3 + (col,) * 3 + (row,) * 3 + (col,) * 3,
        check_vma=False,
    )
```

```python
import functools

import jax
import jax.numpy as jnp
from jax import lax
from jax.experimental import pallas as pl
from jax.experimental.pallas import tpu as pltpu
from jax.sharding import PartitionSpec as P

D = 1280
HEAD_DIM = 64
FF = 5120
SEQ = 1024

eps_norm = 1e-05
masked_score = -1e30
beta_one = 0.9
beta_two = 0.95
eps_adam = 1e-08
decay_rate = 0.1
norm_rate = 0.6

F32 = jnp.float32
BF16 = jnp.bfloat16
AXES = ("dp", "mp")


def exact_gelu(values):
    return jax.nn.gelu(values, approximate=False)


def mm(left, right, dims):
    return lax.dot_general(left, right, (dims, ((), ())), preferred_element_type=F32)


def mm_nn(left, right):
    return mm(left, right, ((1,), (0,)))


def mm_nt(left, right):
    return mm(left, right, ((1,), (1,)))


def mm_tn(left, right):
    return mm(left, right, ((0,), (0,)))


def normalize(token_rows, norm_gain, norm_shift):
    mean_row = jnp.mean(token_rows, axis=-1, keepdims=True)
    centred = token_rows - mean_row
    inv_std = lax.rsqrt(jnp.mean(centred * centred, axis=-1, keepdims=True) + eps_norm)
    scaled = centred * inv_std
    return (scaled * norm_gain + norm_shift, scaled, inv_std)


def normalize_back(grad_out, scaled, inv_std, norm_gain):
    grad_scaled = grad_out * norm_gain
    centre_part = jnp.mean(grad_scaled, axis=-1, keepdims=True)
    along_part = scaled * jnp.mean(grad_scaled * scaled, axis=-1, keepdims=True)
    grad_in = inv_std * (grad_scaled - centre_part - along_part)
    return (grad_in, jnp.sum(grad_out * scaled, axis=0), jnp.sum(grad_out, axis=0))


def adam_step(weight, first_moment, second_moment, gradient, rate, decay, step_number):
    first_new = beta_one * first_moment + (1.0 - beta_one) * gradient
    second_new = beta_two * second_moment + (1.0 - beta_two) * gradient * gradient
    corr_one = 1.0 - jnp.power(beta_one, step_number)
    corr_two = 1.0 - jnp.power(beta_two, step_number)
    update = first_new / corr_one / (jnp.sqrt(second_new / corr_two) + eps_adam)
    return (weight - rate * (update + decay * weight), first_new, second_new)


def attend_kernel(heads, block, bias_ref, q_ref, kv_ref, ctx_ref, lse_ref):
    width = heads * HEAD_DIM
    bias = bias_ref[...]
    for h in range(heads):
        lo = h * HEAD_DIM
        q = q_ref[0, :, lo : lo + HEAD_DIM] * jnp.asarray(HEAD_DIM**-0.5, BF16)
        k = kv_ref[0, :, width + lo : width + lo + HEAD_DIM]
        v = kv_ref[0, :, 2 * width + lo : 2 * width + lo + HEAD_DIM]
        s = mm_nt(q, k) + bias
        top = jnp.max(s, axis=-1, keepdims=True)
        e = jnp.exp(s - top)
        total = jnp.sum(e, axis=-1, keepdims=True)
        ctx = mm_nn(e.astype(BF16), v) / total
        ctx_ref[0, :, lo : lo + HEAD_DIM] = ctx.astype(BF16)
        lse_ref[0, :, h : h + 1] = top + jnp.log(total)


def attend(qkv, bias, heads):
    chunks, seq, _ = qkv.shape
    block = min(256, seq)
    width = heads * HEAD_DIM
    return pl.pallas_call(
        functools.partial(attend_kernel, heads, block),
        grid=(chunks, seq // block),
        in_specs=[
            pl.BlockSpec((1, seq), lambda i, j: (0, 0)),
            pl.BlockSpec((1, block, 3 * width), lambda i, j: (i, j, 0)),
            pl.BlockSpec((1, seq, 3 * width), lambda i, j: (i, 0, 0)),
        ],
        out_specs=[
            pl.BlockSpec((1, block, width), lambda i, j: (i, j, 0)),
            pl.BlockSpec((1, block, 8), lambda i, j: (i, j, 0)),
        ],
        out_shape=[
            jax.ShapeDtypeStruct((chunks, seq, width), BF16),
            jax.ShapeDtypeStruct((chunks, seq, 8), F32),
        ],
        cost_estimate=pl.CostEstimate(
            flops=16 * chunks * heads * seq * seq * HEAD_DIM,
            bytes_accessed=8 * chunks * seq * width,
            transcendentals=chunks * heads * seq * seq,
        ),
        name="attend",
    )(bias, qkv, qkv)


def attend_back_kernel(heads, bias_ref, q_ref, g_ref, o_ref, lse_ref, kv_ref, gq_ref, gkv_ref, acc_ref):
    width = heads * HEAD_DIM
    step = pl.program_id(1)
    scale = HEAD_DIM**-0.5

    @pl.when(step == 0)
    def _():
        acc_ref[...] = jnp.zeros_like(acc_ref)

    bias = bias_ref[...]
    lse_rows = lse_ref[0].T
    for h in range(heads):
        lo = h * HEAD_DIM
        q = q_ref[0, :, lo : lo + HEAD_DIM] * jnp.asarray(scale, BF16)
        g = g_ref[0, :, lo : lo + HEAD_DIM]
        o = o_ref[0, :, lo : lo + HEAD_DIM]
        k = kv_ref[0, :, width + lo : width + lo + HEAD_DIM]
        v = kv_ref[0, :, 2 * width + lo : 2 * width + lo + HEAD_DIM]
        delta = jnp.sum(g.astype(F32) * o.astype(F32), axis=-1, keepdims=True).T
        st = mm_nt(k, q) + bias
        pt = jnp.exp(st - lse_rows[h : h + 1, :])
        gpt = mm_nt(v, g)
        gst = (pt * (gpt - delta)).astype(BF16)
        acc_ref[:, width + lo : width + lo + HEAD_DIM] += mm_nn(pt.astype(BF16), g)
        acc_ref[:, lo : lo + HEAD_DIM] += mm_nn(gst, q)
        gq_ref[0, :, lo : lo + HEAD_DIM] = (mm_tn(gst, k) * scale).astype(BF16)

    @pl.when(step == pl.num_programs(1) - 1)
    def _():
        gkv_ref[0] = acc_ref[...].astype(BF16)


def attend_back(qkv, grad_ctx, ctx, lse, bias_col, heads):
    chunks, seq, _ = qkv.shape
    block = min(256, seq)
    width = heads * HEAD_DIM
    return pl.pallas_call(
        functools.partial(attend_back_kernel, heads),
        grid=(chunks, seq // block),
        in_specs=[
            pl.BlockSpec((seq, 1), lambda i, j: (0, 0)),
            pl.BlockSpec((1, block, 3 * width), lambda i, j: (i, j, 0)),
            pl.BlockSpec((1, block, width), lambda i, j: (i, j, 0)),
            pl.BlockSpec((1, block, width), lambda i, j: (i, j, 0)),
            pl.BlockSpec((1, block, 8), lambda i, j: (i, j, 0)),
            pl.BlockSpec((1, seq, 3 * width), lambda i, j: (i, 0, 0)),
        ],
        out_specs=[
            pl.BlockSpec((1, block, width), lambda i, j: (i, j, 0)),
            pl.BlockSpec((1, seq, 2 * width), lambda i, j: (i, 0, 0)),
        ],
        out_shape=[
            jax.ShapeDtypeStruct((chunks, seq, width), BF16),
            jax.ShapeDtypeStruct((chunks, seq, 2 * width), BF16),
        ],
        scratch_shapes=[pltpu.VMEM((seq, 2 * width), F32)],
        cost_estimate=pl.CostEstimate(
            flops=40 * chunks * heads * seq * seq * HEAD_DIM,
            bytes_accessed=20 * chunks * seq * width,
            transcendentals=chunks * heads * seq * seq,
        ),
        name="attend_back",
    )(bias_col, qkv, grad_ctx, ctx, lse, qkv)


class Routes:
    def __init__(self, dp_size, mp_size):
        self.dp, self.mp = dp_size, mp_size
        self.bits = (dp_size // 2).bit_length() - 1
        self.mp_bits = mp_size.bit_length() - 1

    def _pairs(self, target):
        pairs = []
        for d in range(self.dp):
            for m in range(self.mp):
                dest = target(d // 2, d % 2, m)
                pairs.append((d * self.mp + m, (dest[0] * 2 + dest[1]) * self.mp + dest[2]))
        return pairs

    def send(self, value, target, back=False):
        pairs = self._pairs(target)
        if back:
            pairs = [(b, a) for a, b in pairs]
        return lax.ppermute(value, AXES, pairs)

    def partner(self, value):
        return self.send(value, lambda p, c, m: (p, 1 - c, m))

    def pair_bit(self, value, bit):
        return self.send(value, lambda p, c, m: (p ^ (1 << bit), c, m))

    def mp_bit(self, value, bit):
        return self.send(value, lambda p, c, m: (p, c, m ^ (1 << bit)))

    def cell(self, value, k, back=False):
        return self.send(value, lambda p, c, m: (p, m // 2, 2 * c + ((m % 2) ^ k)), back)

    def shard(self, value, k, back=False):
        return self.send(value, lambda p, c, m: (p, m // 2, m ^ k ^ (2 * c)), back)


def gather_shards(routes, shard):
    got = [routes.shard(shard, k) for k in range(4)]
    chunks = []
    for half in range(2):
        own = jnp.stack([got[half], got[half + 2]])
        order = range(routes.bits) if half else reversed(range(routes.bits))
        pieces = {0: own}
        for bit in order:
            if routes.bits <= 2:
                pieces.update({r | (1 << bit): routes.pair_bit(v, bit) for r, v in list(pieces.items())})
            else:
                keys = sorted(pieces)
                cat = routes.pair_bit(jnp.stack([pieces[r] for r in keys]), bit)
                pieces.update({r | (1 << bit): cat[i] for i, r in enumerate(keys)})
        chunks.append(pieces)
    return chunks


def assemble(pieces, mask):
    count = len(pieces)
    _, rows, width = pieces[0].shape
    full = jnp.zeros((count * 2 * rows, width), pieces[0].dtype)
    for r in range(count):
        for e in range(2):
            full = lax.dynamic_update_slice(full, pieces[r][e], ((((2 * r + e) ^ mask)) * rows, 0))
    return full


def scatter_grads(routes, chunks, mask):
    partial = []
    for half in range(2):
        full = chunks[half]
        count = 1 << routes.bits
        rows = full.shape[0] // (2 * count)
        blocks = full.reshape(2 * count, rows, full.shape[1])
        pieces = {
            r: jnp.stack([lax.dynamic_index_in_dim(blocks, (2 * r + e) ^ mask, 0, keepdims=False) for e in range(2)])
            for r in range(count)
        }
        order = range(routes.bits) if not half else reversed(range(routes.bits))
        for bit in order:
            keys = sorted(r for r in pieces if not r & (1 << bit))
            sent = routes.pair_bit(jnp.stack([pieces[r | (1 << bit)] for r in keys]), bit)
            pieces = {
                r: (pieces[r].astype(F32) + sent[i].astype(F32)).astype(BF16) for i, r in enumerate(keys)
            }
        partial.append(pieces[0])
    total = None
    for k in range(4):
        got = routes.shard(partial[k % 2][k // 2], k, back=True).astype(F32)
        total = got if total is None else total + got
    return total


MESH = pl.DeviceIdType.MESH


class Here:
    def __init__(self):
        self.d, self.m = lax.axis_index("dp"), lax.axis_index("mp")
        self.c = self.d % 2
        self.pair = self.d - self.c
        self.x = (self.d // 2) % 2
        self.y = self.d // 4
        self.t = self.m // 2
        self.b = self.m % 2
        self.over_x = {"dp": self.d + 2 - 4 * self.x, "mp": self.m}
        self.over_y = {"dp": self.d + 4 - 8 * self.y, "mp": self.m}
        self.partner = {"dp": self.d + 1 - 2 * self.c, "mp": self.m}
        self.home = self.t == self.c

    def at(self, core, m):
        return {"dp": self.pair + core, "mp": m}


def remote(src, dst, ssem, rsem, dev):
    return pltpu.make_async_remote_copy(
        src_ref=src, dst_ref=dst, send_sem=ssem, recv_sem=rsem, device_id=dev, device_id_type=MESH
    )


def arrived(dst, rsem, dev):
    remote(dst, dst, rsem, rsem, dev).wait_recv()


class Maybe:
    def __init__(self, src, dst, ssem, rsem, dev, own):
        self.args, self.dev, self.ssem, self.own = (src, dst), dev, ssem, own
        self.rsem = rsem

    def far(self):
        return remote(*self.args, self.ssem, self.rsem, self.dev)

    def start(self):
        pl.when(self.own)(lambda: pltpu.make_async_copy(*self.args, self.rsem).start())
        pl.when(jnp.logical_not(self.own))(lambda: self.far().start())

    def wait_send(self):
        pl.when(jnp.logical_not(self.own))(lambda: self.far().wait_send())


def greet(here):
    barrier = pltpu.get_barrier_semaphore()

    def tell(dev):
        pl.semaphore_signal(barrier, inc=1, device_id=dev, device_id_type=MESH)

    for core in range(2):
        for m in range(4):
            other = jnp.logical_or(here.c != core, here.m != m)
            pl.when(other)(functools.partial(tell, here.at(core, m)))
    tell(here.over_x)
    tell(here.over_y)
    pl.semaphore_wait(barrier, 9)


class Gather:
    def __init__(self, here, shard, full, sems, relayed):
        self.relayed = relayed
        (self.send_z, self.got_z, self.send_f, self.send_x, self.send_y, self.got_x, self.got_y, self.send_r, self.got_r) = sems
        self.here, self.shard, self.full = here, shard, full
        self.rows = shard.shape[0]
        self.first = jnp.where(here.m > 2 * here.c, 1, 0)

    @staticmethod
    def scratch():
        dma = pltpu.SemaphoreType.DMA
        return [dma((5,))] + [dma((2, 2))] * 8

    def plane(self, i):
        return (self.first + i) % 2

    def block(self, i, dp):
        return self.full.at[self.plane(i), pl.ds(dp * self.rows, self.rows), :]

    def z_copies(self):
        h = self.here
        dst = self.full.at[h.b, pl.ds(h.d * self.rows, self.rows), :]
        got = self.got_z.at[h.b, h.c]
        if self.relayed:
            far = [(h.m < 3, (h.m + 1) % 4), (h.m > 0, (h.m + 3) % 4)]
        else:
            far = [(h.m != m, m) for m in range(4)]
        copies = [
            (there, remote(self.shard, dst, self.send_z.at[n], got, h.at(h.t, m))) for n, (there, m) in enumerate(far)
        ]
        return Maybe(self.shard, dst, self.send_z.at[4], got, h.at(h.t, h.m), h.home), copies

    def start_near(self):
        self.z_copies()[0].start()

    def start_far(self):
        for there, copy in self.z_copies()[1]:
            pl.when(there)(copy.start)

    def onward(self, i, e):
        h = self.here
        source = 2 * h.c + self.plane(i)
        up = source < h.m
        there = jnp.logical_or(jnp.logical_and(up, h.m < 3), jnp.logical_and(source > h.m, h.m > 0))
        ref = self.block(i, h.pair + e)
        target = (h.m + 3 - 2 * up.astype(jnp.int32)) % 4
        return there, remote(ref, ref, self.send_f.at[i, e], self.got_z.at[self.plane(i), e], h.at(h.c, target))

    def own_copies(self, i, e):
        h = self.here
        ref = self.block(i, h.pair + e)
        return (
            remote(ref, ref, self.send_x.at[i, e], self.got_x.at[i, e], h.over_x),
            remote(ref, ref, self.send_y.at[i, e], self.got_y.at[i, e], h.over_y),
        )

    def spread(self, i):
        h = self.here
        for e in range(2):
            arrived(self.block(i, h.pair + e), self.got_z.at[self.plane(i), e], h.partner)
            if self.relayed:
                there, copy = self.onward(i, e)
                pl.when(there)(copy.start)
            for copy in self.own_copies(i, e):
                copy.start()

    def relay_copy(self, i, e):
        h = self.here
        if i == 0:
            ref, dev = self.block(i, h.over_y["dp"] - h.c + e), h.over_x
        else:
            ref, dev = self.block(i, h.over_x["dp"] - h.c + e), h.over_y
        return remote(ref, ref, self.send_r.at[i, e], self.got_r.at[i, e], dev)

    def relay(self, i):
        h = self.here
        for e in range(2):
            if i == 0:
                arrived(self.block(i, h.over_y["dp"] - h.c + e), self.got_y.at[i, e], h.over_y)
            else:
                arrived(self.block(i, h.over_x["dp"] - h.c + e), self.got_x.at[i, e], h.over_x)
            self.relay_copy(i, e).start()

    def finish(self):
        self.arrive()
        self.sent()

    def arrive(self):
        h = self.here
        diagonal = h.pair + 2 - 4 * h.x + 4 - 8 * h.y
        for i in range(2):
            for e in range(2):
                if i == 0:
                    arrived(self.block(i, h.over_x["dp"] - h.c + e), self.got_x.at[i, e], h.over_x)
                else:
                    arrived(self.block(i, h.over_y["dp"] - h.c + e), self.got_y.at[i, e], h.over_y)
                arrived(self.block(i, diagonal + e), self.got_r.at[i, e], h.over_x)

    def sent(self):
        near, far = self.z_copies()
        near.wait_send()
        for there, copy in far:
            pl.when(there)(copy.wait_send)
        for i in range(2):
            for e in range(2):
                if self.relayed:
                    there, copy = self.onward(i, e)
                    pl.when(there)(copy.wait_send)
                for copy in self.own_copies(i, e):
                    copy.wait_send()
                self.relay_copy(i, e).wait_send()


class ToCell:
    def __init__(self, here, source, rows, send, got):
        self.here, self.source, self.rows, self.send, self.got = here, source, rows, send, got

    def copy(self, s):
        h = self.here
        target = 2 * h.c + s
        own = jnp.logical_and(h.home, h.m == target)
        return Maybe(self.source.at[s], self.rows.at[h.b], self.send.at[s], self.got.at[h.b], h.at(h.t, target), own)

    def start(self):
        for s in range(2):
            self.copy(s).start()

    def wait(self):
        for b in range(2):
            arrived(self.rows.at[b], self.got.at[b], self.here.partner)

    def finish(self):
        for s in range(2):
            self.copy(s).wait_send()


class Norms:
    def __init__(self, here, slot, slots, sems):
        self.here, self.slot, self.slots = here, slot, slots
        self.send_z, self.got_z, self.send, self.got = sems

    @staticmethod
    def scratch():
        dma = pltpu.SemaphoreType.DMA
        return [dma((4,)), dma((4,)), dma((3,)), dma((3,))]

    def span(self, d, count):
        return self.slots.at[pl.ds(d * 4 // count * count, count)]

    def z_copy(self, m):
        h = self.here
        return Maybe(self.slot, self.slots.at[h.d * 4 + h.m], self.send_z.at[m], self.got_z.at[h.m], {"dp": h.d, "mp": m}, h.m == m)

    def copy(self, k):
        h = self.here
        ref = self.span(h.d, 4 << k)
        return remote(ref, ref, self.send.at[k], self.got.at[k], (h.partner, h.over_x, h.over_y)[k])

    def start_z(self):
        for m in range(4):
            self.z_copy(m).start()

    def wait_z(self):
        h = self.here
        for m in range(4):
            arrived(self.slots.at[h.d * 4 + m], self.got_z.at[m], h.partner)

    def start(self, k):
        self.copy(k).start()

    def wait(self, k):
        h = self.here
        dev = (h.partner, h.over_x, h.over_y)[k]
        arrived(self.span(dev["dp"], 4 << k), self.got.at[k], dev)

    def sent(self):
        for m in range(4):
            self.z_copy(m).wait_send()
        for k in range(3):
            self.copy(k).wait_send()


def norm_rows(values, gain, shift):
    mean_row = jnp.mean(values, axis=-1, keepdims=True)
    centred = values - mean_row
    inv_std = lax.rsqrt(jnp.mean(centred * centred, axis=-1, keepdims=True) + eps_norm)
    return centred * inv_std * gain + shift


ANY = pl.BlockSpec(memory_space=pl.ANY)
VMEM = pl.BlockSpec(memory_space=pltpu.VMEM)


def rows_at(start, size):
    return pl.ds(start * size, size)


def exact_gelu_both(u):
    below = 0.5 * (1.0 + lax.erf(u * (0.5**0.5)))
    density = jnp.exp(-0.5 * u * u) * ((2.0 * jnp.pi) ** -0.5)
    return u * below, below + u * density


class Stores:
    def __init__(self, sems):
        self.sems, self.made = sems, []

    def put(self, src, dst):
        copy = pltpu.make_async_copy(src, dst, self.sems.at[len(self.made)])
        copy.start()
        self.made.append((src, dst))

    def finish(self):
        for i, (src, dst) in enumerate(self.made):
            pltpu.make_async_copy(src, dst, self.sems.at[i]).wait()


def attend_rows(bias, qkv_ref, ctx_ref, lse_ref, chunk, start, block, heads):
    width = heads * HEAD_DIM
    spare = qkv_ref.shape[2] - 3 * width
    rows = pl.ds(start, block)
    stats = []
    for h in range(heads):
        lo = spare + h * HEAD_DIM
        q = qkv_ref[chunk, rows, lo : lo + HEAD_DIM] * jnp.asarray(HEAD_DIM**-0.5, BF16)
        k = qkv_ref[chunk, :, width + lo : width + lo + HEAD_DIM]
        v = qkv_ref[chunk, :, 2 * width + lo : 2 * width + lo + HEAD_DIM]
        s = mm_nt(q, k) + bias
        top = jnp.max(s, axis=-1, keepdims=True)
        e = jnp.exp(s - top)
        total = jnp.sum(e, axis=-1, keepdims=True)
        ctx = mm_nn(e.astype(BF16), v) / total
        ctx_ref[chunk, rows, h * HEAD_DIM : (h + 1) * HEAD_DIM] = ctx.astype(BF16)
        stats.append(top + jnp.log(total))
    stats += [jnp.zeros_like(stats[0])] * (8 - heads)
    lse_ref[chunk, :, rows] = jnp.concatenate(stats, axis=1).T


def forward_kernel(heads, *refs):
    (x_ref, gy_ref, shard_a, shard_1, shard_2, slot_ref) = refs[:6]
    (full_a, full_1, full_2, h1_out, qkv_out, ctx_out, lse_out, x_out, x2_out, h2_out, act_out, slope_out, gy_out,
     grad_out, norm_ref, count_ref) = refs[6:22]
    (weight, x_in, gy_in, h1, qkv, ctx, lse, fold_out, fold_in, x2, h2, act, slope, gy, stage, slots) = refs[22:38]
    sems = refs[38:]
    (cell_sems, swap_send, swap_got, load_sem, store_sems, stage_sems) = (
        sems[:4], sems[4], sems[5], sems[6], sems[7], sems[8]
    )
    here = Here()
    half, width = x2.shape
    seq = 2 * half
    quarter = half // 2
    inner = heads * HEAD_DIM
    greet(here)
    per = len(Gather.scratch())
    norms = Norms(here, slot_ref, slots, sems[9 + 3 * per :])
    block_a, block_1, block_2 = (
        Gather(here, shard, full, sems[9 + per * i : 9 + per * (i + 1)], i <= 1)
        for i, (shard, full) in enumerate(((shard_a, full_a), (shard_1, full_1), (shard_2, full_2)))
    )
    cell_x = ToCell(here, x_ref, x_in, cell_sems[0], cell_sems[1])
    cell_g = ToCell(here, gy_ref, gy_in, cell_sems[2], cell_sems[3])
    stores = Stores(store_sems)

    def swap(n, src, dst):
        return remote(src, dst, swap_send.at[n], swap_got.at[n], here.partner)

    def load(full):
        copies = [pltpu.make_async_copy(full.at[b], weight.at[b], load_sem.at[b]) for b in range(2)]
        for copy in copies:
            copy.start()
        for copy in copies:
            copy.wait()

    own, other = pl.ds(0, half), pl.ds(half, half)
    away = jnp.logical_not(here.home)
    norms.start_z()
    block_a.start_far()
    for block in (block_a, block_1, block_2):
        block.start_near()
    block_a.spread(0)
    norms.wait_z()
    norms.start(0)
    block_a.relay(0)
    norms.wait(0)
    norms.start(1)
    cell_x.start()
    block_a.spread(1)
    norms.wait(1)
    norms.start(2)
    block_a.relay(1)
    pl.when(here.home)(lambda: block_1.spread(0))
    block_1.start_far()
    norms.wait(2)
    columns = norm_ref.shape[1] // 32
    for n in range(32):
        norm_ref[:, n * columns : (n + 1) * columns] = slots[n, 0:4, 0:columns]
    lanes = lax.broadcasted_iota(jnp.int32, (1, 128), 1)
    count_row = slots[(here.pair + here.t) * 4 + here.m, 4:5, :]
    count = jnp.sum(jnp.where(lanes == here.b, count_row, 0.0), axis=1, keepdims=True)
    count_ref[...] = jnp.broadcast_to(count, count_ref.shape)
    cell_x.wait()

    step = 128
    per_quarter = quarter // step

    @pl.loop(0, half // step)
    def _(i):
        rows = pl.ds(pl.multiple_of((i % per_quarter) * step, step), step)
        h1[pl.ds(pl.multiple_of(i * step, step), step), :] = norm_rows(
            x_in[i // per_quarter, rows, :].astype(F32), norm_ref[0:1, :], norm_ref[1:2, :]
        ).astype(BF16)

    swap_h1 = swap(0, h1.at[own], h1.at[other])
    swap_h1.start()
    stores.put(x_in, x_out)
    pl.when(away)(lambda: block_1.spread(0))
    block_1.spread(1)
    block_2.start_far()
    block_a.arrive()
    pl.when(here.home)(lambda: block_1.relay(0))
    pl.when(here.home)(lambda: block_2.spread(0))
    load(full_a)
    swap_h1.wait_recv()
    stores.put(h1, h1_out)

    first = 4 * inner - qkv.shape[2]

    @pl.loop(0, 2)
    def _(b):
        for n in range(0, qkv.shape[2], 512):
            qkv[b, :, n : n + 512] = mm_nn(h1[...], weight[b, :, first + n : first + n + 512]).astype(BF16)

    stores.put(qkv, qkv_out)
    bias = key_bias(here, count, lax.broadcasted_iota(jnp.int32, (1, seq), 1), half)
    q_block = 256
    per_chunk = seq // q_block

    @pl.loop(0, 2 * per_chunk)
    def _(i):
        pl.when(jnp.logical_and(i == 0, away))(lambda: block_1.relay(0))
        pl.when(i == 3)(lambda: block_1.relay(1))
        pl.when(jnp.logical_and(i == 4, here.home))(lambda: block_2.relay(0))
        pl.when(jnp.logical_and(i == 5, away))(lambda: block_2.spread(0))
        pl.when(i == 7)(lambda: block_2.spread(1))
        attend_rows(
            bias, qkv, ctx, lse, i // per_chunk, pl.multiple_of((i % per_chunk) * q_block, q_block), q_block, heads
        )

    stores.put(ctx, ctx_out)
    stores.put(lse, lse_out)

    def branch_tile(rows, n):
        cols = pl.ds(pl.multiple_of(n * 256, 256), 256)
        return mm_nt(ctx[0, rows, :], weight[0, cols, 0:inner]) + mm_nt(ctx[1, rows, :], weight[1, cols, 0:inner]), cols

    @pl.loop(0, width // 256)
    def _(n):
        part, cols = branch_tile(other, n)
        fold_out[:, cols] = part.astype(BF16)

    swap_fold = swap(1, fold_out, fold_in)
    swap_fold.start()

    @pl.loop(0, width // 256)
    def _(n):
        part, cols = branch_tile(own, n)
        for b in range(2):
            rows = pl.ds(b * quarter, quarter)
            x2[rows, cols] = x_in[b, :, cols].astype(F32) + part[b * quarter : (b + 1) * quarter]

    swap_fold.wait_recv()

    @pl.loop(0, half // step)
    def _(i):
        rows = pl.ds(pl.multiple_of(i * step, step), step)
        middle = x2[rows, :] + fold_in[rows, :].astype(F32)
        x2[rows, :] = middle
        h2[rows, :] = norm_rows(middle, norm_ref[2:3, :], norm_ref[3:4, :]).astype(BF16)

    swap_h2 = swap(2, h2.at[own], h2.at[other])
    swap_h2.start()
    stores.put(x2, x2_out)
    cell_g.start()
    block_1.arrive()
    load(full_1)
    swap_h2.wait_recv()
    stores.put(h2, h2_out)
    per_unit = width // 256

    @pl.loop(0, 2 * per_unit)
    def _(i):
        pl.when(jnp.logical_and(i == 0, away))(lambda: block_2.relay(0))
        pl.when(i == 5)(lambda: block_2.relay(1))
        b, cols = i // per_unit, pl.ds(pl.multiple_of((i % per_unit) * 256, 256), 256)
        value, grad = exact_gelu_both(mm_nn(h2[...], weight[b, :, cols]))
        act[b, :, cols] = value.astype(BF16)
        slope[b, :, cols] = grad.astype(BF16)

    stores.put(act, act_out)
    stores.put(slope, slope_out)
    cell_g.wait()

    @pl.loop(0, 2)
    def _(b):
        gy[pl.ds(pl.multiple_of(b * quarter, quarter), quarter), :] = gy_in[b]

    swap_gy = swap(3, gy.at[own], gy.at[other])
    swap_gy.start()
    swap_gy.wait_recv()
    stores.put(gy, gy_out)

    def stage_copy(i):
        slot = i % 2
        return pltpu.make_async_copy(
            stage.at[slot], grad_out.at[:, pl.ds(pl.multiple_of(i * 256, 256), 256), :], stage_sems.at[slot]
        )

    @pl.loop(0, width // 256)
    def _(i):
        pl.when(i >= 2)(lambda: stage_copy(i - 2).wait())
        left = gy[:, pl.ds(pl.multiple_of(i * 256, 256), 256)].T
        for b in range(2):
            stage[i % 2, b] = mm_nn(left, act[b]).astype(BF16)
        stage_copy(i).start()

    for i in range(width // 256 - 2, width // 256):
        stage_copy(i).wait()
    block_2.arrive()
    for block in (block_a, block_1, block_2):
        block.sent()
    cell_x.finish()
    cell_g.finish()
    norms.sent()
    for n, (src, dst) in enumerate(((h1.at[own], h1.at[other]), (fold_out, fold_in), (h2.at[own], h2.at[other]), (gy.at[own], gy.at[other]))):
        swap(n, src, dst).wait_send()
    stores.finish()


def key_bias(here, count, index, half):
    position = jnp.where(index < half, here.c * half + index, (1 - here.c) * half + index - half)
    return jnp.where(position.astype(F32) < 1.0 + count, 0.0, masked_score)


def forward(inputs, cotangent, shards, slot, heads, collective):
    cells, quarter, width = inputs.shape
    rows, wide = shards[0].shape
    half, seq, inner = 2 * quarter, 4 * quarter, heads * HEAD_DIM
    part = (3 * inner + 255) // 256 * 256
    dma = pltpu.SemaphoreType.DMA
    full = ((2, 8 * rows, wide), BF16)
    kept = [
        ((seq, width), BF16), ((2, seq, part), BF16), ((2, seq, inner), BF16), ((2, 8, seq), F32),
        ((2, quarter, width), BF16), ((half, width), F32), ((seq, width), BF16), ((2, seq, wide), BF16),
        ((2, seq, wide), BF16), ((seq, width), BF16), ((2, width, wide), BF16),
    ]
    buffers = [
        full, ((2, quarter, width), BF16), ((2, quarter, width), BF16), kept[0], kept[1], kept[2], kept[3],
        ((half, width), BF16), ((half, width), BF16), kept[5], kept[6], kept[7], kept[8], kept[9],
        ((2, 2, 256, wide), BF16), ((32, 8, 128), F32),
    ]
    return pl.pallas_call(
        functools.partial(forward_kernel, heads),
        out_shape=[jax.ShapeDtypeStruct(*s) for s in [full] * 3 + kept + [((4, width), F32), ((8, 128), F32)]],
        in_specs=[VMEM] * 6,
        out_specs=[ANY] * 14 + [VMEM] * 2,
        scratch_shapes=[pltpu.VMEM(*s) for s in buffers]
        + [dma((2,))] * 4 + [dma((4,)), dma((4,)), dma((2,)), dma((10,)), dma((2,))]
        + Gather.scratch() * 3 + Norms.scratch(),
        compiler_params=pltpu.CompilerParams(
            collective_id=collective, has_side_effects=True, vmem_limit_bytes=67043328
        ),
        name="forward",
    )(inputs, cotangent, *shards, slot)


class Reduce:
    def __init__(self, here, grads, bufs, sems):
        self.here, self.grads = here, grads
        self.own, self.one, self.two, self.far, self.last, self.part = bufs
        (self.sem_own, self.send_one, self.got_one, self.send_two, self.got_two, self.send_z, self.got_far, self.got_z) = sems
        self.piece = self.own.shape[2]
        self.before = None
        self.away = jnp.logical_not(here.home)
        self.outer = here.m % 3 == 0

    @staticmethod
    def scratch(rows, width):
        r = rows // 2
        dma = pltpu.SemaphoreType.DMA
        four = pltpu.VMEM((2, 4, r, width), BF16)
        landing = [pltpu.VMEM((2, 2, 4, r, width), BF16), four, four, pltpu.VMEM((3, 2, r, width), BF16)]
        sems = [dma((2, 2, 4)), dma((2, 2, 4)), dma((2, 4)), dma((2, 4)), dma((2, 4)), dma((2, 4)), dma((3, 2))]
        return pltpu.VMEM((2, 2, r, width), BF16), four, landing, sems

    def rows_of(self, role, dp, j):
        return self.grads.at[role, pl.ds(dp * 2 * self.piece + j * self.piece, self.piece), :]

    def pair_at(self, role, n, far):
        h = self.here
        dx, dy = 2 - 4 * h.x, 4 - 8 * h.y
        first, second = (dx, dy) if role == 0 else (dy, dx)
        return h.pair + (first if far else 0) + (second if n == 0 else 0)

    def copy_one(self, role, n, j):
        dev = self.here.over_x if role == 0 else self.here.over_y
        return remote(
            self.rows_of(role, self.pair_at(role, n, True), j), self.one.at[role, n, j],
            self.send_one.at[role, n, j], self.got_one.at[role, n, j], dev,
        )

    def copy_two(self, role, j):
        dev = self.here.over_y if role == 0 else self.here.over_x
        return remote(
            self.one.at[role, 0, j], self.two.at[role, j], self.send_two.at[role, j], self.got_two.at[role, j], dev
        )

    def to_inner(self, role, j):
        h = self.here
        return remote(
            self.part.at[role, j], self.far.at[role, j], self.send_z.at[role, j], self.got_far.at[role, j],
            h.at(h.c, h.m + 1 - 2 * h.b),
        )

    def to_owner(self, role, j):
        h = self.here
        target = 2 * h.c + role
        slot = jnp.where(self.away, 2, (h.m + target) % 2)
        return remote(
            self.part.at[role, j], self.last.at[slot, j % 2], self.send_z.at[role, j], self.got_z.at[slot, j % 2],
            h.at(j // 2, target),
        )

    def mine(self, role, j):
        return jnp.logical_and(self.here.c == j // 2, self.here.m == 2 * self.here.c + role)

    def direct(self, role, j):
        return jnp.logical_and(self.here.home, jnp.logical_not(self.mine(role, j)))

    def start_one(self, j):
        for n in range(2):
            for role in range(2):
                self.copy_one(role, n, j).start()

    def start(self):
        for j in range(3):
            self.start_one(j)
        for role in range(2):
            for n in range(2):
                self.load_piece(role, n, 0).start()

    def load_piece(self, role, n, j):
        return pltpu.make_async_copy(
            self.rows_of(role, self.pair_at(role, n, False), j), self.own.at[role, n], self.sem_own.at[role, n]
        )

    def add_one(self, role, j):
        h = self.here
        for n in range(2):
            self.load_piece(role, n, j).wait()
            arrived(self.one.at[role, n, j], self.got_one.at[role, n, j], h.over_x)
            self.one[role, n, j] = self.own[role, n] + self.one[role, n, j]
            if n == 0:
                self.copy_two(role, j).start()
            if j < 3:
                self.load_piece(role, n, j + 1).start()

    def add_two(self, role, j):
        arrived(self.two.at[role, j], self.got_two.at[role, j], self.here.over_x)
        total = self.one[role, 1, j] + self.two[role, j]
        if self.before is not None:
            self.before.z_sent(role, j)

        @pl.when(self.mine(role, j))
        def _():
            self.last[0, j % 2] = total

        @pl.when(jnp.logical_not(self.mine(role, j)))
        def _():
            self.part[role, j] = total

        pl.when(self.direct(role, j))(lambda: self.to_owner(role, j).start())
        pl.when(jnp.logical_and(self.away, self.outer))(lambda: self.to_inner(role, j).start())

    def pass_on(self, role, j):
        @pl.when(jnp.logical_and(self.away, jnp.logical_not(self.outer)))
        def _():
            arrived(self.far.at[role, j], self.got_far.at[role, j], self.here.partner)
            self.part[role, j] = self.part[role, j] + self.far[role, j]
            self.to_owner(role, j).start()

    def step(self, j):
        for role in range(2):
            if j < 4:
                self.add_one(role, j)
        if j == 0:
            self.start_one(3)
        for role in range(2):
            if 1 <= j <= 4:
                self.add_two(role, j - 1)
        for role in range(2):
            if j >= 2:
                self.pass_on(role, j - 2)

    def z_sent(self, role, j):
        inner = jnp.logical_and(self.away, jnp.logical_not(self.outer))
        pl.when(jnp.logical_or(self.direct(role, j), inner))(lambda: self.to_owner(role, j).wait_send())
        pl.when(jnp.logical_and(self.away, self.outer))(lambda: self.to_inner(role, j).wait_send())

    def finish(self, total, out_ref, sem):
        h = self.here
        for s in range(2):
            pl.when(self.away)(functools.partial(arrived, self.last.at[0, s], self.got_z.at[0, s], h.partner))
            for n in range(1, 3):
                arrived(self.last.at[n, s], self.got_z.at[n, s], h.partner)
            rows = self.last[0, s].astype(F32)
            for n in range(1, 3):
                rows = rows + self.last[n, s].astype(F32)
            total[pl.ds(s * self.piece, self.piece), :] = rows
        copy = pltpu.make_async_copy(total, out_ref, sem)
        copy.start()
        for role in range(2):
            for j in range(4):
                for n in range(2):
                    self.copy_one(role, n, j).wait_send()
                self.copy_two(role, j).wait_send()
        copy.wait()


class FromCell:
    def __init__(self, here, rows, landing, send, got):
        self.here, self.rows, self.landing, self.send, self.got = here, rows, landing, send, got

    def copy(self, b):
        h = self.here
        target = 2 * h.c + b
        own = jnp.logical_and(h.home, h.m == target)
        return Maybe(self.rows.at[b], self.landing.at[h.b], self.send.at[b], self.got.at[h.b], h.at(h.t, target), own)

    def start(self):
        for b in range(2):
            self.copy(b).start()

    def sent(self):
        for b in range(2):
            self.copy(b).wait_send()

    def arrive(self):
        for s in range(2):
            arrived(self.landing.at[s], self.got.at[s], self.here.partner)


def norm_rows_back(values, grad_out, gain):
    mean_row = jnp.mean(values, axis=-1, keepdims=True)
    centred = values - mean_row
    inv_std = lax.rsqrt(jnp.mean(centred * centred, axis=-1, keepdims=True) + eps_norm)
    scaled = centred * inv_std
    grad_scaled = grad_out * gain
    centre_part = jnp.mean(grad_scaled, axis=-1, keepdims=True)
    along_part = scaled * jnp.mean(grad_scaled * scaled, axis=-1, keepdims=True)
    grad_in = inv_std * (grad_scaled - centre_part - along_part)
    return grad_in, jnp.sum(grad_out * scaled, axis=0, keepdims=True), jnp.sum(grad_out, axis=0, keepdims=True)


def attend_rows_back(bias, qkv_ref, gctx_ref, ctx_ref, lse_ref, grad_ref, acc_ref, chunk, start, block, heads):
    width = heads * HEAD_DIM
    spare = -3 * width % 256
    half = acc_ref.shape[0]
    rows = pl.ds(start, block)
    scale = HEAD_DIM**-0.5
    for h in range(heads):
        at = slice(h * HEAD_DIM, (h + 1) * HEAD_DIM)
        lo = spare + h * HEAD_DIM
        q = qkv_ref[chunk, rows, lo : lo + HEAD_DIM] * jnp.asarray(scale, BF16)
        k = qkv_ref[chunk, :, width + lo : width + lo + HEAD_DIM]
        v = qkv_ref[chunk, :, 2 * width + lo : 2 * width + lo + HEAD_DIM]
        g = gctx_ref[chunk, rows, at]
        delta = jnp.sum(g.astype(F32) * ctx_ref[chunk, rows, at].astype(F32), axis=-1, keepdims=True).T
        pt = jnp.exp(mm_nt(k, q) + bias - lse_ref[chunk, h : h + 1, rows])
        gst = (pt * (mm_nt(v, g) - delta)).astype(BF16)
        gk = mm_nn(gst, q)
        gv = mm_nn(pt.astype(BF16), g)
        for n, part in enumerate((gk[:half], gk[half:], gv[:half], gv[half:])):
            acc_ref[:, n * width + h * HEAD_DIM : n * width + (h + 1) * HEAD_DIM] += part
        grad_ref[chunk, rows, lo : lo + HEAD_DIM] = (mm_tn(gst, k) * scale).astype(BF16)


def backward_kernel(heads, *refs):
    (norm_ref, count_ref, full_a, full_1, full_2, h1_in, qkv_in, ctx_in, lse_in, x_src, x2_src, h2_in, act_in, slope_in,
     gy_src, grad_2) = refs[:16]
    (out_ref, gx_ref, sum_a, sum_1, sum_2, norm_out, grad_1, grad_a) = refs[16:24]
    (weight, gy, slope, act, h2, x2, fold_out, fold_in, gctx, ctx, lse, acc, stage, own, part) = refs[24:39]
    landings = [refs[39 + 4 * i : 43 + 4 * i] for i in range(3)]
    sums, sums_in = refs[51:53]
    sems = refs[53:]
    send_rows = stage
    (load_sems, swap_send, swap_got, cell_sems, stage_sems, own_sem, total_sem) = (
        sems[:10], sems[10], sems[11], sems[12:16], sems[16], sems[17], sems[18]
    )
    per = 7
    here = Here()
    half, width = x2.shape
    seq, quarter, inner = 2 * half, half // 2, heads * HEAD_DIM
    part_width = (3 * inner + 255) // 256 * 256
    first = 4 * inner - part_width
    spare = part_width - 3 * inner
    greet(here)
    blocks = [
        Reduce(here, grads, (own, *landings[i], part), (own_sem, *sems[19 + per * i : 19 + per * (i + 1)]))
        for i, grads in enumerate((grad_2, grad_1, grad_a))
    ]
    block_2, block_1, block_a = blocks
    own_rows, other_rows = pl.ds(0, half), pl.ds(half, half)

    def load(n, src, dst):
        return pltpu.make_async_copy(src, dst, load_sems[n])

    copies = {
        "w2": load(0, full_2, weight), "gy": load(1, gy_src, gy), "slope": load(2, slope_in, slope),
        "act": load(3, act_in, act), "h2": load(4, h2_in, h2), "x2": load(5, x2_src, x2), "ctx": load(6, ctx_in, ctx),
        "lse": load(7, lse_in, lse),
    }
    block_2.start()
    for copy in copies.values():
        copy.start()

    def fetch(src, dst):
        copy = load(9, src, dst)
        copy.start()
        return copy

    def swap(n, src, dst):
        return remote(src, dst, swap_send.at[n], swap_got.at[n], here.partner)

    def tile(n):
        return pl.ds(pl.multiple_of(n * 256, 256), 256)

    tiles = width // 256
    per_unit = width // 256

    copies["w2"].wait()
    copies["act"].wait()

    @pl.loop(0, tiles)
    def _(n):
        cols = tile(n)
        fold_out[:, cols] = (
            mm_nt(act[0, other_rows, :], weight[0, cols, :]) + mm_nt(act[1, other_rows, :], weight[1, cols, :])
        ).astype(BF16)

    swaps = [(fold_out, fold_in.at[0]), (fold_out, fold_in.at[1]), (h2.at[own_rows], h2.at[other_rows]), (fold_out, fold_in.at[0])]
    swap(0, *swaps[0]).start()

    for name in ("gy", "slope"):
        copies[name].wait()

    @pl.loop(0, 2 * per_unit)
    def _(i):
        pl.when(i == 4)(lambda: block_2.step(0))
        b, cols = i // per_unit, tile(i % per_unit)
        grad = mm_nn(gy[...], weight[b, :, cols])
        slope[b, :, cols] = (grad * slope[b, :, cols].astype(F32)).astype(BF16)

    block_2.step(1)
    copies["h2"].wait()

    def stage_copy(grads, i, b):
        return pltpu.make_async_copy(stage.at[b], grads.at[b, tile(i), :], stage_sems.at[b])

    @pl.loop(0, tiles)
    def _(i):
        left = h2[:, tile(i)].T
        for b in range(2):
            pl.when(i >= 1)(lambda: stage_copy(grad_1, i - 1, b).wait())
            stage[b] = mm_nn(left, slope[b]).astype(BF16)
            stage_copy(grad_1, i, b).start()
        pl.when(i == 1)(lambda: block_2.step(2))

    for b in range(2):
        stage_copy(grad_1, tiles - 1, b).wait()
    block_2.step(3)
    block_1.start()
    copies["x2"].wait()
    swap(0, *swaps[0]).wait_recv()

    @pl.loop(0, tiles)
    def _(n):
        cols = tile(n)
        mine = mm_nt(act[0, own_rows, :], weight[0, cols, :]) + mm_nt(act[1, own_rows, :], weight[1, cols, :])
        mine = (mine + x2[:, cols] + fold_in[0, :, cols].astype(F32)).astype(BF16)
        for b in range(2):
            send_rows[b, :, cols] = mine[b * quarter : (b + 1) * quarter]

    cell_out = FromCell(here, send_rows, out_ref, cell_sems[0], cell_sems[1])
    cell_out.start()
    fetch(full_1, weight).wait()
    fetched = fetch(qkv_in, act.at[:, :, 0:part_width])
    swap(0, *swaps[0]).wait_send()

    @pl.loop(0, tiles)
    def _(n):
        cols = tile(n)
        fold_out[:, cols] = (
            mm_nt(slope[0, other_rows, :], weight[0, cols, :]) + mm_nt(slope[1, other_rows, :], weight[1, cols, :])
        ).astype(BF16)

    swap(1, *swaps[1]).start()

    @pl.loop(0, tiles)
    def _(n):
        cols = tile(n)
        acc[:, cols] = mm_nt(slope[0, own_rows, :], weight[0, cols, :]) + mm_nt(slope[1, own_rows, :], weight[1, cols, :])

    fetched.wait()
    fetched = fetch(full_a, weight)
    swap(1, *swaps[1]).wait_recv()
    step = 128
    sums[0] = jnp.zeros(sums.shape[1:], F32)

    @pl.loop(0, half // step)
    def _(i):
        rows = pl.ds(pl.multiple_of(i * step, step), step)
        grad_in, gain_sum, shift_sum = norm_rows_back(
            x2[rows, :], acc[rows, :] + fold_in[1, rows, :].astype(F32), norm_ref[2:3, :]
        )
        sums[0, 2:3, :] += gain_sum
        sums[0, 3:4, :] += shift_sum
        grad_in = gy[rows, :].astype(F32) + grad_in
        x2[rows, :] = grad_in
        h2[rows, :] = grad_in.astype(BF16)

    swap(2, *swaps[2]).start()
    fetched.wait()
    fetched = fetch(h1_in, gy)
    block_2.step(4)
    block_1.before, block_a.before = block_2, block_1
    copies["ctx"].wait()
    copies["lse"].wait()
    swap(2, *swaps[2]).wait_recv()

    for b in range(2):
        gctx[b] = mm_nn(h2[...], weight[b, :, 0:inner]).astype(BF16)
        slope[b, :, 0:spare] = jnp.zeros((seq, spare), BF16)
    bias = key_bias(here, count_ref[0:1, 0:1], lax.broadcasted_iota(jnp.int32, (seq, 1), 0), half)
    q_block = 256
    per_chunk = seq // q_block

    @pl.loop(0, 2 * per_chunk)
    def _(i):
        b, j = i // per_chunk, i % per_chunk

        @pl.when(j == 0)
        def _():
            acc[...] = jnp.zeros_like(acc)

        attend_rows_back(
            bias, act, gctx, ctx, lse, slope, acc, b, pl.multiple_of(j * q_block, q_block), q_block, heads
        )

        @pl.when(j == per_chunk - 1)
        def _():
            for n in range(4):
                lo = spare + (1 + n // 2) * inner
                slope[b, pl.ds((n % 2) * half, half), lo : lo + inner] = acc[:, n * inner : (n + 1) * inner].astype(BF16)

        pl.when(i == 0)(lambda: block_1.step(0))
        pl.when(i == 1)(lambda: block_2.step(5))
        pl.when(i == 2)(lambda: block_1.step(1))
        pl.when(i == 4)(lambda: block_1.step(2))
        pl.when(i == 6)(lambda: block_1.step(3))

    fetched.wait()

    cell_out.sent()
    cell_out.arrive()

    @pl.loop(0, tiles)
    def _(i):
        left = gy[:, tile(i)].T
        left_out = h2[:, tile(i)].T
        for b in range(2):
            pl.when(i >= 1)(lambda: stage_copy(grad_a, i - 1, b).wait())
            stage[b, :, first:] = mm_nn(left, slope[b, :, 0:part_width]).astype(BF16)
            stage[b, :, 0:inner] = mm_nn(left_out, ctx[b]).astype(BF16)
            stage_copy(grad_a, i, b).start()

    for b in range(2):
        stage_copy(grad_a, tiles - 1, b).wait()
    fetched = fetch(x_src, stage)
    block_a.start()
    block_1.step(4)
    total = acc.at[0 : sum_2.shape[0], :]
    swap(1, *swaps[1]).wait_send()

    @pl.loop(0, tiles)
    def _(n):
        cols = tile(n)
        fold_out[:, cols] = sum(
            mm_nt(slope[b, other_rows, 0:part_width], weight[b, cols, first:]) for b in range(2)
        ).astype(BF16)

    swap(3, *swaps[3]).start()
    block_1.step(5)

    @pl.loop(0, tiles)
    def _(n):
        cols = tile(n)
        acc[:, cols] = sum(mm_nt(slope[b, own_rows, 0:part_width], weight[b, cols, first:]) for b in range(2))

    fetched.wait()
    block_a.step(0)
    swap(3, *swaps[3]).wait_recv()
    per_quarter = quarter // step

    @pl.loop(0, half // step)
    def _(i):
        b, inside = i // per_quarter, pl.ds(pl.multiple_of((i % per_quarter) * step, step), step)
        rows = pl.ds(pl.multiple_of(i * step, step), step)
        grad_in, gain_sum, shift_sum = norm_rows_back(
            stage[b, inside, :].astype(F32), acc[rows, :] + fold_in[0, rows, :].astype(F32), norm_ref[0:1, :]
        )
        sums[0, 0:1, :] += gain_sum
        sums[0, 1:2, :] += shift_sum
        send_rows[b, inside, :] = (x2[rows, :] + grad_in).astype(BF16)

    cell_gx = FromCell(here, send_rows, gx_ref, cell_sems[2], cell_sems[3])
    cell_gx.start()
    peers = (
        here.partner, here.over_x, here.over_y, {"dp": here.d, "mp": here.m + 1 - 2 * here.b},
        {"dp": here.d, "mp": here.m + 2 - 4 * here.t},
    )
    sum_send, sum_got = sems[-2:]

    def share(k):
        return remote(sums.at[k], sums_in.at[k], sum_send.at[k], sum_got.at[k], peers[k])

    def add_sums(k):
        share(k).wait_recv()
        sums[k + 1] = sums[k] + sums_in[k]
        if k < 4:
            share(k + 1).start()

    share(0).start()
    block_a.step(1)
    add_sums(0)
    block_2.finish(total, sum_2, total_sem)
    block_a.step(2)
    add_sums(1)
    block_a.step(3)
    add_sums(2)
    block_1.finish(total, sum_1, total_sem)
    block_a.step(4)
    add_sums(3)
    block_a.step(5)
    add_sums(4)
    norm_out[...] = sums[5]
    for k in range(5):
        share(k).wait_send()
    cell_gx.arrive()
    block_a.finish(total, sum_a, total_sem)
    for role in range(2):
        for j in range(4):
            block_a.z_sent(role, j)
    cell_gx.sent()
    for n in (2, 3):
        swap(n, *swaps[n]).wait_send()


def backward(kept, heads, collective):
    kept, (norms, count) = kept[:14], kept[14:]
    (full_a, full_1, full_2, h1, qkv, ctx, lse, x_in, x2, h2, act, slope, gy, grad_2) = kept
    half, width = x2.shape
    quarter, seq = half // 2, 2 * half
    wide = act.shape[2]
    rows = width // 8
    inner = heads * HEAD_DIM
    dma = pltpu.SemaphoreType.DMA
    buffers = [
        (full_a.shape, BF16), (gy.shape, BF16), (slope.shape, BF16), (act.shape, BF16), (h2.shape, BF16), (x2.shape, F32),
        ((half, width), BF16), ((2, half, width), BF16), (ctx.shape, BF16), (ctx.shape, BF16), (lse.shape, F32),
        ((half, width), F32), (x_in.shape, BF16),
    ]
    own, part, landing, reduce_sems = Reduce.scratch(rows, wide)
    return pl.pallas_call(
        functools.partial(backward_kernel, heads),
        out_shape=[jax.ShapeDtypeStruct(x_in.shape, BF16)] * 2
        + [jax.ShapeDtypeStruct((rows, wide), F32)] * 3
        + [jax.ShapeDtypeStruct((4, width), F32)]
        + [jax.ShapeDtypeStruct(grad_2.shape, BF16)] * 2,
        in_specs=[VMEM] * 2 + [ANY] * 14,
        out_specs=[ANY] * 5 + [VMEM] + [ANY] * 2,
        scratch_shapes=[pltpu.VMEM(*s) for s in buffers]
        + [own, part] + landing * 3
        + [pltpu.VMEM((6, 4, width), F32), pltpu.VMEM((5, 4, width), F32)]
        + [dma] * 10 + [dma((4,)), dma((4,))] + [dma((2,))] * 4 + [dma((2,)), dma((2, 2)), dma]
        + reduce_sems * 3 + [dma((5,))] * 2,
        compiler_params=pltpu.CompilerParams(
            collective_id=collective, has_side_effects=True, vmem_limit_bytes=67043328
        ),
        name="backward",
    )(norms, count, *kept)


def gather_norms(routes, norm_params, d, m):
    cur = norm_params
    for bit in range(routes.mp_bits):
        got = routes.mp_bit(cur, bit)
        high = ((m >> bit) & 1) == 1
        cur = jnp.where(high, jnp.concatenate([got, cur], 1), jnp.concatenate([cur, got], 1))
    for bit in range(routes.bits + 1):
        got = routes.partner(cur) if bit == 0 else routes.pair_bit(cur, bit - 1)
        high = ((d >> bit) & 1) == 1
        cur = jnp.where(high, jnp.concatenate([got, cur], 1), jnp.concatenate([cur, got], 1))
    return cur


def scatter_norms(routes, grads, d, m):
    cur = grads
    for bit in reversed(range(routes.bits + 1)):
        low, up = jnp.split(cur, 2, axis=1)
        high = ((d >> bit) & 1) == 1
        give = jnp.where(high, low, up)
        got = routes.partner(give) if bit == 0 else routes.pair_bit(give, bit - 1)
        cur = jnp.where(high, up, low) + got
    for bit in reversed(range(routes.mp_bits)):
        low, up = jnp.split(cur, 2, axis=1)
        high = ((m >> bit) & 1) == 1
        cur = jnp.where(high, up, low) + routes.mp_bit(jnp.where(high, low, up), bit)
    return cur


def update(
    outputs, input_grad, norm_sum, attend_sum, expand_sum, reduce_sum, step_count, norm_params, norm_first, norm_second,
    attend_weight, attend_first, attend_second, output_weight, output_first, output_second,
    expand_weight, expand_first, expand_second, reduce_weight, reduce_first, reduce_second,
):
    width = attend_weight.shape[2]
    step_number = step_count[0].astype(F32)
    norm_new = adam_step(norm_params, norm_first, norm_second, norm_sum, norm_rate, 0.0, step_number)
    attend_reduced = jnp.stack([attend_sum[:, i * width : (i + 1) * width] for i in range(1, 4)])
    attend_new = adam_step(
        attend_weight, attend_first, attend_second, attend_reduced, 2.0 * D ** (-0.5), decay_rate, step_number
    )
    output_new = adam_step(
        output_weight, output_first, output_second, attend_sum[:, :width].T,
        2.0 * (2 * D // SEQ) ** (-0.5), decay_rate, step_number,
    )
    expand_new = adam_step(
        expand_weight, expand_first, expand_second, expand_sum, 2.0 * D ** (-0.5), decay_rate, step_number
    )
    reduce_new = adam_step(
        reduce_weight, reduce_first, reduce_second, reduce_sum.T, 2.0 * FF ** (-0.5), decay_rate, step_number
    )
    return (
        outputs, input_grad,
        norm_new[0], norm_new[1], norm_new[2][0:2], norm_new[2][2:4],
        *attend_new, *output_new, *expand_new, *reduce_new,
    )


def per_device_plain(
    inputs, cotangent, gene_counts, step_count, norm_params, norm_first, norm_second,
    attend_weight, attend_first, attend_second, output_weight, output_first, output_second,
    expand_weight, expand_first, expand_second, reduce_weight, reduce_first, reduce_second,
):
    routes = Routes(lax.axis_size("dp"), lax.axis_size("mp"))
    d, m = lax.axis_index("dp"), lax.axis_index("mp")
    c = d % 2
    cells, quarter, _ = inputs.shape
    assert routes.mp == 4 and 2 * cells == routes.mp and routes.dp % 2 == 0
    half = 2 * quarter
    seq = 2 * half
    heads = attend_weight.shape[2] // HEAD_DIM
    width = heads * HEAD_DIM
    m_low, m_high = m % 2, m // 2
    mask = 2 * (d // 2) + ((c + m_high) % 2)

    norm_full = gather_norms(routes, norm_params, d, m)

    def to_cell(values):
        got = [
            routes.cell(lax.dynamic_index_in_dim(values, (m_low + k) % 2, 0, keepdims=False), k) for k in range(2)
        ]
        return jnp.concatenate(got, 0)

    def from_cell(rows):
        rows = rows.astype(BF16)
        got = [routes.cell(rows[k * quarter : (k + 1) * quarter], k, back=True) for k in range(2)]
        flip = m_low == 1
        return jnp.stack([jnp.where(flip, got[1], got[0]), jnp.where(flip, got[0], got[1])]).astype(F32)

    attend_shard = jnp.concatenate(
        [output_weight.T, attend_weight[0], attend_weight[1], attend_weight[2]], axis=1
    ).astype(BF16)
    expand_shard = expand_weight.astype(BF16)
    reduce_shard = reduce_weight.T.astype(BF16)

    x_mine = to_cell(inputs).astype(F32)
    attend_w = [assemble(pieces, mask) for pieces in gather_shards(routes, attend_shard)]
    expand_w = [assemble(pieces, mask) for pieces in gather_shards(routes, expand_shard)]
    reduce_w = [assemble(pieces, mask) for pieces in gather_shards(routes, reduce_shard)]
    gy_mine = to_cell(cotangent)

    other_counts = routes.partner(gene_counts)
    mine = jnp.where(m_high == c, gene_counts, other_counts)
    count = jnp.where(m_low == 1, mine[1], mine[0])
    inside = jnp.arange(quarter)
    first = m_low
    positions = jnp.concatenate(
        [h * half + b * quarter + inside for h, b in ((c, first), (c, 1 - first), (1 - c, first), (1 - c, 1 - first))]
    )
    bias = jnp.where(positions < 1 + count, 0.0, masked_score).astype(F32)

    def both(rows):
        return jnp.concatenate([rows, routes.partner(rows)], 0)

    def fold(partial):
        return partial[:half] + routes.partner(partial[half:].astype(BF16)).astype(F32)

    normed, scaled_one, inv_one = normalize(x_mine, norm_full[0], norm_full[1])
    h1 = both(normed.astype(BF16))
    qkv = jnp.stack([mm_nn(h1, w[:, width:]).astype(BF16) for w in attend_w])
    ctx, lse = attend(qkv, bias[None, :], heads)
    branch = mm_nt(ctx[0], attend_w[0][:, :width]) + mm_nt(ctx[1], attend_w[1][:, :width])
    x2 = x_mine + fold(branch)
    normed, scaled_two, inv_two = normalize(x2, norm_full[2], norm_full[3])
    h2 = both(normed.astype(BF16))
    hidden = [mm_nn(h2, w) for w in expand_w]
    active = [exact_gelu(u).astype(BF16) for u in hidden]
    branch = mm_nt(active[0], reduce_w[0]) + mm_nt(active[1], reduce_w[1])
    outputs = from_cell(x2 + fold(branch))

    gy = both(gy_mine)
    reduce_grad = [mm_tn(gy, a).astype(BF16) for a in active]
    grad_hidden = [
        jax.vjp(exact_gelu, u)[1](mm_nn(gy, w))[0].astype(BF16) for u, w in zip(hidden, reduce_w)
    ]
    expand_grad = [mm_tn(h2, g).astype(BF16) for g in grad_hidden]
    gh2 = fold(mm_nt(grad_hidden[0], expand_w[0]) + mm_nt(grad_hidden[1], expand_w[1]))
    grad_in, gain_two, shift_two = normalize_back(gh2, scaled_two, inv_two, norm_full[2])
    gx2 = gy_mine.astype(F32) + grad_in
    gb = both(gx2.astype(BF16))
    grad_ctx = jnp.stack([mm_nn(gb, w[:, :width]).astype(BF16) for w in attend_w])
    gq, gkv = attend_back(qkv, grad_ctx, ctx, lse, bias[:, None], heads)
    attend_grad = [
        jnp.concatenate(
            [mm_tn(gb, ctx[i]), mm_tn(h1, gq[i]), mm_tn(h1, gkv[i])], axis=1
        ).astype(BF16)
        for i in range(2)
    ]
    gh1 = fold(
        sum(
            mm_nt(gq[i], attend_w[i][:, width : 2 * width]) + mm_nt(gkv[i], attend_w[i][:, 2 * width :])
            for i in range(2)
        )
    )
    grad_in, gain_one, shift_one = normalize_back(gh1, scaled_one, inv_one, norm_full[0])
    input_grad = from_cell(gx2 + grad_in)

    reduce_sum = scatter_grads(routes, reduce_grad, mask)
    expand_sum = scatter_grads(routes, expand_grad, mask)
    attend_sum = scatter_grads(routes, attend_grad, mask)
    norm_sum = scatter_norms(routes, jnp.stack([gain_one, shift_one, gain_two, shift_two]), d, m)

    return update(
        outputs, input_grad, norm_sum, attend_sum, expand_sum, reduce_sum, step_count, norm_params, norm_first,
        norm_second, attend_weight, attend_first, attend_second, output_weight, output_first, output_second,
        expand_weight, expand_first, expand_second, reduce_weight, reduce_first, reduce_second,
    )


def per_device(
    inputs, cotangent, gene_counts, step_count, norm_params, norm_first, norm_second,
    attend_weight, attend_first, attend_second, output_weight, output_first, output_second,
    expand_weight, expand_first, expand_second, reduce_weight, reduce_first, reduce_second,
):
    d, m, mp_size = lax.axis_index("dp"), lax.axis_index("mp"), lax.axis_size("mp")
    cells = inputs.shape[0]
    assert mp_size == 4 and 2 * cells == mp_size and lax.axis_size("dp") == 8
    heads = attend_weight.shape[2] // HEAD_DIM
    shards = (
        jnp.concatenate([output_weight.T, attend_weight[0], attend_weight[1], attend_weight[2]], axis=1).astype(BF16),
        expand_weight.astype(BF16),
        reduce_weight.T.astype(BF16),
    )
    slot = jnp.zeros((8, 128), F32)
    slot = slot.at[0:4, 0 : norm_params.shape[1]].set(norm_params).at[4, 0:cells].set(gene_counts.astype(F32))
    kept = forward(inputs, cotangent, shards, slot, heads, 1)
    outputs, input_grad, attend_sum, expand_sum, reduce_sum, norm_part, _, _ = backward(kept, heads, 2)
    outputs, input_grad = outputs.astype(F32), input_grad.astype(F32)
    columns = norm_params.shape[1]
    norm_sum = lax.dynamic_slice(norm_part, (0, (d * mp_size + m) * columns), (4, columns))
    return update(
        outputs, input_grad, norm_sum, attend_sum, expand_sum, reduce_sum, step_count, norm_params, norm_first,
        norm_second, attend_weight, attend_first, attend_second, output_weight, output_first, output_second,
        expand_weight, expand_first, expand_second, reduce_weight, reduce_first, reduce_second,
    )


def solution(mesh):
    norms = P(None, ("dp", "mp"))
    attend_spec, col, row = P(None, "dp", "mp"), P("mp", "dp"), P("dp", "mp")
    tokens = P("dp", "mp", None)
    return jax.shard_map(
        per_device if mesh.shape["dp"] == 8 else per_device_plain,
        mesh=mesh,
        in_specs=(tokens, tokens, P("dp"), P(), norms, norms, norms)
        + (attend_spec,) * 3 + (col,) * 3 + (row,) * 3 + (col,) * 3,
        out_specs=(tokens, tokens, norms, norms, norms, norms)
        + (attend_spec,) * 3 + (col,) * 3 + (row,) * 3 + (col,) * 3,
        check_vma=False,
    )
```

```python
import functools

import jax
import jax.numpy as jnp
from jax import lax
from jax.experimental import pallas as pl
from jax.experimental.pallas import tpu as pltpu
from jax.sharding import PartitionSpec as P

D = 1280
HEAD_DIM = 64
FF = 5120
SEQ = 1024

eps_norm = 1e-05
masked_score = -1e30
beta_one = 0.9
beta_two = 0.95
eps_adam = 1e-08
decay_rate = 0.1
norm_rate = 0.6

F32 = jnp.float32
BF16 = jnp.bfloat16
AXES = ("dp", "mp")


def exact_gelu(values):
    return jax.nn.gelu(values, approximate=False)


def mm(left, right, dims):
    return lax.dot_general(left, right, (dims, ((), ())), preferred_element_type=F32)


def mm_nn(left, right):
    return mm(left, right, ((1,), (0,)))


def mm_nt(left, right):
    return mm(left, right, ((1,), (1,)))


def mm_tn(left, right):
    return mm(left, right, ((0,), (0,)))


def normalize(token_rows, norm_gain, norm_shift):
    mean_row = jnp.mean(token_rows, axis=-1, keepdims=True)
    centred = token_rows - mean_row
    inv_std = lax.rsqrt(jnp.mean(centred * centred, axis=-1, keepdims=True) + eps_norm)
    scaled = centred * inv_std
    return (scaled * norm_gain + norm_shift, scaled, inv_std)


def normalize_back(grad_out, scaled, inv_std, norm_gain):
    grad_scaled = grad_out * norm_gain
    centre_part = jnp.mean(grad_scaled, axis=-1, keepdims=True)
    along_part = scaled * jnp.mean(grad_scaled * scaled, axis=-1, keepdims=True)
    grad_in = inv_std * (grad_scaled - centre_part - along_part)
    return (grad_in, jnp.sum(grad_out * scaled, axis=0), jnp.sum(grad_out, axis=0))


def adam_step(weight, first_moment, second_moment, gradient, rate, decay, step_number):
    first_new = beta_one * first_moment + (1.0 - beta_one) * gradient
    second_new = beta_two * second_moment + (1.0 - beta_two) * gradient * gradient
    corr_one = 1.0 - jnp.power(beta_one, step_number)
    corr_two = 1.0 - jnp.power(beta_two, step_number)
    update = first_new / corr_one / (jnp.sqrt(second_new / corr_two) + eps_adam)
    return (weight - rate * (update + decay * weight), first_new, second_new)


def attend_kernel(heads, block, bias_ref, q_ref, kv_ref, ctx_ref, lse_ref):
    width = heads * HEAD_DIM
    bias = bias_ref[...]
    for h in range(heads):
        lo = h * HEAD_DIM
        q = q_ref[0, :, lo : lo + HEAD_DIM] * jnp.asarray(HEAD_DIM**-0.5, BF16)
        k = kv_ref[0, :, width + lo : width + lo + HEAD_DIM]
        v = kv_ref[0, :, 2 * width + lo : 2 * width + lo + HEAD_DIM]
        s = mm_nt(q, k) + bias
        top = jnp.max(s, axis=-1, keepdims=True)
        e = jnp.exp(s - top)
        total = jnp.sum(e, axis=-1, keepdims=True)
        ctx = mm_nn(e.astype(BF16), v) / total
        ctx_ref[0, :, lo : lo + HEAD_DIM] = ctx.astype(BF16)
        lse_ref[0, :, h : h + 1] = top + jnp.log(total)


def attend(qkv, bias, heads):
    chunks, seq, _ = qkv.shape
    block = min(256, seq)
    width = heads * HEAD_DIM
    return pl.pallas_call(
        functools.partial(attend_kernel, heads, block),
        grid=(chunks, seq // block),
        in_specs=[
            pl.BlockSpec((1, seq), lambda i, j: (0, 0)),
            pl.BlockSpec((1, block, 3 * width), lambda i, j: (i, j, 0)),
            pl.BlockSpec((1, seq, 3 * width), lambda i, j: (i, 0, 0)),
        ],
        out_specs=[
            pl.BlockSpec((1, block, width), lambda i, j: (i, j, 0)),
            pl.BlockSpec((1, block, 8), lambda i, j: (i, j, 0)),
        ],
        out_shape=[
            jax.ShapeDtypeStruct((chunks, seq, width), BF16),
            jax.ShapeDtypeStruct((chunks, seq, 8), F32),
        ],
        cost_estimate=pl.CostEstimate(
            flops=16 * chunks * heads * seq * seq * HEAD_DIM,
            bytes_accessed=8 * chunks * seq * width,
            transcendentals=chunks * heads * seq * seq,
        ),
        name="attend",
    )(bias, qkv, qkv)


def attend_back_kernel(heads, bias_ref, q_ref, g_ref, o_ref, lse_ref, kv_ref, gq_ref, gkv_ref, acc_ref):
    width = heads * HEAD_DIM
    step = pl.program_id(1)
    scale = HEAD_DIM**-0.5

    @pl.when(step == 0)
    def _():
        acc_ref[...] = jnp.zeros_like(acc_ref)

    bias = bias_ref[...]
    lse_rows = lse_ref[0].T
    for h in range(heads):
        lo = h * HEAD_DIM
        q = q_ref[0, :, lo : lo + HEAD_DIM] * jnp.asarray(scale, BF16)
        g = g_ref[0, :, lo : lo + HEAD_DIM]
        o = o_ref[0, :, lo : lo + HEAD_DIM]
        k = kv_ref[0, :, width + lo : width + lo + HEAD_DIM]
        v = kv_ref[0, :, 2 * width + lo : 2 * width + lo + HEAD_DIM]
        delta = jnp.sum(g.astype(F32) * o.astype(F32), axis=-1, keepdims=True).T
        st = mm_nt(k, q) + bias
        pt = jnp.exp(st - lse_rows[h : h + 1, :])
        gpt = mm_nt(v, g)
        gst = (pt * (gpt - delta)).astype(BF16)
        acc_ref[:, width + lo : width + lo + HEAD_DIM] += mm_nn(pt.astype(BF16), g)
        acc_ref[:, lo : lo + HEAD_DIM] += mm_nn(gst, q)
        gq_ref[0, :, lo : lo + HEAD_DIM] = (mm_tn(gst, k) * scale).astype(BF16)

    @pl.when(step == pl.num_programs(1) - 1)
    def _():
        gkv_ref[0] = acc_ref[...].astype(BF16)


def attend_back(qkv, grad_ctx, ctx, lse, bias_col, heads):
    chunks, seq, _ = qkv.shape
    block = min(256, seq)
    width = heads * HEAD_DIM
    return pl.pallas_call(
        functools.partial(attend_back_kernel, heads),
        grid=(chunks, seq // block),
        in_specs=[
            pl.BlockSpec((seq, 1), lambda i, j: (0, 0)),
            pl.BlockSpec((1, block, 3 * width), lambda i, j: (i, j, 0)),
            pl.BlockSpec((1, block, width), lambda i, j: (i, j, 0)),
            pl.BlockSpec((1, block, width), lambda i, j: (i, j, 0)),
            pl.BlockSpec((1, block, 8), lambda i, j: (i, j, 0)),
            pl.BlockSpec((1, seq, 3 * width), lambda i, j: (i, 0, 0)),
        ],
        out_specs=[
            pl.BlockSpec((1, block, width), lambda i, j: (i, j, 0)),
            pl.BlockSpec((1, seq, 2 * width), lambda i, j: (i, 0, 0)),
        ],
        out_shape=[
            jax.ShapeDtypeStruct((chunks, seq, width), BF16),
            jax.ShapeDtypeStruct((chunks, seq, 2 * width), BF16),
        ],
        scratch_shapes=[pltpu.VMEM((seq, 2 * width), F32)],
        cost_estimate=pl.CostEstimate(
            flops=40 * chunks * heads * seq * seq * HEAD_DIM,
            bytes_accessed=20 * chunks * seq * width,
            transcendentals=chunks * heads * seq * seq,
        ),
        name="attend_back",
    )(bias_col, qkv, grad_ctx, ctx, lse, qkv)


class Routes:
    def __init__(self, dp_size, mp_size):
        self.dp, self.mp = dp_size, mp_size
        self.bits = (dp_size // 2).bit_length() - 1
        self.mp_bits = mp_size.bit_length() - 1

    def _pairs(self, target):
        pairs = []
        for d in range(self.dp):
            for m in range(self.mp):
                dest = target(d // 2, d % 2, m)
                pairs.append((d * self.mp + m, (dest[0] * 2 + dest[1]) * self.mp + dest[2]))
        return pairs

    def send(self, value, target, back=False):
        pairs = self._pairs(target)
        if back:
            pairs = [(b, a) for a, b in pairs]
        return lax.ppermute(value, AXES, pairs)

    def partner(self, value):
        return self.send(value, lambda p, c, m: (p, 1 - c, m))

    def pair_bit(self, value, bit):
        return self.send(value, lambda p, c, m: (p ^ (1 << bit), c, m))

    def mp_bit(self, value, bit):
        return self.send(value, lambda p, c, m: (p, c, m ^ (1 << bit)))

    def cell(self, value, k, back=False):
        return self.send(value, lambda p, c, m: (p, m // 2, 2 * c + ((m % 2) ^ k)), back)

    def shard(self, value, k, back=False):
        return self.send(value, lambda p, c, m: (p, m // 2, m ^ k ^ (2 * c)), back)


def gather_shards(routes, shard):
    got = [routes.shard(shard, k) for k in range(4)]
    chunks = []
    for half in range(2):
        own = jnp.stack([got[half], got[half + 2]])
        order = range(routes.bits) if half else reversed(range(routes.bits))
        pieces = {0: own}
        for bit in order:
            if routes.bits <= 2:
                pieces.update({r | (1 << bit): routes.pair_bit(v, bit) for r, v in list(pieces.items())})
            else:
                keys = sorted(pieces)
                cat = routes.pair_bit(jnp.stack([pieces[r] for r in keys]), bit)
                pieces.update({r | (1 << bit): cat[i] for i, r in enumerate(keys)})
        chunks.append(pieces)
    return chunks


def assemble(pieces, mask):
    count = len(pieces)
    _, rows, width = pieces[0].shape
    full = jnp.zeros((count * 2 * rows, width), pieces[0].dtype)
    for r in range(count):
        for e in range(2):
            full = lax.dynamic_update_slice(full, pieces[r][e], ((((2 * r + e) ^ mask)) * rows, 0))
    return full


def scatter_grads(routes, chunks, mask):
    partial = []
    for half in range(2):
        full = chunks[half]
        count = 1 << routes.bits
        rows = full.shape[0] // (2 * count)
        blocks = full.reshape(2 * count, rows, full.shape[1])
        pieces = {
            r: jnp.stack([lax.dynamic_index_in_dim(blocks, (2 * r + e) ^ mask, 0, keepdims=False) for e in range(2)])
            for r in range(count)
        }
        order = range(routes.bits) if not half else reversed(range(routes.bits))
        for bit in order:
            keys = sorted(r for r in pieces if not r & (1 << bit))
            sent = routes.pair_bit(jnp.stack([pieces[r | (1 << bit)] for r in keys]), bit)
            pieces = {
                r: (pieces[r].astype(F32) + sent[i].astype(F32)).astype(BF16) for i, r in enumerate(keys)
            }
        partial.append(pieces[0])
    total = None
    for k in range(4):
        got = routes.shard(partial[k % 2][k // 2], k, back=True).astype(F32)
        total = got if total is None else total + got
    return total


MESH = pl.DeviceIdType.MESH


class Here:
    def __init__(self):
        self.d, self.m = lax.axis_index("dp"), lax.axis_index("mp")
        self.c = self.d % 2
        self.pair = self.d - self.c
        self.x = (self.d // 2) % 2
        self.y = self.d // 4
        self.t = self.m // 2
        self.b = self.m % 2
        self.over_x = {"dp": self.d + 2 - 4 * self.x, "mp": self.m}
        self.over_y = {"dp": self.d + 4 - 8 * self.y, "mp": self.m}
        self.partner = {"dp": self.d + 1 - 2 * self.c, "mp": self.m}
        self.home = self.t == self.c

    def at(self, core, m):
        return {"dp": self.pair + core, "mp": m}


def remote(src, dst, ssem, rsem, dev):
    return pltpu.make_async_remote_copy(
        src_ref=src, dst_ref=dst, send_sem=ssem, recv_sem=rsem, device_id=dev, device_id_type=MESH
    )


def arrived(dst, rsem, dev):
    remote(dst, dst, rsem, rsem, dev).wait_recv()


class Maybe:
    def __init__(self, src, dst, ssem, rsem, dev, own):
        self.args, self.dev, self.ssem, self.own = (src, dst), dev, ssem, own
        self.rsem = rsem

    def far(self):
        return remote(*self.args, self.ssem, self.rsem, self.dev)

    def start(self):
        pl.when(self.own)(lambda: pltpu.make_async_copy(*self.args, self.rsem).start())
        pl.when(jnp.logical_not(self.own))(lambda: self.far().start())

    def wait_send(self):
        pl.when(jnp.logical_not(self.own))(lambda: self.far().wait_send())


def greet(here):
    barrier = pltpu.get_barrier_semaphore()

    def tell(dev):
        pl.semaphore_signal(barrier, inc=1, device_id=dev, device_id_type=MESH)

    for core in range(2):
        for m in range(4):
            other = jnp.logical_or(here.c != core, here.m != m)
            pl.when(other)(functools.partial(tell, here.at(core, m)))
    tell(here.over_x)
    tell(here.over_y)
    pl.semaphore_wait(barrier, 9)


class Gather:
    def __init__(self, here, shard, full, sems, relayed):
        self.relayed = relayed
        (self.send_z, self.got_z, self.send_f, self.send_x, self.send_y, self.got_x, self.got_y, self.send_r, self.got_r) = sems
        self.here, self.shard, self.full = here, shard, full
        self.rows = shard.shape[0]
        self.first = jnp.where(here.m > 2 * here.c, 1, 0)

    @staticmethod
    def scratch():
        dma = pltpu.SemaphoreType.DMA
        return [dma((5,))] + [dma((2, 2))] * 8

    def plane(self, i):
        return (self.first + i) % 2

    def block(self, i, dp):
        return self.full.at[self.plane(i), pl.ds(dp * self.rows, self.rows), :]

    def z_copies(self):
        h = self.here
        dst = self.full.at[h.b, pl.ds(h.d * self.rows, self.rows), :]
        got = self.got_z.at[h.b, h.c]
        if self.relayed:
            far = [(h.m < 3, (h.m + 1) % 4), (h.m > 0, (h.m + 3) % 4)]
        else:
            far = [(h.m != m, m) for m in range(4)]
        copies = [
            (there, remote(self.shard, dst, self.send_z.at[n], got, h.at(h.t, m))) for n, (there, m) in enumerate(far)
        ]
        return Maybe(self.shard, dst, self.send_z.at[4], got, h.at(h.t, h.m), h.home), copies

    def start_near(self):
        self.z_copies()[0].start()

    def start_far(self):
        for there, copy in self.z_copies()[1]:
            pl.when(there)(copy.start)

    def onward(self, i, e):
        h = self.here
        source = 2 * h.c + self.plane(i)
        up = source < h.m
        there = jnp.logical_or(jnp.logical_and(up, h.m < 3), jnp.logical_and(source > h.m, h.m > 0))
        ref = self.block(i, h.pair + e)
        target = (h.m + 3 - 2 * up.astype(jnp.int32)) % 4
        return there, remote(ref, ref, self.send_f.at[i, e], self.got_z.at[self.plane(i), e], h.at(h.c, target))

    def own_copies(self, i, e):
        h = self.here
        ref = self.block(i, h.pair + e)
        return (
            remote(ref, ref, self.send_x.at[i, e], self.got_x.at[i, e], h.over_x),
            remote(ref, ref, self.send_y.at[i, e], self.got_y.at[i, e], h.over_y),
        )

    def spread(self, i):
        h = self.here
        for e in range(2):
            arrived(self.block(i, h.pair + e), self.got_z.at[self.plane(i), e], h.partner)
            if self.relayed:
                there, copy = self.onward(i, e)
                pl.when(there)(copy.start)
            for copy in self.own_copies(i, e):
                copy.start()

    def relay_copy(self, i, e):
        h = self.here
        if i == 0:
            ref, dev = self.block(i, h.over_y["dp"] - h.c + e), h.over_x
        else:
            ref, dev = self.block(i, h.over_x["dp"] - h.c + e), h.over_y
        return remote(ref, ref, self.send_r.at[i, e], self.got_r.at[i, e], dev)

    def relay(self, i):
        h = self.here
        for e in range(2):
            if i == 0:
                arrived(self.block(i, h.over_y["dp"] - h.c + e), self.got_y.at[i, e], h.over_y)
            else:
                arrived(self.block(i, h.over_x["dp"] - h.c + e), self.got_x.at[i, e], h.over_x)
            self.relay_copy(i, e).start()

    def finish(self):
        self.arrive()
        self.sent()

    def arrive(self):
        h = self.here
        diagonal = h.pair + 2 - 4 * h.x + 4 - 8 * h.y
        for i in range(2):
            for e in range(2):
                if i == 0:
                    arrived(self.block(i, h.over_x["dp"] - h.c + e), self.got_x.at[i, e], h.over_x)
                else:
                    arrived(self.block(i, h.over_y["dp"] - h.c + e), self.got_y.at[i, e], h.over_y)
                arrived(self.block(i, diagonal + e), self.got_r.at[i, e], h.over_x)

    def sent(self):
        near, far = self.z_copies()
        near.wait_send()
        for there, copy in far:
            pl.when(there)(copy.wait_send)
        for i in range(2):
            for e in range(2):
                if self.relayed:
                    there, copy = self.onward(i, e)
                    pl.when(there)(copy.wait_send)
                for copy in self.own_copies(i, e):
                    copy.wait_send()
                self.relay_copy(i, e).wait_send()


class ToCell:
    def __init__(self, here, source, rows, send, got):
        self.here, self.source, self.rows, self.send, self.got = here, source, rows, send, got

    def copy(self, s):
        h = self.here
        target = 2 * h.c + s
        own = jnp.logical_and(h.home, h.m == target)
        return Maybe(self.source.at[s], self.rows.at[h.b], self.send.at[s], self.got.at[h.b], h.at(h.t, target), own)

    def start(self):
        for s in range(2):
            self.copy(s).start()

    def wait(self):
        for b in range(2):
            arrived(self.rows.at[b], self.got.at[b], self.here.partner)

    def finish(self):
        for s in range(2):
            self.copy(s).wait_send()


class Norms:
    def __init__(self, here, slot, slots, sems):
        self.here, self.slot, self.slots = here, slot, slots
        self.send_z, self.got_z, self.send, self.got = sems

    @staticmethod
    def scratch():
        dma = pltpu.SemaphoreType.DMA
        return [dma((4,)), dma((4,)), dma((3,)), dma((3,))]

    def span(self, d, count):
        return self.slots.at[pl.ds(d * 4 // count * count, count)]

    def z_copy(self, m):
        h = self.here
        return Maybe(self.slot, self.slots.at[h.d * 4 + h.m], self.send_z.at[m], self.got_z.at[h.m], {"dp": h.d, "mp": m}, h.m == m)

    def copy(self, k):
        h = self.here
        ref = self.span(h.d, 4 << k)
        return remote(ref, ref, self.send.at[k], self.got.at[k], (h.partner, h.over_x, h.over_y)[k])

    def start_z(self):
        for m in range(4):
            self.z_copy(m).start()

    def wait_z(self):
        h = self.here
        for m in range(4):
            arrived(self.slots.at[h.d * 4 + m], self.got_z.at[m], h.partner)

    def start(self, k):
        self.copy(k).start()

    def wait(self, k):
        h = self.here
        dev = (h.partner, h.over_x, h.over_y)[k]
        arrived(self.span(dev["dp"], 4 << k), self.got.at[k], dev)

    def sent(self):
        for m in range(4):
            self.z_copy(m).wait_send()
        for k in range(3):
            self.copy(k).wait_send()


def norm_rows(values, gain, shift):
    mean_row = jnp.mean(values, axis=-1, keepdims=True)
    centred = values - mean_row
    inv_std = lax.rsqrt(jnp.mean(centred * centred, axis=-1, keepdims=True) + eps_norm)
    return centred * inv_std * gain + shift


ANY = pl.BlockSpec(memory_space=pl.ANY)
VMEM = pl.BlockSpec(memory_space=pltpu.VMEM)


def rows_at(start, size):
    return pl.ds(start * size, size)


def exact_gelu_both(u):
    below = 0.5 * (1.0 + lax.erf(u * (0.5**0.5)))
    density = jnp.exp(-0.5 * u * u) * ((2.0 * jnp.pi) ** -0.5)
    return u * below, below + u * density


class Stores:
    def __init__(self, sems):
        self.sems, self.made = sems, []

    def put(self, src, dst):
        copy = pltpu.make_async_copy(src, dst, self.sems.at[len(self.made)])
        copy.start()
        self.made.append((src, dst))

    def finish(self):
        for i, (src, dst) in enumerate(self.made):
            pltpu.make_async_copy(src, dst, self.sems.at[i]).wait()


def attend_rows(bias, qkv_ref, ctx_ref, lse_ref, chunk, start, block, heads):
    width = heads * HEAD_DIM
    spare = qkv_ref.shape[2] - 3 * width
    rows = pl.ds(start, block)
    stats = []
    for h in range(heads):
        lo = spare + h * HEAD_DIM
        q = qkv_ref[chunk, rows, lo : lo + HEAD_DIM] * jnp.asarray(HEAD_DIM**-0.5, BF16)
        k = qkv_ref[chunk, :, width + lo : width + lo + HEAD_DIM]
        v = qkv_ref[chunk, :, 2 * width + lo : 2 * width + lo + HEAD_DIM]
        s = mm_nt(q, k) + bias
        top = jnp.max(s, axis=-1, keepdims=True)
        e = jnp.exp(s - top)
        total = jnp.sum(e, axis=-1, keepdims=True)
        ctx = mm_nn(e.astype(BF16), v) / total
        ctx_ref[chunk, rows, h * HEAD_DIM : (h + 1) * HEAD_DIM] = ctx.astype(BF16)
        stats.append(top + jnp.log(total))
    stats += [jnp.zeros_like(stats[0])] * (8 - heads)
    lse_ref[chunk, :, rows] = jnp.concatenate(stats, axis=1).T


def forward_kernel(heads, *refs):
    (x_ref, gy_ref, shard_a, shard_1, shard_2, slot_ref) = refs[:6]
    (full_a, full_1, full_2, h1_out, qkv_out, ctx_out, lse_out, x_out, x2_out, h2_out, act_out, slope_out, gy_out,
     grad_out, norm_ref, count_ref) = refs[6:22]
    (weight, x_in, gy_in, h1, qkv, ctx, lse, fold_out, fold_in, x2, h2, act, slope, gy, stage, slots) = refs[22:38]
    sems = refs[38:]
    (cell_sems, swap_send, swap_got, load_sem, store_sems, stage_sems) = (
        sems[:4], sems[4], sems[5], sems[6], sems[7], sems[8]
    )
    here = Here()
    half, width = x2.shape
    seq = 2 * half
    quarter = half // 2
    inner = heads * HEAD_DIM
    greet(here)
    per = len(Gather.scratch())
    norms = Norms(here, slot_ref, slots, sems[9 + 3 * per :])
    block_a, block_1, block_2 = (
        Gather(here, shard, full, sems[9 + per * i : 9 + per * (i + 1)], i <= 1)
        for i, (shard, full) in enumerate(((shard_a, full_a), (shard_1, full_1), (shard_2, full_2)))
    )
    cell_x = ToCell(here, x_ref, x_in, cell_sems[0], cell_sems[1])
    cell_g = ToCell(here, gy_ref, gy_in, cell_sems[2], cell_sems[3])
    stores = Stores(store_sems)

    def swap(n, src, dst):
        return remote(src, dst, swap_send.at[n], swap_got.at[n], here.partner)

    def load(full):
        copies = [pltpu.make_async_copy(full.at[b], weight.at[b], load_sem.at[b]) for b in range(2)]
        for copy in copies:
            copy.start()
        for copy in copies:
            copy.wait()

    own, other = pl.ds(0, half), pl.ds(half, half)
    away = jnp.logical_not(here.home)
    norms.start_z()
    block_a.start_far()
    for block in (block_a, block_1, block_2):
        block.start_near()
    block_a.spread(0)
    norms.wait_z()
    norms.start(0)
    block_a.relay(0)
    norms.wait(0)
    norms.start(1)
    cell_x.start()
    block_a.spread(1)
    block_1.start_far()
    norms.wait(1)
    norms.start(2)
    block_a.relay(1)
    pl.when(here.home)(lambda: block_1.spread(0))
    norms.wait(2)
    columns = norm_ref.shape[1] // 32
    for n in range(32):
        norm_ref[:, n * columns : (n + 1) * columns] = slots[n, 0:4, 0:columns]
    lanes = lax.broadcasted_iota(jnp.int32, (1, 128), 1)
    count_row = slots[(here.pair + here.t) * 4 + here.m, 4:5, :]
    count = jnp.sum(jnp.where(lanes == here.b, count_row, 0.0), axis=1, keepdims=True)
    count_ref[...] = jnp.broadcast_to(count, count_ref.shape)
    cell_x.wait()

    step = 128
    per_quarter = quarter // step

    @pl.loop(0, half // step)
    def _(i):
        rows = pl.ds(pl.multiple_of((i % per_quarter) * step, step), step)
        h1[pl.ds(pl.multiple_of(i * step, step), step), :] = norm_rows(
            x_in[i // per_quarter, rows, :].astype(F32), norm_ref[0:1, :], norm_ref[1:2, :]
        ).astype(BF16)

    swap_h1 = swap(0, h1.at[own], h1.at[other])
    swap_h1.start()
    stores.put(x_in, x_out)
    pl.when(away)(lambda: block_1.spread(0))
    block_1.spread(1)
    block_2.start_far()
    block_a.arrive()
    pl.when(here.home)(lambda: block_1.relay(0))
    pl.when(here.home)(lambda: block_2.spread(0))
    load(full_a)
    swap_h1.wait_recv()
    stores.put(h1, h1_out)

    first = 4 * inner - qkv.shape[2]

    @pl.loop(0, 2)
    def _(b):
        for n in range(0, qkv.shape[2], 512):
            qkv[b, :, n : n + 512] = mm_nn(h1[...], weight[b, :, first + n : first + n + 512]).astype(BF16)

    stores.put(qkv, qkv_out)
    bias = key_bias(here, count, lax.broadcasted_iota(jnp.int32, (1, seq), 1), half)
    q_block = 256
    per_chunk = seq // q_block

    @pl.loop(0, 2 * per_chunk)
    def _(i):
        pl.when(jnp.logical_and(i == 0, away))(lambda: block_1.relay(0))
        pl.when(i == 3)(lambda: block_1.relay(1))
        pl.when(jnp.logical_and(i == 4, here.home))(lambda: block_2.relay(0))
        pl.when(jnp.logical_and(i == 5, away))(lambda: block_2.spread(0))
        pl.when(i == 7)(lambda: block_2.spread(1))
        attend_rows(
            bias, qkv, ctx, lse, i // per_chunk, pl.multiple_of((i % per_chunk) * q_block, q_block), q_block, heads
        )

    stores.put(ctx, ctx_out)
    stores.put(lse, lse_out)

    def branch_tile(rows, n):
        cols = pl.ds(pl.multiple_of(n * 256, 256), 256)
        return mm_nt(ctx[0, rows, :], weight[0, cols, 0:inner]) + mm_nt(ctx[1, rows, :], weight[1, cols, 0:inner]), cols

    @pl.loop(0, width // 256)
    def _(n):
        part, cols = branch_tile(other, n)
        fold_out[:, cols] = part.astype(BF16)

    swap_fold = swap(1, fold_out, fold_in)
    swap_fold.start()

    @pl.loop(0, width // 256)
    def _(n):
        part, cols = branch_tile(own, n)
        for b in range(2):
            rows = pl.ds(b * quarter, quarter)
            x2[rows, cols] = x_in[b, :, cols].astype(F32) + part[b * quarter : (b + 1) * quarter]

    swap_fold.wait_recv()

    @pl.loop(0, half // step)
    def _(i):
        rows = pl.ds(pl.multiple_of(i * step, step), step)
        middle = x2[rows, :] + fold_in[rows, :].astype(F32)
        x2[rows, :] = middle
        h2[rows, :] = norm_rows(middle, norm_ref[2:3, :], norm_ref[3:4, :]).astype(BF16)

    swap_h2 = swap(2, h2.at[own], h2.at[other])
    swap_h2.start()
    stores.put(x2, x2_out)
    cell_g.start()
    block_1.arrive()
    load(full_1)
    swap_h2.wait_recv()
    stores.put(h2, h2_out)
    per_unit = width // 256

    @pl.loop(0, 2 * per_unit)
    def _(i):
        pl.when(jnp.logical_and(i == 0, away))(lambda: block_2.relay(0))
        pl.when(i == 5)(lambda: block_2.relay(1))
        b, cols = i // per_unit, pl.ds(pl.multiple_of((i % per_unit) * 256, 256), 256)
        value, grad = exact_gelu_both(mm_nn(h2[...], weight[b, :, cols]))
        act[b, :, cols] = value.astype(BF16)
        slope[b, :, cols] = grad.astype(BF16)

    stores.put(act, act_out)
    stores.put(slope, slope_out)
    cell_g.wait()

    @pl.loop(0, 2)
    def _(b):
        gy[pl.ds(pl.multiple_of(b * quarter, quarter), quarter), :] = gy_in[b]

    swap_gy = swap(3, gy.at[own], gy.at[other])
    swap_gy.start()
    swap_gy.wait_recv()
    stores.put(gy, gy_out)

    def stage_copy(i):
        slot = i % 2
        return pltpu.make_async_copy(
            stage.at[slot], grad_out.at[:, pl.ds(pl.multiple_of(i * 256, 256), 256), :], stage_sems.at[slot]
        )

    @pl.loop(0, width // 256)
    def _(i):
        pl.when(i >= 2)(lambda: stage_copy(i - 2).wait())
        left = gy[:, pl.ds(pl.multiple_of(i * 256, 256), 256)].T
        for b in range(2):
            stage[i % 2, b] = mm_nn(left, act[b]).astype(BF16)
        stage_copy(i).start()

    for i in range(width // 256 - 2, width // 256):
        stage_copy(i).wait()
    block_2.arrive()
    for block in (block_a, block_1, block_2):
        block.sent()
    cell_x.finish()
    cell_g.finish()
    norms.sent()
    for n, (src, dst) in enumerate(((h1.at[own], h1.at[other]), (fold_out, fold_in), (h2.at[own], h2.at[other]), (gy.at[own], gy.at[other]))):
        swap(n, src, dst).wait_send()
    stores.finish()


def key_bias(here, count, index, half):
    position = jnp.where(index < half, here.c * half + index, (1 - here.c) * half + index - half)
    return jnp.where(position.astype(F32) < 1.0 + count, 0.0, masked_score)


def forward(inputs, cotangent, shards, slot, heads, collective):
    cells, quarter, width = inputs.shape
    rows, wide = shards[0].shape
    half, seq, inner = 2 * quarter, 4 * quarter, heads * HEAD_DIM
    part = (3 * inner + 255) // 256 * 256
    dma = pltpu.SemaphoreType.DMA
    full = ((2, 8 * rows, wide), BF16)
    kept = [
        ((seq, width), BF16), ((2, seq, part), BF16), ((2, seq, inner), BF16), ((2, 8, seq), F32),
        ((2, quarter, width), BF16), ((half, width), F32), ((seq, width), BF16), ((2, seq, wide), BF16),
        ((2, seq, wide), BF16), ((seq, width), BF16), ((2, width, wide), BF16),
    ]
    buffers = [
        full, ((2, quarter, width), BF16), ((2, quarter, width), BF16), kept[0], kept[1], kept[2], kept[3],
        ((half, width), BF16), ((half, width), BF16), kept[5], kept[6], kept[7], kept[8], kept[9],
        ((2, 2, 256, wide), BF16), ((32, 8, 128), F32),
    ]
    return pl.pallas_call(
        functools.partial(forward_kernel, heads),
        out_shape=[jax.ShapeDtypeStruct(*s) for s in [full] * 3 + kept + [((4, width), F32), ((8, 128), F32)]],
        in_specs=[VMEM] * 6,
        out_specs=[ANY] * 14 + [VMEM] * 2,
        scratch_shapes=[pltpu.VMEM(*s) for s in buffers]
        + [dma((2,))] * 4 + [dma((4,)), dma((4,)), dma((2,)), dma((10,)), dma((2,))]
        + Gather.scratch() * 3 + Norms.scratch(),
        compiler_params=pltpu.CompilerParams(
            collective_id=collective, has_side_effects=True, vmem_limit_bytes=67043328
        ),
        name="forward",
    )(inputs, cotangent, *shards, slot)


class Reduce:
    def __init__(self, here, grads, bufs, sems):
        self.here, self.grads = here, grads
        self.own, self.one, self.two, self.far, self.last, self.part = bufs
        (self.sem_own, self.send_one, self.got_one, self.send_two, self.got_two, self.send_z, self.got_far, self.got_z) = sems
        self.piece = self.own.shape[2]
        self.before = None
        self.away = jnp.logical_not(here.home)
        self.outer = here.m % 3 == 0

    @staticmethod
    def scratch(rows, width):
        r = rows // 2
        dma = pltpu.SemaphoreType.DMA
        four = pltpu.VMEM((2, 4, r, width), BF16)
        landing = [pltpu.VMEM((2, 2, 4, r, width), BF16), four, four, pltpu.VMEM((3, 2, r, width), BF16)]
        sems = [dma((2, 2, 4)), dma((2, 2, 4)), dma((2, 4)), dma((2, 4)), dma((2, 4)), dma((2, 4)), dma((3, 2))]
        return pltpu.VMEM((2, 2, r, width), BF16), four, landing, sems

    def rows_of(self, role, dp, j):
        return self.grads.at[role, pl.ds(dp * 2 * self.piece + j * self.piece, self.piece), :]

    def pair_at(self, role, n, far):
        h = self.here
        dx, dy = 2 - 4 * h.x, 4 - 8 * h.y
        first, second = (dx, dy) if role == 0 else (dy, dx)
        return h.pair + (first if far else 0) + (second if n == 0 else 0)

    def copy_one(self, role, n, j):
        dev = self.here.over_x if role == 0 else self.here.over_y
        return remote(
            self.rows_of(role, self.pair_at(role, n, True), j), self.one.at[role, n, j],
            self.send_one.at[role, n, j], self.got_one.at[role, n, j], dev,
        )

    def copy_two(self, role, j):
        dev = self.here.over_y if role == 0 else self.here.over_x
        return remote(
            self.one.at[role, 0, j], self.two.at[role, j], self.send_two.at[role, j], self.got_two.at[role, j], dev
        )

    def to_inner(self, role, j):
        h = self.here
        return remote(
            self.part.at[role, j], self.far.at[role, j], self.send_z.at[role, j], self.got_far.at[role, j],
            h.at(h.c, h.m + 1 - 2 * h.b),
        )

    def to_owner(self, role, j):
        h = self.here
        target = 2 * h.c + role
        slot = jnp.where(self.away, 2, (h.m + target) % 2)
        return remote(
            self.part.at[role, j], self.last.at[slot, j % 2], self.send_z.at[role, j], self.got_z.at[slot, j % 2],
            h.at(j // 2, target),
        )

    def mine(self, role, j):
        return jnp.logical_and(self.here.c == j // 2, self.here.m == 2 * self.here.c + role)

    def direct(self, role, j):
        return jnp.logical_and(self.here.home, jnp.logical_not(self.mine(role, j)))

    def start_one(self, j):
        for n in range(2):
            for role in range(2):
                self.copy_one(role, n, j).start()

    def start(self):
        for j in range(3):
            self.start_one(j)
        for role in range(2):
            for n in range(2):
                self.load_piece(role, n, 0).start()

    def load_piece(self, role, n, j):
        return pltpu.make_async_copy(
            self.rows_of(role, self.pair_at(role, n, False), j), self.own.at[role, n], self.sem_own.at[role, n]
        )

    def add_one(self, role, j):
        h = self.here
        for n in range(2):
            self.load_piece(role, n, j).wait()
            arrived(self.one.at[role, n, j], self.got_one.at[role, n, j], h.over_x)
            self.one[role, n, j] = self.own[role, n] + self.one[role, n, j]
            if n == 0:
                self.copy_two(role, j).start()
            if j < 3:
                self.load_piece(role, n, j + 1).start()

    def add_two(self, role, j):
        arrived(self.two.at[role, j], self.got_two.at[role, j], self.here.over_x)
        total = self.one[role, 1, j] + self.two[role, j]
        if self.before is not None:
            self.before.z_sent(role, j)

        @pl.when(self.mine(role, j))
        def _():
            self.last[0, j % 2] = total

        @pl.when(jnp.logical_not(self.mine(role, j)))
        def _():
            self.part[role, j] = total

        pl.when(self.direct(role, j))(lambda: self.to_owner(role, j).start())
        pl.when(jnp.logical_and(self.away, self.outer))(lambda: self.to_inner(role, j).start())

    def pass_on(self, role, j):
        @pl.when(jnp.logical_and(self.away, jnp.logical_not(self.outer)))
        def _():
            arrived(self.far.at[role, j], self.got_far.at[role, j], self.here.partner)
            self.part[role, j] = self.part[role, j] + self.far[role, j]
            self.to_owner(role, j).start()

    def step(self, j):
        for role in range(2):
            if j < 4:
                self.add_one(role, j)
        if j == 0:
            self.start_one(3)
        for role in range(2):
            if 1 <= j <= 4:
                self.add_two(role, j - 1)
        for role in range(2):
            if j >= 2:
                self.pass_on(role, j - 2)

    def z_sent(self, role, j):
        inner = jnp.logical_and(self.away, jnp.logical_not(self.outer))
        pl.when(jnp.logical_or(self.direct(role, j), inner))(lambda: self.to_owner(role, j).wait_send())
        pl.when(jnp.logical_and(self.away, self.outer))(lambda: self.to_inner(role, j).wait_send())

    def finish(self, total, out_ref, sem):
        h = self.here
        for s in range(2):
            pl.when(self.away)(functools.partial(arrived, self.last.at[0, s], self.got_z.at[0, s], h.partner))
            for n in range(1, 3):
                arrived(self.last.at[n, s], self.got_z.at[n, s], h.partner)
            rows = self.last[0, s].astype(F32)
            for n in range(1, 3):
                rows = rows + self.last[n, s].astype(F32)
            total[pl.ds(s * self.piece, self.piece), :] = rows
        copy = pltpu.make_async_copy(total, out_ref, sem)
        copy.start()
        for role in range(2):
            for j in range(4):
                for n in range(2):
                    self.copy_one(role, n, j).wait_send()
                self.copy_two(role, j).wait_send()
        copy.wait()


class FromCell:
    def __init__(self, here, rows, landing, send, got):
        self.here, self.rows, self.landing, self.send, self.got = here, rows, landing, send, got

    def copy(self, b):
        h = self.here
        target = 2 * h.c + b
        own = jnp.logical_and(h.home, h.m == target)
        return Maybe(self.rows.at[b], self.landing.at[h.b], self.send.at[b], self.got.at[h.b], h.at(h.t, target), own)

    def start(self):
        for b in range(2):
            self.copy(b).start()

    def sent(self):
        for b in range(2):
            self.copy(b).wait_send()

    def arrive(self):
        for s in range(2):
            arrived(self.landing.at[s], self.got.at[s], self.here.partner)


def norm_rows_back(values, grad_out, gain):
    mean_row = jnp.mean(values, axis=-1, keepdims=True)
    centred = values - mean_row
    inv_std = lax.rsqrt(jnp.mean(centred * centred, axis=-1, keepdims=True) + eps_norm)
    scaled = centred * inv_std
    grad_scaled = grad_out * gain
    centre_part = jnp.mean(grad_scaled, axis=-1, keepdims=True)
    along_part = scaled * jnp.mean(grad_scaled * scaled, axis=-1, keepdims=True)
    grad_in = inv_std * (grad_scaled - centre_part - along_part)
    return grad_in, jnp.sum(grad_out * scaled, axis=0, keepdims=True), jnp.sum(grad_out, axis=0, keepdims=True)


def attend_rows_back(bias, qkv_ref, gctx_ref, ctx_ref, lse_ref, grad_ref, acc_ref, chunk, start, block, heads):
    width = heads * HEAD_DIM
    spare = -3 * width % 256
    half = acc_ref.shape[0]
    rows = pl.ds(start, block)
    scale = HEAD_DIM**-0.5
    for h in range(heads):
        at = slice(h * HEAD_DIM, (h + 1) * HEAD_DIM)
        lo = spare + h * HEAD_DIM
        q = qkv_ref[chunk, rows, lo : lo + HEAD_DIM] * jnp.asarray(scale, BF16)
        k = qkv_ref[chunk, :, width + lo : width + lo + HEAD_DIM]
        v = qkv_ref[chunk, :, 2 * width + lo : 2 * width + lo + HEAD_DIM]
        g = gctx_ref[chunk, rows, at]
        delta = jnp.sum(g.astype(F32) * ctx_ref[chunk, rows, at].astype(F32), axis=-1, keepdims=True).T
        pt = jnp.exp(mm_nt(k, q) + bias - lse_ref[chunk, h : h + 1, rows])
        gst = (pt * (mm_nt(v, g) - delta)).astype(BF16)
        gk = mm_nn(gst, q)
        gv = mm_nn(pt.astype(BF16), g)
        for n, part in enumerate((gk[:half], gk[half:], gv[:half], gv[half:])):
            acc_ref[:, n * width + h * HEAD_DIM : n * width + (h + 1) * HEAD_DIM] += part
        grad_ref[chunk, rows, lo : lo + HEAD_DIM] = (mm_tn(gst, k) * scale).astype(BF16)


def backward_kernel(heads, *refs):
    (norm_ref, count_ref, full_a, full_1, full_2, h1_in, qkv_in, ctx_in, lse_in, x_src, x2_src, h2_in, act_in, slope_in,
     gy_src, grad_2) = refs[:16]
    (out_ref, gx_ref, sum_a, sum_1, sum_2, norm_out, grad_1, grad_a) = refs[16:24]
    (weight, gy, slope, act, h2, x2, fold_out, fold_in, gctx, ctx, lse, acc, stage, own, part) = refs[24:39]
    landings = [refs[39 + 4 * i : 43 + 4 * i] for i in range(3)]
    sums, sums_in = refs[51:53]
    sems = refs[53:]
    send_rows = stage
    (load_sems, swap_send, swap_got, cell_sems, stage_sems, own_sem, total_sem) = (
        sems[:10], sems[10], sems[11], sems[12:16], sems[16], sems[17], sems[18]
    )
    per = 7
    here = Here()
    half, width = x2.shape
    seq, quarter, inner = 2 * half, half // 2, heads * HEAD_DIM
    part_width = (3 * inner + 255) // 256 * 256
    first = 4 * inner - part_width
    spare = part_width - 3 * inner
    greet(here)
    blocks = [
        Reduce(here, grads, (own, *landings[i], part), (own_sem, *sems[19 + per * i : 19 + per * (i + 1)]))
        for i, grads in enumerate((grad_2, grad_1, grad_a))
    ]
    block_2, block_1, block_a = blocks
    own_rows, other_rows = pl.ds(0, half), pl.ds(half, half)

    def load(n, src, dst):
        return pltpu.make_async_copy(src, dst, load_sems[n])

    copies = {
        "w2": load(0, full_2, weight), "gy": load(1, gy_src, gy), "slope": load(2, slope_in, slope),
        "act": load(3, act_in, act), "h2": load(4, h2_in, h2), "x2": load(5, x2_src, x2), "ctx": load(6, ctx_in, ctx),
        "lse": load(7, lse_in, lse),
    }
    block_2.start()
    for copy in copies.values():
        copy.start()

    def fetch(src, dst):
        copy = load(9, src, dst)
        copy.start()
        return copy

    def swap(n, src, dst):
        return remote(src, dst, swap_send.at[n], swap_got.at[n], here.partner)

    def tile(n):
        return pl.ds(pl.multiple_of(n * 256, 256), 256)

    tiles = width // 256
    per_unit = width // 256

    copies["w2"].wait()
    copies["act"].wait()

    @pl.loop(0, tiles)
    def _(n):
        cols = tile(n)
        fold_out[:, cols] = (
            mm_nt(act[0, other_rows, :], weight[0, cols, :]) + mm_nt(act[1, other_rows, :], weight[1, cols, :])
        ).astype(BF16)

    swaps = [(fold_out, fold_in.at[0]), (fold_out, fold_in.at[1]), (h2.at[own_rows], h2.at[other_rows]), (fold_out, fold_in.at[0])]
    swap(0, *swaps[0]).start()

    for name in ("gy", "slope"):
        copies[name].wait()

    @pl.loop(0, 2 * per_unit)
    def _(i):
        pl.when(i == 4)(lambda: block_2.step(0))
        b, cols = i // per_unit, tile(i % per_unit)
        grad = mm_nn(gy[...], weight[b, :, cols])
        slope[b, :, cols] = (grad * slope[b, :, cols].astype(F32)).astype(BF16)

    block_2.step(1)
    copies["h2"].wait()

    def stage_copy(grads, i, b):
        return pltpu.make_async_copy(stage.at[b], grads.at[b, tile(i), :], stage_sems.at[b])

    @pl.loop(0, tiles)
    def _(i):
        left = h2[:, tile(i)].T
        for b in range(2):
            pl.when(i >= 1)(lambda: stage_copy(grad_1, i - 1, b).wait())
            stage[b] = mm_nn(left, slope[b]).astype(BF16)
            stage_copy(grad_1, i, b).start()
        pl.when(i == 1)(lambda: block_2.step(2))

    for b in range(2):
        stage_copy(grad_1, tiles - 1, b).wait()
    block_2.step(3)
    block_1.start()
    copies["x2"].wait()
    swap(0, *swaps[0]).wait_recv()

    @pl.loop(0, tiles)
    def _(n):
        cols = tile(n)
        mine = mm_nt(act[0, own_rows, :], weight[0, cols, :]) + mm_nt(act[1, own_rows, :], weight[1, cols, :])
        mine = (mine + x2[:, cols] + fold_in[0, :, cols].astype(F32)).astype(BF16)
        for b in range(2):
            send_rows[b, :, cols] = mine[b * quarter : (b + 1) * quarter]

    cell_out = FromCell(here, send_rows, out_ref, cell_sems[0], cell_sems[1])
    cell_out.start()
    fetch(full_1, weight).wait()
    fetched = fetch(qkv_in, act.at[:, :, 0:part_width])
    swap(0, *swaps[0]).wait_send()

    @pl.loop(0, tiles)
    def _(n):
        cols = tile(n)
        fold_out[:, cols] = (
            mm_nt(slope[0, other_rows, :], weight[0, cols, :]) + mm_nt(slope[1, other_rows, :], weight[1, cols, :])
        ).astype(BF16)

    swap(1, *swaps[1]).start()

    @pl.loop(0, tiles)
    def _(n):
        cols = tile(n)
        acc[:, cols] = mm_nt(slope[0, own_rows, :], weight[0, cols, :]) + mm_nt(slope[1, own_rows, :], weight[1, cols, :])

    fetched.wait()
    fetched = fetch(full_a, weight)
    swap(1, *swaps[1]).wait_recv()
    step = 128
    sums[0] = jnp.zeros(sums.shape[1:], F32)

    @pl.loop(0, half // step)
    def _(i):
        rows = pl.ds(pl.multiple_of(i * step, step), step)
        grad_in, gain_sum, shift_sum = norm_rows_back(
            x2[rows, :], acc[rows, :] + fold_in[1, rows, :].astype(F32), norm_ref[2:3, :]
        )
        sums[0, 2:3, :] += gain_sum
        sums[0, 3:4, :] += shift_sum
        grad_in = gy[rows, :].astype(F32) + grad_in
        x2[rows, :] = grad_in
        h2[rows, :] = grad_in.astype(BF16)

    swap(2, *swaps[2]).start()
    fetched.wait()
    fetched = fetch(h1_in, gy)
    block_2.step(4)
    block_1.before, block_a.before = block_2, block_1
    copies["ctx"].wait()
    copies["lse"].wait()
    swap(2, *swaps[2]).wait_recv()

    for b in range(2):
        gctx[b] = mm_nn(h2[...], weight[b, :, 0:inner]).astype(BF16)
        slope[b, :, 0:spare] = jnp.zeros((seq, spare), BF16)
    bias = key_bias(here, count_ref[0:1, 0:1], lax.broadcasted_iota(jnp.int32, (seq, 1), 0), half)
    q_block = 256
    per_chunk = seq // q_block

    @pl.loop(0, 2 * per_chunk)
    def _(i):
        b, j = i // per_chunk, i % per_chunk

        @pl.when(j == 0)
        def _():
            acc[...] = jnp.zeros_like(acc)

        attend_rows_back(
            bias, act, gctx, ctx, lse, slope, acc, b, pl.multiple_of(j * q_block, q_block), q_block, heads
        )

        @pl.when(j == per_chunk - 1)
        def _():
            for n in range(4):
                lo = spare + (1 + n // 2) * inner
                slope[b, pl.ds((n % 2) * half, half), lo : lo + inner] = acc[:, n * inner : (n + 1) * inner].astype(BF16)

        pl.when(i == 0)(lambda: block_1.step(0))
        pl.when(i == 1)(lambda: block_2.step(5))
        pl.when(i == 2)(lambda: block_1.step(1))
        pl.when(i == 4)(lambda: block_1.step(2))
        pl.when(i == 6)(lambda: block_1.step(3))

    fetched.wait()

    cell_out.sent()
    cell_out.arrive()

    @pl.loop(0, tiles)
    def _(i):
        left = gy[:, tile(i)].T
        left_out = h2[:, tile(i)].T
        for b in range(2):
            pl.when(i >= 1)(lambda: stage_copy(grad_a, i - 1, b).wait())
            stage[b, :, first:] = mm_nn(left, slope[b, :, 0:part_width]).astype(BF16)
            stage[b, :, 0:inner] = mm_nn(left_out, ctx[b]).astype(BF16)
            stage_copy(grad_a, i, b).start()

    for b in range(2):
        stage_copy(grad_a, tiles - 1, b).wait()
    fetched = fetch(x_src, stage)
    block_a.start()
    block_1.step(4)
    total = acc.at[0 : sum_2.shape[0], :]
    swap(1, *swaps[1]).wait_send()

    @pl.loop(0, tiles)
    def _(n):
        cols = tile(n)
        fold_out[:, cols] = sum(
            mm_nt(slope[b, other_rows, 0:part_width], weight[b, cols, first:]) for b in range(2)
        ).astype(BF16)

    swap(3, *swaps[3]).start()
    block_1.step(5)

    @pl.loop(0, tiles)
    def _(n):
        cols = tile(n)
        acc[:, cols] = sum(mm_nt(slope[b, own_rows, 0:part_width], weight[b, cols, first:]) for b in range(2))

    fetched.wait()
    block_a.step(0)
    swap(3, *swaps[3]).wait_recv()
    per_quarter = quarter // step

    @pl.loop(0, half // step)
    def _(i):
        b, inside = i // per_quarter, pl.ds(pl.multiple_of((i % per_quarter) * step, step), step)
        rows = pl.ds(pl.multiple_of(i * step, step), step)
        grad_in, gain_sum, shift_sum = norm_rows_back(
            stage[b, inside, :].astype(F32), acc[rows, :] + fold_in[0, rows, :].astype(F32), norm_ref[0:1, :]
        )
        sums[0, 0:1, :] += gain_sum
        sums[0, 1:2, :] += shift_sum
        send_rows[b, inside, :] = (x2[rows, :] + grad_in).astype(BF16)

    cell_gx = FromCell(here, send_rows, gx_ref, cell_sems[2], cell_sems[3])
    cell_gx.start()
    peers = (
        here.partner, here.over_x, here.over_y, {"dp": here.d, "mp": here.m + 1 - 2 * here.b},
        {"dp": here.d, "mp": here.m + 2 - 4 * here.t},
    )
    sum_send, sum_got = sems[-2:]

    def share(k):
        return remote(sums.at[k], sums_in.at[k], sum_send.at[k], sum_got.at[k], peers[k])

    def add_sums(k):
        share(k).wait_recv()
        sums[k + 1] = sums[k] + sums_in[k]
        if k < 4:
            share(k + 1).start()

    share(0).start()
    block_a.step(1)
    add_sums(0)
    block_2.finish(total, sum_2, total_sem)
    block_a.step(2)
    add_sums(1)
    block_a.step(3)
    add_sums(2)
    block_1.finish(total, sum_1, total_sem)
    block_a.step(4)
    add_sums(3)
    block_a.step(5)
    add_sums(4)
    norm_out[...] = sums[5]
    for k in range(5):
        share(k).wait_send()
    cell_gx.arrive()
    block_a.finish(total, sum_a, total_sem)
    for role in range(2):
        for j in range(4):
            block_a.z_sent(role, j)
    cell_gx.sent()
    for n in (2, 3):
        swap(n, *swaps[n]).wait_send()


def backward(kept, heads, collective):
    kept, (norms, count) = kept[:14], kept[14:]
    (full_a, full_1, full_2, h1, qkv, ctx, lse, x_in, x2, h2, act, slope, gy, grad_2) = kept
    half, width = x2.shape
    quarter, seq = half // 2, 2 * half
    wide = act.shape[2]
    rows = width // 8
    inner = heads * HEAD_DIM
    dma = pltpu.SemaphoreType.DMA
    buffers = [
        (full_a.shape, BF16), (gy.shape, BF16), (slope.shape, BF16), (act.shape, BF16), (h2.shape, BF16), (x2.shape, F32),
        ((half, width), BF16), ((2, half, width), BF16), (ctx.shape, BF16), (ctx.shape, BF16), (lse.shape, F32),
        ((half, width), F32), (x_in.shape, BF16),
    ]
    own, part, landing, reduce_sems = Reduce.scratch(rows, wide)
    return pl.pallas_call(
        functools.partial(backward_kernel, heads),
        out_shape=[jax.ShapeDtypeStruct(x_in.shape, BF16)] * 2
        + [jax.ShapeDtypeStruct((rows, wide), F32)] * 3
        + [jax.ShapeDtypeStruct((4, width), F32)]
        + [jax.ShapeDtypeStruct(grad_2.shape, BF16)] * 2,
        in_specs=[VMEM] * 2 + [ANY] * 14,
        out_specs=[ANY] * 5 + [VMEM] + [ANY] * 2,
        scratch_shapes=[pltpu.VMEM(*s) for s in buffers]
        + [own, part] + landing * 3
        + [pltpu.VMEM((6, 4, width), F32), pltpu.VMEM((5, 4, width), F32)]
        + [dma] * 10 + [dma((4,)), dma((4,))] + [dma((2,))] * 4 + [dma((2,)), dma((2, 2)), dma]
        + reduce_sems * 3 + [dma((5,))] * 2,
        compiler_params=pltpu.CompilerParams(
            collective_id=collective, has_side_effects=True, vmem_limit_bytes=67043328
        ),
        name="backward",
    )(norms, count, *kept)


def gather_norms(routes, norm_params, d, m):
    cur = norm_params
    for bit in range(routes.mp_bits):
        got = routes.mp_bit(cur, bit)
        high = ((m >> bit) & 1) == 1
        cur = jnp.where(high, jnp.concatenate([got, cur], 1), jnp.concatenate([cur, got], 1))
    for bit in range(routes.bits + 1):
        got = routes.partner(cur) if bit == 0 else routes.pair_bit(cur, bit - 1)
        high = ((d >> bit) & 1) == 1
        cur = jnp.where(high, jnp.concatenate([got, cur], 1), jnp.concatenate([cur, got], 1))
    return cur


def scatter_norms(routes, grads, d, m):
    cur = grads
    for bit in reversed(range(routes.bits + 1)):
        low, up = jnp.split(cur, 2, axis=1)
        high = ((d >> bit) & 1) == 1
        give = jnp.where(high, low, up)
        got = routes.partner(give) if bit == 0 else routes.pair_bit(give, bit - 1)
        cur = jnp.where(high, up, low) + got
    for bit in reversed(range(routes.mp_bits)):
        low, up = jnp.split(cur, 2, axis=1)
        high = ((m >> bit) & 1) == 1
        cur = jnp.where(high, up, low) + routes.mp_bit(jnp.where(high, low, up), bit)
    return cur


def update(
    outputs, input_grad, norm_sum, attend_sum, expand_sum, reduce_sum, step_count, norm_params, norm_first, norm_second,
    attend_weight, attend_first, attend_second, output_weight, output_first, output_second,
    expand_weight, expand_first, expand_second, reduce_weight, reduce_first, reduce_second,
):
    width = attend_weight.shape[2]
    step_number = step_count[0].astype(F32)
    norm_new = adam_step(norm_params, norm_first, norm_second, norm_sum, norm_rate, 0.0, step_number)
    attend_reduced = jnp.stack([attend_sum[:, i * width : (i + 1) * width] for i in range(1, 4)])
    attend_new = adam_step(
        attend_weight, attend_first, attend_second, attend_reduced, 2.0 * D ** (-0.5), decay_rate, step_number
    )
    output_new = adam_step(
        output_weight, output_first, output_second, attend_sum[:, :width].T,
        2.0 * (2 * D // SEQ) ** (-0.5), decay_rate, step_number,
    )
    expand_new = adam_step(
        expand_weight, expand_first, expand_second, expand_sum, 2.0 * D ** (-0.5), decay_rate, step_number
    )
    reduce_new = adam_step(
        reduce_weight, reduce_first, reduce_second, reduce_sum.T, 2.0 * FF ** (-0.5), decay_rate, step_number
    )
    return (
        outputs, input_grad,
        norm_new[0], norm_new[1], norm_new[2][0:2], norm_new[2][2:4],
        *attend_new, *output_new, *expand_new, *reduce_new,
    )


def per_device_plain(
    inputs, cotangent, gene_counts, step_count, norm_params, norm_first, norm_second,
    attend_weight, attend_first, attend_second, output_weight, output_first, output_second,
    expand_weight, expand_first, expand_second, reduce_weight, reduce_first, reduce_second,
):
    routes = Routes(lax.axis_size("dp"), lax.axis_size("mp"))
    d, m = lax.axis_index("dp"), lax.axis_index("mp")
    c = d % 2
    cells, quarter, _ = inputs.shape
    assert routes.mp == 4 and 2 * cells == routes.mp and routes.dp % 2 == 0
    half = 2 * quarter
    seq = 2 * half
    heads = attend_weight.shape[2] // HEAD_DIM
    width = heads * HEAD_DIM
    m_low, m_high = m % 2, m // 2
    mask = 2 * (d // 2) + ((c + m_high) % 2)

    norm_full = gather_norms(routes, norm_params, d, m)

    def to_cell(values):
        got = [
            routes.cell(lax.dynamic_index_in_dim(values, (m_low + k) % 2, 0, keepdims=False), k) for k in range(2)
        ]
        return jnp.concatenate(got, 0)

    def from_cell(rows):
        rows = rows.astype(BF16)
        got = [routes.cell(rows[k * quarter : (k + 1) * quarter], k, back=True) for k in range(2)]
        flip = m_low == 1
        return jnp.stack([jnp.where(flip, got[1], got[0]), jnp.where(flip, got[0], got[1])]).astype(F32)

    attend_shard = jnp.concatenate(
        [output_weight.T, attend_weight[0], attend_weight[1], attend_weight[2]], axis=1
    ).astype(BF16)
    expand_shard = expand_weight.astype(BF16)
    reduce_shard = reduce_weight.T.astype(BF16)

    x_mine = to_cell(inputs).astype(F32)
    attend_w = [assemble(pieces, mask) for pieces in gather_shards(routes, attend_shard)]
    expand_w = [assemble(pieces, mask) for pieces in gather_shards(routes, expand_shard)]
    reduce_w = [assemble(pieces, mask) for pieces in gather_shards(routes, reduce_shard)]
    gy_mine = to_cell(cotangent)

    other_counts = routes.partner(gene_counts)
    mine = jnp.where(m_high == c, gene_counts, other_counts)
    count = jnp.where(m_low == 1, mine[1], mine[0])
    inside = jnp.arange(quarter)
    first = m_low
    positions = jnp.concatenate(
        [h * half + b * quarter + inside for h, b in ((c, first), (c, 1 - first), (1 - c, first), (1 - c, 1 - first))]
    )
    bias = jnp.where(positions < 1 + count, 0.0, masked_score).astype(F32)

    def both(rows):
        return jnp.concatenate([rows, routes.partner(rows)], 0)

    def fold(partial):
        return partial[:half] + routes.partner(partial[half:].astype(BF16)).astype(F32)

    normed, scaled_one, inv_one = normalize(x_mine, norm_full[0], norm_full[1])
    h1 = both(normed.astype(BF16))
    qkv = jnp.stack([mm_nn(h1, w[:, width:]).astype(BF16) for w in attend_w])
    ctx, lse = attend(qkv, bias[None, :], heads)
    branch = mm_nt(ctx[0], attend_w[0][:, :width]) + mm_nt(ctx[1], attend_w[1][:, :width])
    x2 = x_mine + fold(branch)
    normed, scaled_two, inv_two = normalize(x2, norm_full[2], norm_full[3])
    h2 = both(normed.astype(BF16))
    hidden = [mm_nn(h2, w) for w in expand_w]
    active = [exact_gelu(u).astype(BF16) for u in hidden]
    branch = mm_nt(active[0], reduce_w[0]) + mm_nt(active[1], reduce_w[1])
    outputs = from_cell(x2 + fold(branch))

    gy = both(gy_mine)
    reduce_grad = [mm_tn(gy, a).astype(BF16) for a in active]
    grad_hidden = [
        jax.vjp(exact_gelu, u)[1](mm_nn(gy, w))[0].astype(BF16) for u, w in zip(hidden, reduce_w)
    ]
    expand_grad = [mm_tn(h2, g).astype(BF16) for g in grad_hidden]
    gh2 = fold(mm_nt(grad_hidden[0], expand_w[0]) + mm_nt(grad_hidden[1], expand_w[1]))
    grad_in, gain_two, shift_two = normalize_back(gh2, scaled_two, inv_two, norm_full[2])
    gx2 = gy_mine.astype(F32) + grad_in
    gb = both(gx2.astype(BF16))
    grad_ctx = jnp.stack([mm_nn(gb, w[:, :width]).astype(BF16) for w in attend_w])
    gq, gkv = attend_back(qkv, grad_ctx, ctx, lse, bias[:, None], heads)
    attend_grad = [
        jnp.concatenate(
            [mm_tn(gb, ctx[i]), mm_tn(h1, gq[i]), mm_tn(h1, gkv[i])], axis=1
        ).astype(BF16)
        for i in range(2)
    ]
    gh1 = fold(
        sum(
            mm_nt(gq[i], attend_w[i][:, width : 2 * width]) + mm_nt(gkv[i], attend_w[i][:, 2 * width :])
            for i in range(2)
        )
    )
    grad_in, gain_one, shift_one = normalize_back(gh1, scaled_one, inv_one, norm_full[0])
    input_grad = from_cell(gx2 + grad_in)

    reduce_sum = scatter_grads(routes, reduce_grad, mask)
    expand_sum = scatter_grads(routes, expand_grad, mask)
    attend_sum = scatter_grads(routes, attend_grad, mask)
    norm_sum = scatter_norms(routes, jnp.stack([gain_one, shift_one, gain_two, shift_two]), d, m)

    return update(
        outputs, input_grad, norm_sum, attend_sum, expand_sum, reduce_sum, step_count, norm_params, norm_first,
        norm_second, attend_weight, attend_first, attend_second, output_weight, output_first, output_second,
        expand_weight, expand_first, expand_second, reduce_weight, reduce_first, reduce_second,
    )


def per_device(
    inputs, cotangent, gene_counts, step_count, norm_params, norm_first, norm_second,
    attend_weight, attend_first, attend_second, output_weight, output_first, output_second,
    expand_weight, expand_first, expand_second, reduce_weight, reduce_first, reduce_second,
):
    d, m, mp_size = lax.axis_index("dp"), lax.axis_index("mp"), lax.axis_size("mp")
    cells = inputs.shape[0]
    assert mp_size == 4 and 2 * cells == mp_size and lax.axis_size("dp") == 8
    heads = attend_weight.shape[2] // HEAD_DIM
    shards = (
        jnp.concatenate([output_weight.T, attend_weight[0], attend_weight[1], attend_weight[2]], axis=1).astype(BF16),
        expand_weight.astype(BF16),
        reduce_weight.T.astype(BF16),
    )
    slot = jnp.zeros((8, 128), F32)
    slot = slot.at[0:4, 0 : norm_params.shape[1]].set(norm_params).at[4, 0:cells].set(gene_counts.astype(F32))
    kept = forward(inputs, cotangent, shards, slot, heads, 1)
    outputs, input_grad, attend_sum, expand_sum, reduce_sum, norm_part, _, _ = backward(kept, heads, 2)
    outputs, input_grad = outputs.astype(F32), input_grad.astype(F32)
    columns = norm_params.shape[1]
    norm_sum = lax.dynamic_slice(norm_part, (0, (d * mp_size + m) * columns), (4, columns))
    return update(
        outputs, input_grad, norm_sum, attend_sum, expand_sum, reduce_sum, step_count, norm_params, norm_first,
        norm_second, attend_weight, attend_first, attend_second, output_weight, output_first, output_second,
        expand_weight, expand_first, expand_second, reduce_weight, reduce_first, reduce_second,
    )


def solution(mesh):
    norms = P(None, ("dp", "mp"))
    attend_spec, col, row = P(None, "dp", "mp"), P("mp", "dp"), P("dp", "mp")
    tokens = P("dp", "mp", None)
    return jax.shard_map(
        per_device if mesh.shape["dp"] == 8 else per_device_plain,
        mesh=mesh,
        in_specs=(tokens, tokens, P("dp"), P(), norms, norms, norms)
        + (attend_spec,) * 3 + (col,) * 3 + (row,) * 3 + (col,) * 3,
        out_specs=(tokens, tokens, norms, norms, norms, norms)
        + (attend_spec,) * 3 + (col,) * 3 + (row,) * 3 + (col,) * 3,
        check_vma=False,
    )
```
